32 devices in a mesh: pair: 8 (over z, x), row: 4 (over y, core).
Axes of the slice: x: 2, y: 2, z: 4, core: 2. Of those that a mesh axis runs over, the one named last changes fastest.
Arguments:
- records: bfloat16 [128, 4096, 8], P('row', 'pair'), may hold values from -10 to 10
- offsets: float32 [8, 128], P('pair', 'row'), may hold values from -1 to 1
- counts: int32 [8], replicated, may hold values from 64 to 128, as said below
- damping: float32 [1], replicated, may hold values from 0.1 to 1
Outputs:
- offset_step: float32 [8, 128], P('pair', 'row')
The draws below stay inside these ranges and needn't reach their ends.
Inputs may be any that keep to these rules, and one draw needn't show every extreme that they name: Channel i of block b is live when i < counts[b]; in every draw some block has all 128 channels live.
All inputs are finite; a program needn't handle non-finite values.
Results may differ from the reference program's by a relative error of at most 0.0044.
Values may be sent and summed in bfloat16 or wider, within the bound.
No kernel may reach another device: no remote copies, remote signals or barrier semaphores. Data moves between devices by JAX's collectives and lax.ppermute only.
A program may use at most 64 MiB of HBM per device.

```python
import math
import jax
import jax.numpy as jnp
from jax import lax

CB = 128
NF = 512
NLAG = 256
TT = 4096
NB = 8


def draw_records(key, part):
    base_key = jax.random.fold_in(key, 17)
    key_bins, key_phase, key_delay, key_noise = jax.random.split(base_key, 4)
    modes = 32
    bins = jax.random.randint(key_bins, (modes,), TT // 8, TT // 8 + NF)
    phases = jax.random.uniform(key_phase, (modes, CB), jnp.float32, -math.pi, math.pi)
    delays = jax.random.uniform(key_delay, (NB, CB), jnp.float32, -1.0, 1.0)
    sample_ids = jnp.arange(TT, dtype=jnp.int32)
    noise = jax.random.truncated_normal(key_noise, -6.0, 6.0, (NB, CB, TT), jnp.float32)
    amplitude = 0.1

    def add_mode(mode, field):
        freq_bin = bins[mode]
        angular = freq_bin.astype(jnp.float32) * (2.0 * math.pi / TT)
        ramp = (sample_ids * freq_bin % TT).astype(jnp.float32) * (2.0 * math.pi / TT)
        wave = jnp.cos(ramp[None, None, :] - angular * delays[:, :, None] + phases[mode][None, :, None])
        return field + amplitude * wave
    field = lax.fori_loop(0, modes, add_mode, noise)
    return jnp.transpose(field, (1, 2, 0)).astype(jnp.bfloat16)


def draw_counts(key, part):
    base_key = jax.random.fold_in(key, 23)
    key_base, key_full = jax.random.split(base_key, 2)
    drawn = jax.random.randint(key_base, (NB,), CB // 2, CB + 1)
    full_block = jax.random.randint(key_full, (), 0, NB)
    return jnp.where(jnp.arange(NB, dtype=jnp.int32) == full_block, CB, drawn).astype(jnp.int32)


def levels(stream_key, extent, shards, low, top_value):
    def one(position, blocks):
        steps = jax.random.uniform(jax.random.fold_in(jax.random.fold_in(stream_key, 6), position), (blocks,), jnp.float32, low / len(shards), top_value / len(shards))
        return jnp.repeat(jnp.exp(steps), extent[position] // blocks).reshape((-1,) + (1,) * (len(extent) - position - 1))

    loudness = one(*shards[0])
    for cut in shards[1:]:
        loudness = loudness * one(*cut)
    return loudness


def setup_inputs(seed: int = 0) -> dict:
    keys = jax.random.split(jax.random.key(seed), 5)
    return {
        "records": draw_records(jax.random.fold_in(keys[4], 71), 0),
        "offsets": jnp.clip(jax.random.uniform(keys[1], (NB, CB), jnp.float32, -1.0, 1.0) * levels(keys[1], (NB, CB), ((0, 8), (1, 4)), -0.4, 0.0), -1.0, 1.0),
        "counts": draw_counts(jax.random.fold_in(keys[4], 71), 0),
        "damping": jnp.clip(jnp.exp(jax.random.uniform(keys[3], (1,), jnp.float32, math.log(0.1), math.log(1.0))), 0.1, 1.0),
    }


def band_table(row_start, row_count, samples, first_bin, freq_count):
    sample_ids = row_start + jnp.arange(row_count, dtype=jnp.int32)
    freq_bins = first_bin + jnp.arange(freq_count, dtype=jnp.int32)
    phase_ids = sample_ids[:, None] * freq_bins[None, :] % samples
    angles = phase_ids.astype(jnp.float32) * (2.0 * math.pi / samples)
    return jnp.concatenate([jnp.cos(angles), jnp.sin(angles)], axis=1)

def lag_weights(samples, first_bin, freq_count, lag_count):
    freq_bins = first_bin + jnp.arange(freq_count, dtype=jnp.int32)
    lag_ids = 1 + jnp.arange(lag_count, dtype=jnp.int32)
    phase_ids = freq_bins[:, None] * lag_ids[None, :] % samples
    angles = phase_ids.astype(jnp.float32) * (2.0 * math.pi / samples)
    centre = (jnp.arange(freq_count, dtype=jnp.float32) + 0.5) * (math.pi / freq_count)
    weight = jnp.sin(centre) ** 2
    return (-2.0 * weight[:, None] * jnp.sin(angles)).astype(jnp.bfloat16)

def pair_stats(own_spec, partners, lag_table, angular):
    own_re = own_spec[:, 0].astype(jnp.float32)
    own_im = own_spec[:, 1].astype(jnp.float32)
    far_re = partners[:, :, 0].astype(jnp.float32)
    far_im = partners[:, :, 1].astype(jnp.float32)
    cross_re = own_re * far_re + own_im * far_im
    cross_im = own_im * far_re - own_re * far_im
    stacked = jnp.stack([cross_im, angular * cross_re]).astype(jnp.bfloat16)
    lagged = jnp.einsum('knif,fl->knil', stacked.astype(jnp.float32), lag_table.astype(jnp.float32))
    residual = lagged[0]
    jacobian = lagged[1]
    return (lax.optimization_barrier(jnp.sum(jacobian * jacobian, axis=-1)), lax.optimization_barrier(jnp.sum(jacobian * residual, axis=-1)))

def reference(records, offsets, counts, damping):
    first_bin = TT // 8
    dft_table = band_table(0, TT, TT, first_bin, NF)
    flat_rows = jnp.transpose(records.astype(jnp.float32), (2, 0, 1)).reshape(NB * CB, TT)
    spectrum = jnp.dot(flat_rows.astype(jnp.float32), dft_table.astype(jnp.float32), precision=lax.Precision.HIGHEST, preferred_element_type=jnp.float32)
    cosine_part = spectrum[:, :NF]
    sine_part = spectrum[:, NF:]
    angular = (first_bin + jnp.arange(NF, dtype=jnp.int32)).astype(jnp.float32) * (2.0 * math.pi / TT)
    shift_angle = offsets.reshape(NB * CB)[:, None] * angular[None, :]
    shift_cos = jnp.cos(shift_angle)
    shift_sin = jnp.sin(shift_angle)
    real_part = cosine_part * shift_cos + sine_part * shift_sin
    imag_part = cosine_part * shift_sin - sine_part * shift_cos
    alive = (jnp.arange(CB, dtype=jnp.int32)[None, :] < counts[:, None]).astype(jnp.float32).reshape(NB * CB)
    energy = lax.optimization_barrier(jnp.mean(real_part * real_part + imag_part * imag_part, axis=1))
    weight_scale = alive / jnp.sqrt(energy + 1e-06)
    spec = jnp.stack([real_part * weight_scale[:, None], imag_part * weight_scale[:, None]], axis=1)
    spec = spec.astype(jnp.bfloat16).reshape(NB, CB, 2, NF)
    lag_table = lag_weights(TT, first_bin, NF, NLAG)

    def per_block(own_spec):
        return pair_stats(own_spec, spec, lag_table, angular)
    squares, products = lax.map(per_block, spec)
    block_ids = jnp.arange(NB, dtype=jnp.int32)
    upper_mask = (block_ids[:, None] < block_ids[None, :]).astype(jnp.float32)[:, :, None]
    squares = squares * upper_mask
    products = products * upper_mask
    symmetric = squares + jnp.transpose(squares, (1, 0, 2))
    sym_t = jnp.transpose(symmetric, (2, 0, 1))
    eye_blocks = jnp.eye(NB, dtype=jnp.float32)
    hessian = lax.optimization_barrier(jnp.sum(sym_t, axis=2))[:, :, None] * eye_blocks[None] - sym_t
    gradient = (lax.optimization_barrier(jnp.sum(products, axis=1)) - lax.optimization_barrier(jnp.sum(products, axis=0))).T
    diagonal = jnp.diagonal(hessian, axis1=1, axis2=2)
    level_mean = jnp.sum(diagonal) / (NB * CB)
    damped = damping[0] * (diagonal + level_mean)
    system = hessian + damped[:, :, None] * eye_blocks[None]
    factor = jnp.linalg.cholesky(system)
    update = -jax.scipy.linalg.cho_solve((factor, True), gradient[:, :, None])[:, :, 0]
    return update.T
```

```python
import functools
import math

import jax
import jax.numpy as jnp
from jax import lax
from jax.experimental import pallas as pl
from jax.experimental.pallas import tpu as pltpu
from jax.sharding import PartitionSpec as P

CB = 128
NF = 512
NLAG = 256


def band_table(row_start, row_count, samples, first_bin, freq_count):
    sample_ids = row_start + jnp.arange(row_count, dtype=jnp.int32)
    freq_bins = first_bin + jnp.arange(freq_count, dtype=jnp.int32)
    phase_ids = sample_ids[:, None] * freq_bins[None, :] % samples
    angles = phase_ids.astype(jnp.float32) * (2.0 * math.pi / samples)
    return jnp.concatenate([jnp.cos(angles), jnp.sin(angles)], axis=1)


def lag_weights(samples, first_bin, freq_count, lag_count):
    freq_bins = first_bin + jnp.arange(freq_count, dtype=jnp.int32)
    lag_ids = 1 + jnp.arange(lag_count, dtype=jnp.int32)
    phase_ids = freq_bins[:, None] * lag_ids[None, :] % samples
    angles = phase_ids.astype(jnp.float32) * (2.0 * math.pi / samples)
    centre = (jnp.arange(freq_count, dtype=jnp.float32) + 0.5) * (math.pi / freq_count)
    weight = jnp.sin(centre) ** 2
    return (-2.0 * weight[:, None] * jnp.sin(angles)).astype(jnp.bfloat16)


def pair_stats(own_spec, partners, lag_table, angular):
    own_re = own_spec[:, 0].astype(jnp.float32)
    own_im = own_spec[:, 1].astype(jnp.float32)
    far_re = partners[:, :, 0].astype(jnp.float32)
    far_im = partners[:, :, 1].astype(jnp.float32)
    cross_re = own_re * far_re + own_im * far_im
    cross_im = own_im * far_re - own_re * far_im
    stacked = jnp.stack([cross_im, angular * cross_re]).astype(jnp.bfloat16)
    lagged = jnp.dot(stacked, lag_table, preferred_element_type=jnp.float32)
    residual = lagged[0]
    jacobian = lagged[1]
    return (jnp.sum(jacobian * jacobian, axis=-1), jnp.sum(jacobian * residual, axis=-1))


def per_device_general(records, offsets, counts, damping):
    nblock = lax.axis_size("pair")
    block_rank = lax.axis_index("pair")
    quarter = lax.axis_index("row")
    relaid = lax.all_to_all(records, "pair", split_axis=2, concat_axis=1, tiled=True)
    signal = relaid[:, :, 0]
    channels = signal.shape[0]
    samples = signal.shape[1]
    first_bin = samples // 8
    block_len = samples // 8

    def accumulate(partial_value, turn_index):
        first_row = turn_index * block_len
        segment = lax.dynamic_slice_in_dim(signal, first_row, block_len, 1)
        dft_table = band_table(first_row, block_len, samples, first_bin, NF)
        table_high = dft_table.astype(jnp.bfloat16)
        table_low = (dft_table - table_high.astype(jnp.float32)).astype(jnp.bfloat16)
        partial_value = partial_value + jnp.dot(
            segment, table_high, preferred_element_type=jnp.float32
        )
        partial_value = partial_value + jnp.dot(
            segment, table_low, preferred_element_type=jnp.float32
        )
        return (partial_value, None)

    spectrum, _ = lax.scan(
        accumulate, jnp.zeros((channels, 2 * NF), jnp.float32), jnp.arange(8, dtype=jnp.int32)
    )
    cosine_part = spectrum[:, :NF]
    sine_part = spectrum[:, NF:]
    angular = (first_bin + jnp.arange(NF, dtype=jnp.int32)).astype(jnp.float32) * (
        2.0 * math.pi / samples
    )
    shift_angle = offsets[0][:, None] * angular[None, :]
    shift_cos = jnp.cos(shift_angle)
    shift_sin = jnp.sin(shift_angle)
    real_part = cosine_part * shift_cos + sine_part * shift_sin
    imag_part = cosine_part * shift_sin - sine_part * shift_cos
    live_count = lax.dynamic_index_in_dim(counts, block_rank, keepdims=False)
    channel_ids = quarter * channels + jnp.arange(channels, dtype=jnp.int32)
    alive = (channel_ids < live_count).astype(jnp.float32)
    energy = jnp.mean(real_part * real_part + imag_part * imag_part, axis=1)
    weight_scale = alive / jnp.sqrt(energy + 1e-06)
    own_spec = jnp.stack(
        [real_part * weight_scale[:, None], imag_part * weight_scale[:, None]], axis=1
    ).astype(jnp.bfloat16)
    lag_table = lag_weights(samples, first_bin, NF, NLAG)
    segment = lax.all_gather(own_spec[None], "pair", axis=0, tiled=True)
    squares_part, products_part = pair_stats(own_spec, segment, lag_table, angular)
    partner_ids = jnp.arange(segment.shape[0], dtype=jnp.int32)
    keep_mask = (partner_ids > block_rank).astype(jnp.float32)[:, None]
    new_squares = squares_part * keep_mask
    new_products = products_part * keep_mask
    eye_blocks = jnp.eye(nblock, dtype=jnp.float32)
    onehot = (jnp.arange(nblock, dtype=jnp.int32) == block_rank).astype(jnp.float32)
    sq_t = new_squares.T
    pr_t = new_products.T
    crossing = sq_t[:, None, :] * onehot[None, :, None]
    diag_vals = sq_t + onehot[None, :] * jnp.sum(sq_t, axis=1, keepdims=True)
    hessian = diag_vals[:, :, None] * eye_blocks[None] - crossing - jnp.swapaxes(crossing, 1, 2)
    gradient = onehot[None, :] * jnp.sum(pr_t, axis=1, keepdims=True) - pr_t
    hessian, gradient = lax.psum((hessian, gradient), "pair")
    diagonal = jnp.diagonal(hessian, axis1=1, axis2=2)
    trace_sum = lax.psum(jnp.sum(diagonal), "row")
    level_mean = trace_sum / (nblock * CB)
    damped = damping[0] * (diagonal + level_mean)
    system = hessian + damped[:, :, None] * eye_blocks[None]
    factor = jnp.linalg.cholesky(system)
    update = -jax.scipy.linalg.cho_solve((factor, True), gradient[:, :, None])[:, :, 0]
    return lax.dynamic_slice_in_dim(update, block_rank, 1, 1).T


LANES = 128
NBLOCK = 8
REACH = NBLOCK // 2
VMEM = pl.BlockSpec(memory_space=pltpu.VMEM)
ANY = pl.BlockSpec(memory_space=pl.ANY)


def pack_kernel(own, cols, rec_ref, off_ref, out_ref, wide, sems):
    ndest = out_ref.shape[0]
    copies = []
    for dest in range(ndest):
        for col in range(cols):
            copies.append(
                pltpu.make_async_copy(
                    rec_ref.at[pl.ds(dest * own, own), :, pl.ds(col * LANES, LANES)],
                    out_ref.at[dest, pl.ds(col * own, own)],
                    sems.at[dest, col],
                )
            )
            copies[-1].start()
    channels = off_ref.shape[1]
    wide[...] = jnp.zeros_like(wide)
    wide[:, :channels] = jnp.broadcast_to(off_ref[...], (NBLOCK, channels))
    value = wide[...]
    high = value.astype(jnp.bfloat16).astype(jnp.float32)
    middle = (value - high).astype(jnp.bfloat16).astype(jnp.float32)
    low = value - high - middle
    pieces = high + pltpu.roll(middle, channels, 1) + pltpu.roll(low, 2 * channels, 1)
    for dest in range(ndest):
        tile = pieces if dest == 0 else pltpu.roll(pieces, LANES - dest * own, 1)
        out_ref[dest, cols * own] = tile.astype(jnp.bfloat16)
    for copy in copies:
        copy.wait()


def sin_cos(angle):
    square = angle * angle
    sine = jnp.float32(-1.0 / 39916800.0)
    for factor in (1.0 / 362880.0, -1.0 / 5040.0, 1.0 / 120.0, -1.0 / 6.0, 1.0):
        sine = sine * square + jnp.float32(factor)
    cosine = jnp.float32(1.0 / 479001600.0)
    for factor in (-1.0 / 3628800.0, 1.0 / 40320.0, -1.0 / 720.0, 1.0 / 24.0, -0.5, 1.0):
        cosine = cosine * square + jnp.float32(factor)
    return sine * angle, cosine


def stats_kernel(
    own, cols, x_ref, high_ref, low_ref, turn_ref, ang_ref, lag_ref, live_ref, out_ref,
    spectrum, re_ref, im_ref, stacked,
):
    shards = x_ref.shape[0]
    rows = own * NBLOCK
    signal = jnp.concatenate(
        [
            jnp.concatenate(
                [
                    jnp.concatenate(
                        [x_ref[shard, col * own + c].astype(jnp.float32) for col in range(cols)],
                        axis=1,
                    )
                    for c in range(own)
                ],
                axis=0,
            )
            for shard in range(shards)
        ],
        axis=0,
    ).astype(jnp.bfloat16)
    spectrum[...] = jnp.dot(
        signal, high_ref[...], preferred_element_type=jnp.float32
    ) + jnp.dot(signal, low_ref[...], preferred_element_type=jnp.float32)

    block_ids = lax.broadcasted_iota(jnp.int32, (NBLOCK, LANES), 0)
    pieces = jnp.zeros((NBLOCK, LANES), jnp.float32)
    for shard in range(shards):
        pieces = jnp.where(
            block_ids == shard, x_ref[shard, cols * own].astype(jnp.float32), pieces
        )
    channels = own * shards
    shift = (pieces + pltpu.roll(pieces, LANES - channels, 1)) + pltpu.roll(
        pieces, LANES - 2 * channels, 1
    )
    energy = [jnp.zeros((NBLOCK, 1), jnp.float32)] * own
    for col in range(NF // LANES):
        at = pl.ds(col * LANES, LANES)
        at_sine = pl.ds(NF + col * LANES, LANES)
        cosine_part = spectrum[pl.ds(0, rows), at]
        sine_part = spectrum[pl.ds(0, rows), at_sine]
        for shard in range(1, shards):
            turn_cos = turn_ref[pl.ds(shard, 1), at]
            turn_sin = turn_ref[pl.ds(shard, 1), at_sine]
            part_cos = spectrum[pl.ds(shard * rows, rows), at]
            part_sin = spectrum[pl.ds(shard * rows, rows), at_sine]
            cosine_part += turn_cos * part_cos - turn_sin * part_sin
            sine_part += turn_sin * part_cos + turn_cos * part_sin
        for c in range(own):
            piece = slice(c * NBLOCK, (c + 1) * NBLOCK)
            shift_sin, shift_cos = sin_cos(shift[:, c : c + 1] * ang_ref[:, at])
            real = cosine_part[piece] * shift_cos + sine_part[piece] * shift_sin
            imag = cosine_part[piece] * shift_sin - sine_part[piece] * shift_cos
            energy[c] += jnp.sum(real * real + imag * imag, axis=1, keepdims=True)
            re_ref[pl.ds(c * NBLOCK, NBLOCK), at] = real
            im_ref[pl.ds(c * NBLOCK, NBLOCK), at] = imag

    half = own * REACH * NBLOCK
    angular = ang_ref[...]
    for c in range(own):
        at = pl.ds(c * NBLOCK, NBLOCK)
        scale = live_ref[c][:, :1] / jnp.sqrt(energy[c] * (1.0 / NF) + 1e-06)
        real = (re_ref[at, :] * scale).astype(jnp.bfloat16).astype(jnp.float32)
        imag = (im_ref[at, :] * scale).astype(jnp.bfloat16).astype(jnp.float32)
        crossings = []
        for reach in range(1, REACH + 1):
            far_re = pltpu.roll(real, NBLOCK - reach, 0)
            far_im = pltpu.roll(imag, NBLOCK - reach, 0)
            cross_re = real * far_re + imag * far_im
            cross_im = imag * far_re - real * far_im
            crossings.append((cross_im, angular * cross_re))
        width = REACH * NBLOCK
        for part in range(2):
            stacked[pl.ds(part * half + c * width, width), :] = jnp.concatenate(
                [crossing[part] for crossing in crossings], axis=0
            ).astype(jnp.bfloat16)
    lagged = lax.dot_general(
        lag_ref[...], stacked[...], (((1,), (1,)), ((), ())), preferred_element_type=jnp.float32
    )
    residual = lagged[:, :half]
    jacobian = lagged[:, half:]
    squares = jnp.sum(jacobian * jacobian, axis=0, keepdims=True)
    products = jnp.sum(jacobian * residual, axis=0, keepdims=True)
    both = jnp.concatenate([squares, products], axis=0)
    out_ref[...] = jnp.broadcast_to(both[None], out_ref.shape)


def solve_kernel(own, total, got_ref, damp_ref, out_ref, steps):
    shards = got_ref.shape[0]
    quarter = lax.axis_index("row")
    me = lax.axis_index("pair")
    span = REACH * NBLOCK
    lane_ids = lax.broadcasted_iota(jnp.int32, (NBLOCK, LANES), 1)
    block_ids = lax.broadcasted_iota(jnp.int32, (NBLOCK, LANES), 0)

    summed = jnp.zeros((1, LANES), jnp.float32)
    for shard in range(shards):
        for other in range(got_ref.shape[1]):
            summed += got_ref[shard, other, 0:1, :]
    inner = (lane_ids[:1] % span) < (REACH - 1) * NBLOCK
    level = jnp.sum(jnp.where(inner, 2.0 * summed, summed), axis=1, keepdims=True) / total

    squares = jnp.concatenate(
        [got_ref[shard, quarter, 0:1, :] for shard in range(shards)], axis=0
    )
    products = jnp.concatenate(
        [got_ref[shard, quarter, 1:2, :] for shard in range(shards)], axis=0
    )

    def entry(array, reach, block):
        lane = (reach - 1) * NBLOCK + block
        return array if lane == 0 else pltpu.roll(array, LANES - lane, 1)

    weight = {}
    slope = {}
    for reach in range(1, REACH + 1):
        for block in range(NBLOCK if reach < REACH else NBLOCK // 2):
            far = (block + reach) % NBLOCK
            value = entry(squares, reach, block)
            weight[block, far] = value
            weight[far, block] = value
            value = entry(products, reach, block)
            slope[block, far] = value
            slope[far, block] = -value
    damping = damp_ref[...]
    matrix = {}
    right = []
    for a in range(NBLOCK):
        others = [b for b in range(NBLOCK) if b != a]
        diagonal = functools.reduce(lambda x, y: x + y, [weight[a, b] for b in others])
        matrix[a, a] = diagonal + damping * (diagonal + level)
        for b in range(a):
            matrix[a, b] = -weight[a, b]
        right.append(functools.reduce(lambda x, y: x + y, [slope[a, b] for b in others]))
    inverse = []
    for k in range(NBLOCK):
        inverse.append(1.0 / matrix[k, k])
        for i in range(k + 1, NBLOCK):
            ratio = matrix[i, k] * inverse[k]
            for j in range(k + 1, i + 1):
                matrix[i, j] = matrix[i, j] - ratio * matrix[j, k]
            right[i] = right[i] - ratio * right[k]
    step = [None] * NBLOCK
    for i in reversed(range(NBLOCK)):
        value = right[i]
        for j in range(i + 1, NBLOCK):
            value = value - matrix[j, i] * step[j]
        step[i] = value * inverse[i]
        steps[i] = -step[i]
    mine = steps[me]
    placed = jnp.zeros((NBLOCK, LANES), jnp.float32)
    for c in range(own):
        column = jnp.broadcast_to(mine[:, c * span : c * span + 1], (NBLOCK, LANES))
        placed = jnp.where(lane_ids == block_ids * own + c, column, placed)
    out_ref[...] = jnp.sum(placed, axis=0, keepdims=True)[:, : out_ref.shape[1]]


def per_device(records, offsets, counts, damping):
    shards = lax.axis_size("pair")
    rows = lax.axis_size("row")
    me = lax.axis_index("pair")
    quarter = lax.axis_index("row")
    channels, length, _ = records.shape
    samples = length * shards
    first_bin = samples // 8
    own = channels // shards
    cols = length // LANES
    tiles = own * cols + 1

    payload = pl.pallas_call(
        functools.partial(pack_kernel, own, cols),
        out_shape=jax.ShapeDtypeStruct((shards, tiles, NBLOCK, LANES), jnp.bfloat16),
        in_specs=[ANY, VMEM],
        out_specs=VMEM,
        scratch_shapes=[
            pltpu.VMEM((NBLOCK, LANES), jnp.float32),
            pltpu.SemaphoreType.DMA((shards, cols)),
        ],
        name="pack",
    )(jnp.transpose(records, (0, 2, 1)), offsets)
    received = lax.all_to_all(payload, "pair", split_axis=0, concat_axis=0, tiled=True)

    table = band_table(0, length, samples, first_bin, NF)
    table_high = table.astype(jnp.bfloat16)
    table_low = (table - lax.reduce_precision(table, 8, 7)).astype(jnp.bfloat16)
    turn_ids = length * jnp.arange(shards, dtype=jnp.int32)[:, None]
    bins = first_bin + jnp.arange(NF, dtype=jnp.int32)
    turn_angle = (turn_ids * bins[None, :] % samples).astype(jnp.float32) * (
        2.0 * math.pi / samples
    )
    turn = jnp.concatenate([jnp.cos(turn_angle), jnp.sin(turn_angle)], axis=1)
    angular = (bins.astype(jnp.float32) * (2.0 * math.pi / samples))[None, :]
    lag_table = lag_weights(samples, first_bin, NF, NLAG).T
    channel_ids = quarter * channels + me * own + jnp.arange(own, dtype=jnp.int32)
    alive = (channel_ids[:, None] < counts[None, :]).astype(jnp.float32)
    live = jnp.broadcast_to(alive[:, :, None], (own, NBLOCK, LANES))

    stats = pl.pallas_call(
        functools.partial(stats_kernel, own, cols),
        out_shape=jax.ShapeDtypeStruct((shards * rows, 2, LANES), jnp.float32),
        in_specs=[VMEM] * 7,
        out_specs=VMEM,
        scratch_shapes=[
            pltpu.VMEM((shards * own * NBLOCK, 2 * NF), jnp.float32),
            pltpu.VMEM((own * NBLOCK, NF), jnp.float32),
            pltpu.VMEM((own * NBLOCK, NF), jnp.float32),
            pltpu.VMEM((2 * own * REACH * NBLOCK, NF), jnp.bfloat16),
        ],
        name="stats",
    )(received, table_high, table_low, turn, angular, lag_table, live)
    gathered = lax.all_to_all(stats, ("pair", "row"), split_axis=0, concat_axis=0, tiled=True)
    gathered = gathered.reshape(shards, rows, 2, LANES)
    return pl.pallas_call(
        functools.partial(solve_kernel, own, float(NBLOCK * CB)),
        out_shape=jax.ShapeDtypeStruct((1, channels), jnp.float32),
        in_specs=[VMEM, VMEM],
        out_specs=VMEM,
        scratch_shapes=[pltpu.VMEM((NBLOCK, NBLOCK, LANES), jnp.float32)],
        name="solve",
    )(gathered, jnp.broadcast_to(damping[None, :], (NBLOCK, LANES)))


def body(records, offsets, counts, damping):
    shards = lax.axis_size("pair")
    channels, length, nblock = records.shape
    own = channels // shards
    whole = own * shards == channels and own * REACH * NBLOCK == LANES
    if shards == NBLOCK and nblock == NBLOCK and whole and length % LANES == 0:
        return per_device(records, offsets, counts, damping)
    return per_device_general(records, offsets, counts, damping)


def solution(mesh):
    return jax.shard_map(
        body,
        mesh=mesh,
        in_specs=(P("row", "pair", None), P("pair", "row"), P(), P()),
        out_specs=P("pair", "row"),
        check_vma=False,
    )
```

```python
import functools
import math

import jax
import jax.numpy as jnp
from jax import lax
from jax.experimental import pallas as pl
from jax.experimental.pallas import tpu as pltpu
from jax.sharding import PartitionSpec as P

CB = 128
NF = 512
NLAG = 256


def band_table(row_start, row_count, samples, first_bin, freq_count):
    sample_ids = row_start + jnp.arange(row_count, dtype=jnp.int32)
    freq_bins = first_bin + jnp.arange(freq_count, dtype=jnp.int32)
    phase_ids = sample_ids[:, None] * freq_bins[None, :] % samples
    angles = phase_ids.astype(jnp.float32) * (2.0 * math.pi / samples)
    return jnp.concatenate([jnp.cos(angles), jnp.sin(angles)], axis=1)


def lag_weights(samples, first_bin, freq_count, lag_count):
    freq_bins = first_bin + jnp.arange(freq_count, dtype=jnp.int32)
    lag_ids = 1 + jnp.arange(lag_count, dtype=jnp.int32)
    phase_ids = freq_bins[:, None] * lag_ids[None, :] % samples
    angles = phase_ids.astype(jnp.float32) * (2.0 * math.pi / samples)
    centre = (jnp.arange(freq_count, dtype=jnp.float32) + 0.5) * (math.pi / freq_count)
    weight = jnp.sin(centre) ** 2
    return (-2.0 * weight[:, None] * jnp.sin(angles)).astype(jnp.bfloat16)


def pair_stats(own_spec, partners, lag_table, angular):
    own_re = own_spec[:, 0].astype(jnp.float32)
    own_im = own_spec[:, 1].astype(jnp.float32)
    far_re = partners[:, :, 0].astype(jnp.float32)
    far_im = partners[:, :, 1].astype(jnp.float32)
    cross_re = own_re * far_re + own_im * far_im
    cross_im = own_im * far_re - own_re * far_im
    stacked = jnp.stack([cross_im, angular * cross_re]).astype(jnp.bfloat16)
    lagged = jnp.dot(stacked, lag_table, preferred_element_type=jnp.float32)
    residual = lagged[0]
    jacobian = lagged[1]
    return (jnp.sum(jacobian * jacobian, axis=-1), jnp.sum(jacobian * residual, axis=-1))


def per_device_general(records, offsets, counts, damping):
    nblock = lax.axis_size("pair")
    block_rank = lax.axis_index("pair")
    quarter = lax.axis_index("row")
    relaid = lax.all_to_all(records, "pair", split_axis=2, concat_axis=1, tiled=True)
    signal = relaid[:, :, 0]
    channels = signal.shape[0]
    samples = signal.shape[1]
    first_bin = samples // 8
    block_len = samples // 8

    def accumulate(partial_value, turn_index):
        first_row = turn_index * block_len
        segment = lax.dynamic_slice_in_dim(signal, first_row, block_len, 1)
        dft_table = band_table(first_row, block_len, samples, first_bin, NF)
        table_high = dft_table.astype(jnp.bfloat16)
        table_low = (dft_table - table_high.astype(jnp.float32)).astype(jnp.bfloat16)
        partial_value = partial_value + jnp.dot(
            segment, table_high, preferred_element_type=jnp.float32
        )
        partial_value = partial_value + jnp.dot(
            segment, table_low, preferred_element_type=jnp.float32
        )
        return (partial_value, None)

    spectrum, _ = lax.scan(
        accumulate, jnp.zeros((channels, 2 * NF), jnp.float32), jnp.arange(8, dtype=jnp.int32)
    )
    cosine_part = spectrum[:, :NF]
    sine_part = spectrum[:, NF:]
    angular = (first_bin + jnp.arange(NF, dtype=jnp.int32)).astype(jnp.float32) * (
        2.0 * math.pi / samples
    )
    shift_angle = offsets[0][:, None] * angular[None, :]
    shift_cos = jnp.cos(shift_angle)
    shift_sin = jnp.sin(shift_angle)
    real_part = cosine_part * shift_cos + sine_part * shift_sin
    imag_part = cosine_part * shift_sin - sine_part * shift_cos
    live_count = lax.dynamic_index_in_dim(counts, block_rank, keepdims=False)
    channel_ids = quarter * channels + jnp.arange(channels, dtype=jnp.int32)
    alive = (channel_ids < live_count).astype(jnp.float32)
    energy = jnp.mean(real_part * real_part + imag_part * imag_part, axis=1)
    weight_scale = alive / jnp.sqrt(energy + 1e-06)
    own_spec = jnp.stack(
        [real_part * weight_scale[:, None], imag_part * weight_scale[:, None]], axis=1
    ).astype(jnp.bfloat16)
    lag_table = lag_weights(samples, first_bin, NF, NLAG)
    segment = lax.all_gather(own_spec[None], "pair", axis=0, tiled=True)
    squares_part, products_part = pair_stats(own_spec, segment, lag_table, angular)
    partner_ids = jnp.arange(segment.shape[0], dtype=jnp.int32)
    keep_mask = (partner_ids > block_rank).astype(jnp.float32)[:, None]
    new_squares = squares_part * keep_mask
    new_products = products_part * keep_mask
    eye_blocks = jnp.eye(nblock, dtype=jnp.float32)
    onehot = (jnp.arange(nblock, dtype=jnp.int32) == block_rank).astype(jnp.float32)
    sq_t = new_squares.T
    pr_t = new_products.T
    crossing = sq_t[:, None, :] * onehot[None, :, None]
    diag_vals = sq_t + onehot[None, :] * jnp.sum(sq_t, axis=1, keepdims=True)
    hessian = diag_vals[:, :, None] * eye_blocks[None] - crossing - jnp.swapaxes(crossing, 1, 2)
    gradient = onehot[None, :] * jnp.sum(pr_t, axis=1, keepdims=True) - pr_t
    hessian, gradient = lax.psum((hessian, gradient), "pair")
    diagonal = jnp.diagonal(hessian, axis1=1, axis2=2)
    trace_sum = lax.psum(jnp.sum(diagonal), "row")
    level_mean = trace_sum / (nblock * CB)
    damped = damping[0] * (diagonal + level_mean)
    system = hessian + damped[:, :, None] * eye_blocks[None]
    factor = jnp.linalg.cholesky(system)
    update = -jax.scipy.linalg.cho_solve((factor, True), gradient[:, :, None])[:, :, 0]
    return lax.dynamic_slice_in_dim(update, block_rank, 1, 1).T


LANES = 128
NBLOCK = 8
REACH = NBLOCK // 2
VMEM = pl.BlockSpec(memory_space=pltpu.VMEM)
ANY = pl.BlockSpec(memory_space=pl.ANY)


def pack_kernel(rec_ref, off_ref, out_ref, wide, sems):
    ndest, own, _, length = rec_ref.shape
    cols = length // LANES
    copies = [
        pltpu.make_async_copy(
            rec_ref.at[:, :, :, pl.ds(col * LANES, LANES)],
            out_ref.at[:, pl.ds(col * own, own)],
            sems.at[col],
        )
        for col in range(cols)
    ]
    for copy in copies:
        copy.start()
    channels = off_ref.shape[1]
    wide[...] = jnp.zeros_like(wide)
    wide[:, :channels] = jnp.broadcast_to(off_ref[...], (NBLOCK, channels))
    value = wide[...]
    high = value.astype(jnp.bfloat16).astype(jnp.float32)
    middle = (value - high).astype(jnp.bfloat16).astype(jnp.float32)
    low = value - high - middle
    pieces = high + pltpu.roll(middle, channels, 1) + pltpu.roll(low, 2 * channels, 1)
    for dest in range(ndest):
        tile = pieces if dest == 0 else pltpu.roll(pieces, LANES - dest * own, 1)
        out_ref[dest, cols * own] = tile.astype(jnp.bfloat16)
    for copy in copies:
        copy.wait()


def sin_cos(angle):
    square = angle * angle
    sine = jnp.float32(-1.0 / 39916800.0)
    for factor in (1.0 / 362880.0, -1.0 / 5040.0, 1.0 / 120.0, -1.0 / 6.0, 1.0):
        sine = sine * square + jnp.float32(factor)
    cosine = jnp.float32(1.0 / 479001600.0)
    for factor in (-1.0 / 3628800.0, 1.0 / 40320.0, -1.0 / 720.0, 1.0 / 24.0, -0.5, 1.0):
        cosine = cosine * square + jnp.float32(factor)
    return sine * angle, cosine


def unit_circle(phase, samples):
    phase = lax.bitwise_and(phase, samples - 1)
    phase = jnp.where(phase >= samples // 2, phase - samples, phase)
    sine, cosine = sin_cos(phase.astype(jnp.float32) * jnp.float32(math.pi / samples))
    return 1.0 - 2.0 * sine * sine, 2.0 * sine * cosine


def table_kernel(
    order, samples, counts_ref, damp_ref,
    high_ref, low_ref, turn_ref, ang_ref, lag_ref, live_ref, wide_ref, coarse,
):
    shards = len(order)
    length = samples // shards
    own = live_ref.shape[0]
    rows = 16
    first_bin = samples // 8

    def bins(height):
        return first_bin + lax.broadcasted_iota(jnp.int32, (height, NF), 1)

    def ids(height):
        return lax.broadcasted_iota(jnp.int32, (height, NF), 0)

    fine_cos, fine_sin = unit_circle(ids(rows) * bins(rows), samples)
    height = length // rows
    wide_cos, wide_sin = unit_circle(ids(height) * rows * bins(height), samples)
    coarse[pl.ds(0, height), :NF] = wide_cos
    coarse[pl.ds(0, height), NF:] = wide_sin

    @pl.loop(0, height)
    def _(step):
        row_cos = coarse[pl.ds(step, 1), :NF]
        row_sin = coarse[pl.ds(step, 1), NF:]
        at = pl.ds(pl.multiple_of(step * rows, rows), rows)
        for part, value in enumerate(
            (row_cos * fine_cos - row_sin * fine_sin, row_sin * fine_cos + row_cos * fine_sin)
        ):
            cut = pl.ds(part * NF, NF)
            high = value.astype(jnp.bfloat16)
            high_ref[at, cut] = high
            low_ref[at, cut] = (value - high.astype(jnp.float32)).astype(jnp.bfloat16)

    lags = NLAG // rows
    wide_cos, wide_sin = unit_circle((ids(lags) * rows + 1) * bins(lags), samples)
    coarse[pl.ds(0, lags), :NF] = wide_cos
    coarse[pl.ds(0, lags), NF:] = wide_sin
    centre = (lax.broadcasted_iota(jnp.int32, (1, NF), 1).astype(jnp.float32) + 0.5) * (
        math.pi / NF
    )
    _, weight = sin_cos(centre - jnp.float32(math.pi / 2))
    factor = -2.0 * (weight * weight)
    lag_cos = fine_cos * factor
    lag_sin = fine_sin * factor

    @pl.loop(0, lags)
    def _(step):
        row_cos = coarse[pl.ds(step, 1), :NF]
        row_sin = coarse[pl.ds(step, 1), NF:]
        at = pl.ds(pl.multiple_of(step * rows, rows), rows)
        lag_ref[at, :] = (row_sin * lag_cos + row_cos * lag_sin).astype(jnp.bfloat16)

    turn_cos, turn_sin = unit_circle(ids(shards) * length * bins(shards), samples)
    turn_ref[:, :NF] = turn_cos
    turn_ref[:, NF:] = turn_sin
    ang_ref[...] = bins(NBLOCK).astype(jnp.float32) * jnp.float32(2.0 * math.pi / samples)

    me = lax.axis_index("pair")
    slot = jnp.where(me == order[0], 0, jnp.where(me < order[0], me + 1, me))
    first_channel = (lax.axis_index("row") * shards + slot) * own
    block_ids = lax.broadcasted_iota(jnp.int32, (NBLOCK, LANES), 0)
    limit = jnp.zeros((NBLOCK, LANES), jnp.int32)
    for block in range(NBLOCK):
        limit = jnp.where(block_ids == block, counts_ref[block], limit)
    for c in range(own):
        live_ref[c] = (limit > first_channel + c).astype(jnp.float32)
    wide_ref[...] = jnp.full((NBLOCK, LANES), damp_ref[0], jnp.float32)


def stats_kernel(
    order, own, cols, x_ref, high_ref, low_ref, turn_ref, ang_ref, lag_ref, live_ref, out_ref,
    spectrum, re_ref, im_ref, stacked,
):
    shards = x_ref.shape[0]
    rows = own * NBLOCK
    signal = jnp.concatenate(
        [
            jnp.concatenate(
                [
                    jnp.concatenate(
                        [x_ref[shard, col * own + c].astype(jnp.float32) for col in range(cols)],
                        axis=1,
                    )
                    for c in range(own)
                ],
                axis=0,
            )
            for shard in range(shards)
        ],
        axis=0,
    ).astype(jnp.bfloat16)
    spectrum[...] = jnp.dot(
        signal, high_ref[...], preferred_element_type=jnp.float32
    ) + jnp.dot(signal, low_ref[...], preferred_element_type=jnp.float32)

    block_ids = lax.broadcasted_iota(jnp.int32, (NBLOCK, LANES), 0)
    pieces = jnp.zeros((NBLOCK, LANES), jnp.float32)
    for shard in range(shards):
        pieces = jnp.where(
            block_ids == order[shard], x_ref[shard, cols * own].astype(jnp.float32), pieces
        )
    channels = own * shards
    shift = (pieces + pltpu.roll(pieces, LANES - channels, 1)) + pltpu.roll(
        pieces, LANES - 2 * channels, 1
    )
    energy = [jnp.zeros((NBLOCK, 1), jnp.float32)] * own
    for col in range(NF // LANES):
        at = pl.ds(col * LANES, LANES)
        at_sine = pl.ds(NF + col * LANES, LANES)
        home = order.index(0)
        cosine_part = spectrum[pl.ds(home * rows, rows), at]
        sine_part = spectrum[pl.ds(home * rows, rows), at_sine]
        for shard in range(shards):
            if shard == home:
                continue
            turn_cos = turn_ref[pl.ds(order[shard], 1), at]
            turn_sin = turn_ref[pl.ds(order[shard], 1), at_sine]
            part_cos = spectrum[pl.ds(shard * rows, rows), at]
            part_sin = spectrum[pl.ds(shard * rows, rows), at_sine]
            cosine_part += turn_cos * part_cos - turn_sin * part_sin
            sine_part += turn_sin * part_cos + turn_cos * part_sin
        for c in range(own):
            piece = slice(c * NBLOCK, (c + 1) * NBLOCK)
            shift_sin, shift_cos = sin_cos(shift[:, c : c + 1] * ang_ref[:, at])
            real = cosine_part[piece] * shift_cos + sine_part[piece] * shift_sin
            imag = cosine_part[piece] * shift_sin - sine_part[piece] * shift_cos
            energy[c] += jnp.sum(real * real + imag * imag, axis=1, keepdims=True)
            re_ref[pl.ds(c * NBLOCK, NBLOCK), at] = real
            im_ref[pl.ds(c * NBLOCK, NBLOCK), at] = imag

    half = own * REACH * NBLOCK
    angular = ang_ref[...]
    for c in range(own):
        at = pl.ds(c * NBLOCK, NBLOCK)
        scale = live_ref[c][:, :1] / jnp.sqrt(energy[c] * (1.0 / NF) + 1e-06)
        real = (re_ref[at, :] * scale).astype(jnp.bfloat16).astype(jnp.float32)
        imag = (im_ref[at, :] * scale).astype(jnp.bfloat16).astype(jnp.float32)
        crossings = []
        for reach in range(1, REACH + 1):
            far_re = pltpu.roll(real, NBLOCK - reach, 0)
            far_im = pltpu.roll(imag, NBLOCK - reach, 0)
            cross_re = real * far_re + imag * far_im
            cross_im = imag * far_re - real * far_im
            crossings.append((cross_im, angular * cross_re))
        width = REACH * NBLOCK
        for part in range(2):
            stacked[pl.ds(part * half + c * width, width), :] = jnp.concatenate(
                [crossing[part] for crossing in crossings], axis=0
            ).astype(jnp.bfloat16)
    lagged = lax.dot_general(
        lag_ref[...], stacked[...], (((1,), (1,)), ((), ())), preferred_element_type=jnp.float32
    )
    residual = lagged[:, :half]
    jacobian = lagged[:, half:]
    squares = jnp.sum(jacobian * jacobian, axis=0, keepdims=True)
    products = jnp.sum(jacobian * residual, axis=0, keepdims=True)
    both = jnp.concatenate([squares, products], axis=0)
    out_ref[...] = jnp.broadcast_to(both[None], out_ref.shape)


def solve_kernel(order, own, total, got_ref, damp_ref, out_ref, steps):
    shards = got_ref.shape[0]
    quarter = lax.axis_index("row")
    me = lax.axis_index("pair")
    span = REACH * NBLOCK
    lane_ids = lax.broadcasted_iota(jnp.int32, (NBLOCK, LANES), 1)
    block_ids = lax.broadcasted_iota(jnp.int32, (NBLOCK, LANES), 0)

    summed = jnp.zeros((1, LANES), jnp.float32)
    for shard in range(shards):
        for other in range(got_ref.shape[1]):
            summed += got_ref[shard, other, 0:1, :]
    inner = (lane_ids[:1] % span) < (REACH - 1) * NBLOCK
    level = jnp.sum(jnp.where(inner, 2.0 * summed, summed), axis=1, keepdims=True) / total

    squares = jnp.concatenate(
        [got_ref[shard, quarter, 0:1, :] for shard in order], axis=0
    )
    products = jnp.concatenate(
        [got_ref[shard, quarter, 1:2, :] for shard in order], axis=0
    )

    def entry(array, reach, block):
        lane = (reach - 1) * NBLOCK + block
        return array if lane == 0 else pltpu.roll(array, LANES - lane, 1)

    weight = {}
    slope = {}
    for reach in range(1, REACH + 1):
        for block in range(NBLOCK if reach < REACH else NBLOCK // 2):
            far = (block + reach) % NBLOCK
            value = entry(squares, reach, block)
            weight[block, far] = value
            weight[far, block] = value
            value = entry(products, reach, block)
            slope[block, far] = value
            slope[far, block] = -value
    damping = damp_ref[...]
    matrix = {}
    right = []
    for a in range(NBLOCK):
        others = [b for b in range(NBLOCK) if b != a]
        diagonal = functools.reduce(lambda x, y: x + y, [weight[a, b] for b in others])
        matrix[a, a] = diagonal + damping * (diagonal + level)
        for b in range(a):
            matrix[a, b] = -weight[a, b]
        right.append(functools.reduce(lambda x, y: x + y, [slope[a, b] for b in others]))
    inverse = []
    for k in range(NBLOCK):
        inverse.append(1.0 / matrix[k, k])
        for i in range(k + 1, NBLOCK):
            ratio = matrix[i, k] * inverse[k]
            for j in range(k + 1, i + 1):
                matrix[i, j] = matrix[i, j] - ratio * matrix[j, k]
            right[i] = right[i] - ratio * right[k]
    step = [None] * NBLOCK
    for i in reversed(range(NBLOCK)):
        value = right[i]
        for j in range(i + 1, NBLOCK):
            value = value - matrix[j, i] * step[j]
        step[i] = value * inverse[i]
        steps[i] = -step[i]
    mine = steps[me]
    placed = jnp.zeros((NBLOCK, LANES), jnp.float32)
    for c in range(own):
        column = jnp.broadcast_to(mine[:, c * span : c * span + 1], (NBLOCK, LANES))
        placed = jnp.where(lane_ids == block_ids * own + c, column, placed)
    out_ref[...] = jnp.sum(placed, axis=0, keepdims=True)[:, : out_ref.shape[1]]


def room(mebibytes):
    return pltpu.CompilerParams(vmem_limit_bytes=mebibytes << 20)


def per_device(records, offsets, counts, damping):
    shards = lax.axis_size("pair")
    rows = lax.axis_size("row")
    channels, length, _ = records.shape
    samples = length * shards
    own = channels // shards
    cols = length // LANES
    tiles = own * cols + 1
    lead = shards // 2
    order = (lead, *range(lead), *range(lead + 1, shards))

    by_owner = jnp.transpose(records, (0, 2, 1)).reshape(shards, own, NBLOCK, length)
    payload = pl.pallas_call(
        pack_kernel,
        out_shape=jax.ShapeDtypeStruct((shards, tiles, NBLOCK, LANES), jnp.bfloat16),
        in_specs=[ANY, VMEM],
        out_specs=VMEM,
        scratch_shapes=[
            pltpu.VMEM((NBLOCK, LANES), jnp.float32),
            pltpu.SemaphoreType.DMA((cols,)),
        ],
        compiler_params=room(4),
        name="pack",
    )(by_owner, offsets)
    received = lax.all_to_all(
        payload, "pair", split_axis=0, concat_axis=0, tiled=True, axis_index_groups=[list(order)]
    )

    tables = pl.pallas_call(
        functools.partial(table_kernel, order, samples),
        out_shape=(
            jax.ShapeDtypeStruct((length, 2 * NF), jnp.bfloat16),
            jax.ShapeDtypeStruct((length, 2 * NF), jnp.bfloat16),
            jax.ShapeDtypeStruct((shards, 2 * NF), jnp.float32),
            jax.ShapeDtypeStruct((NBLOCK, NF), jnp.float32),
            jax.ShapeDtypeStruct((NLAG, NF), jnp.bfloat16),
            jax.ShapeDtypeStruct((own, NBLOCK, LANES), jnp.float32),
            jax.ShapeDtypeStruct((NBLOCK, LANES), jnp.float32),
        ),
        in_specs=[pl.BlockSpec(memory_space=pltpu.SMEM)] * 2,
        out_specs=(VMEM,) * 7,
        scratch_shapes=[pltpu.VMEM((max(length, NLAG) // 16, 2 * NF), jnp.float32)],
        compiler_params=room(8),
        name="tables",
    )(counts, damping)

    stats = pl.pallas_call(
        functools.partial(stats_kernel, order, own, cols),
        out_shape=jax.ShapeDtypeStruct((shards * rows, 2, LANES), jnp.float32),
        in_specs=[VMEM] * 7,
        out_specs=VMEM,
        scratch_shapes=[
            pltpu.VMEM((shards * own * NBLOCK, 2 * NF), jnp.float32),
            pltpu.VMEM((own * NBLOCK, NF), jnp.float32),
            pltpu.VMEM((own * NBLOCK, NF), jnp.float32),
            pltpu.VMEM((2 * own * REACH * NBLOCK, NF), jnp.bfloat16),
        ],
        compiler_params=room(12),
        name="stats",
    )(received, *tables[:6])
    gathered = lax.all_to_all(stats, ("pair", "row"), split_axis=0, concat_axis=0, tiled=True)
    gathered = gathered.reshape(shards, rows, 2, LANES)
    return pl.pallas_call(
        functools.partial(solve_kernel, order, own, float(NBLOCK * CB)),
        out_shape=jax.ShapeDtypeStruct((1, channels), jnp.float32),
        in_specs=[VMEM, VMEM],
        out_specs=VMEM,
        scratch_shapes=[pltpu.VMEM((NBLOCK, NBLOCK, LANES), jnp.float32)],
        compiler_params=room(4),
        name="solve",
    )(gathered, tables[6])


def body(records, offsets, counts, damping):
    shards = lax.axis_size("pair")
    channels, length, nblock = records.shape
    own = channels // shards
    whole = own * shards == channels and own * REACH * NBLOCK == LANES
    even = length % LANES == 0 and length & (length - 1) == 0
    if shards == NBLOCK and nblock == NBLOCK and whole and even:
        return per_device(records, offsets, counts, damping)
    return per_device_general(records, offsets, counts, damping)


def solution(mesh):
    return jax.shard_map(
        body,
        mesh=mesh,
        in_specs=(P("row", "pair", None), P("pair", "row"), P(), P()),
        out_specs=P("pair", "row"),
        check_vma=False,
    )
```

```python
import functools
import math

import jax
import jax.numpy as jnp
from jax import lax
from jax.experimental import pallas as pl
from jax.experimental.pallas import tpu as pltpu
from jax.sharding import PartitionSpec as P

CB = 128
NF = 512
NLAG = 256


def band_table(row_start, row_count, samples, first_bin, freq_count):
    sample_ids = row_start + jnp.arange(row_count, dtype=jnp.int32)
    freq_bins = first_bin + jnp.arange(freq_count, dtype=jnp.int32)
    phase_ids = sample_ids[:, None] * freq_bins[None, :] % samples
    angles = phase_ids.astype(jnp.float32) * (2.0 * math.pi / samples)
    return jnp.concatenate([jnp.cos(angles), jnp.sin(angles)], axis=1)


def lag_weights(samples, first_bin, freq_count, lag_count):
    freq_bins = first_bin + jnp.arange(freq_count, dtype=jnp.int32)
    lag_ids = 1 + jnp.arange(lag_count, dtype=jnp.int32)
    phase_ids = freq_bins[:, None] * lag_ids[None, :] % samples
    angles = phase_ids.astype(jnp.float32) * (2.0 * math.pi / samples)
    centre = (jnp.arange(freq_count, dtype=jnp.float32) + 0.5) * (math.pi / freq_count)
    weight = jnp.sin(centre) ** 2
    return (-2.0 * weight[:, None] * jnp.sin(angles)).astype(jnp.bfloat16)


def pair_stats(own_spec, partners, lag_table, angular):
    own_re = own_spec[:, 0].astype(jnp.float32)
    own_im = own_spec[:, 1].astype(jnp.float32)
    far_re = partners[:, :, 0].astype(jnp.float32)
    far_im = partners[:, :, 1].astype(jnp.float32)
    cross_re = own_re * far_re + own_im * far_im
    cross_im = own_im * far_re - own_re * far_im
    stacked = jnp.stack([cross_im, angular * cross_re]).astype(jnp.bfloat16)
    lagged = jnp.dot(stacked, lag_table, preferred_element_type=jnp.float32)
    residual = lagged[0]
    jacobian = lagged[1]
    return (jnp.sum(jacobian * jacobian, axis=-1), jnp.sum(jacobian * residual, axis=-1))


def per_device_general(records, offsets, counts, damping):
    nblock = lax.axis_size("pair")
    block_rank = lax.axis_index("pair")
    quarter = lax.axis_index("row")
    relaid = lax.all_to_all(records, "pair", split_axis=2, concat_axis=1, tiled=True)
    signal = relaid[:, :, 0]
    channels = signal.shape[0]
    samples = signal.shape[1]
    first_bin = samples // 8
    block_len = samples // 8

    def accumulate(partial_value, turn_index):
        first_row = turn_index * block_len
        segment = lax.dynamic_slice_in_dim(signal, first_row, block_len, 1)
        dft_table = band_table(first_row, block_len, samples, first_bin, NF)
        table_high = dft_table.astype(jnp.bfloat16)
        table_low = (dft_table - table_high.astype(jnp.float32)).astype(jnp.bfloat16)
        partial_value = partial_value + jnp.dot(
            segment, table_high, preferred_element_type=jnp.float32
        )
        partial_value = partial_value + jnp.dot(
            segment, table_low, preferred_element_type=jnp.float32
        )
        return (partial_value, None)

    spectrum, _ = lax.scan(
        accumulate, jnp.zeros((channels, 2 * NF), jnp.float32), jnp.arange(8, dtype=jnp.int32)
    )
    cosine_part = spectrum[:, :NF]
    sine_part = spectrum[:, NF:]
    angular = (first_bin + jnp.arange(NF, dtype=jnp.int32)).astype(jnp.float32) * (
        2.0 * math.pi / samples
    )
    shift_angle = offsets[0][:, None] * angular[None, :]
    shift_cos = jnp.cos(shift_angle)
    shift_sin = jnp.sin(shift_angle)
    real_part = cosine_part * shift_cos + sine_part * shift_sin
    imag_part = cosine_part * shift_sin - sine_part * shift_cos
    live_count = lax.dynamic_index_in_dim(counts, block_rank, keepdims=False)
    channel_ids = quarter * channels + jnp.arange(channels, dtype=jnp.int32)
    alive = (channel_ids < live_count).astype(jnp.float32)
    energy = jnp.mean(real_part * real_part + imag_part * imag_part, axis=1)
    weight_scale = alive / jnp.sqrt(energy + 1e-06)
    own_spec = jnp.stack(
        [real_part * weight_scale[:, None], imag_part * weight_scale[:, None]], axis=1
    ).astype(jnp.bfloat16)
    lag_table = lag_weights(samples, first_bin, NF, NLAG)
    segment = lax.all_gather(own_spec[None], "pair", axis=0, tiled=True)
    squares_part, products_part = pair_stats(own_spec, segment, lag_table, angular)
    partner_ids = jnp.arange(segment.shape[0], dtype=jnp.int32)
    keep_mask = (partner_ids > block_rank).astype(jnp.float32)[:, None]
    new_squares = squares_part * keep_mask
    new_products = products_part * keep_mask
    eye_blocks = jnp.eye(nblock, dtype=jnp.float32)
    onehot = (jnp.arange(nblock, dtype=jnp.int32) == block_rank).astype(jnp.float32)
    sq_t = new_squares.T
    pr_t = new_products.T
    crossing = sq_t[:, None, :] * onehot[None, :, None]
    diag_vals = sq_t + onehot[None, :] * jnp.sum(sq_t, axis=1, keepdims=True)
    hessian = diag_vals[:, :, None] * eye_blocks[None] - crossing - jnp.swapaxes(crossing, 1, 2)
    gradient = onehot[None, :] * jnp.sum(pr_t, axis=1, keepdims=True) - pr_t
    hessian, gradient = lax.psum((hessian, gradient), "pair")
    diagonal = jnp.diagonal(hessian, axis1=1, axis2=2)
    trace_sum = lax.psum(jnp.sum(diagonal), "row")
    level_mean = trace_sum / (nblock * CB)
    damped = damping[0] * (diagonal + level_mean)
    system = hessian + damped[:, :, None] * eye_blocks[None]
    factor = jnp.linalg.cholesky(system)
    update = -jax.scipy.linalg.cho_solve((factor, True), gradient[:, :, None])[:, :, 0]
    return lax.dynamic_slice_in_dim(update, block_rank, 1, 1).T


LANES = 128
NBLOCK = 8
REACH = NBLOCK // 2
VMEM = pl.BlockSpec(memory_space=pltpu.VMEM)
HBM = pl.BlockSpec(memory_space=pltpu.HBM)


def pack_kernel(rec_hbm, off_hbm, out_hbm, held, off_ref, wide, sems, done):
    ndest, own, _, length = rec_hbm.shape
    cols = length // LANES
    parts = [pl.ds(col * own, own) for col in range(cols)] + [pl.ds(cols * own, 1)]
    leaving = [
        pltpu.make_async_copy(held.at[:, part], out_hbm.at[:, part], done.at[index])
        for index, part in enumerate(parts)
    ]
    offsets = pltpu.make_async_copy(off_hbm, off_ref, sems.at[cols])
    offsets.start()
    arriving = [
        pltpu.make_async_copy(
            rec_hbm.at[:, :, :, pl.ds(col * LANES, LANES)], held.at[:, parts[col]], sems.at[col]
        )
        for col in range(cols)
    ]
    for copy in arriving:
        copy.start()
    channels = off_ref.shape[1]
    wide[...] = jnp.zeros_like(wide)
    offsets.wait()
    wide[:, :channels] = jnp.broadcast_to(off_ref[...], (NBLOCK, channels))
    value = wide[...]
    high = value.astype(jnp.bfloat16).astype(jnp.float32)
    middle = (value - high).astype(jnp.bfloat16).astype(jnp.float32)
    low = value - high - middle
    pieces = high + pltpu.roll(middle, channels, 1) + pltpu.roll(low, 2 * channels, 1)
    for dest in range(ndest):
        tile = pieces if dest == 0 else pltpu.roll(pieces, LANES - dest * own, 1)
        held[dest, cols * own] = tile.astype(jnp.bfloat16)
    leaving[cols].start()
    for copy, onward in zip(arriving, leaving):
        copy.wait()
        onward.start()
    for copy in leaving:
        copy.wait()


def sin_cos(angle):
    square = angle * angle
    sine = jnp.float32(-1.0 / 39916800.0)
    for factor in (1.0 / 362880.0, -1.0 / 5040.0, 1.0 / 120.0, -1.0 / 6.0, 1.0):
        sine = sine * square + jnp.float32(factor)
    cosine = jnp.float32(1.0 / 479001600.0)
    for factor in (-1.0 / 3628800.0, 1.0 / 40320.0, -1.0 / 720.0, 1.0 / 24.0, -0.5, 1.0):
        cosine = cosine * square + jnp.float32(factor)
    return sine * angle, cosine


def unit_circle(phase, samples):
    phase = lax.bitwise_and(phase, samples - 1)
    phase = jnp.where(phase >= samples // 2, phase - samples, phase)
    sine, cosine = sin_cos(phase.astype(jnp.float32) * jnp.float32(math.pi / samples))
    return 1.0 - 2.0 * sine * sine, 2.0 * sine * cosine


def table_kernel(
    order, samples, counts_ref, damp_ref,
    high_ref, low_ref, turn_ref, ang_ref, lag_ref, live_ref, wide_ref, coarse,
):
    shards = len(order)
    length = samples // shards
    own = live_ref.shape[0]
    rows = 16
    first_bin = samples // 8

    def bins(height):
        return first_bin + lax.broadcasted_iota(jnp.int32, (height, NF), 1)

    def ids(height):
        return lax.broadcasted_iota(jnp.int32, (height, NF), 0)

    fine_cos, fine_sin = unit_circle(ids(rows) * bins(rows), samples)
    height = length // rows
    wide_cos, wide_sin = unit_circle(ids(height) * rows * bins(height), samples)
    coarse[pl.ds(0, height), :NF] = wide_cos
    coarse[pl.ds(0, height), NF:] = wide_sin

    @pl.loop(0, height)
    def _(step):
        row_cos = coarse[pl.ds(step, 1), :NF]
        row_sin = coarse[pl.ds(step, 1), NF:]
        at = pl.ds(pl.multiple_of(step * rows, rows), rows)
        for part, value in enumerate(
            (row_cos * fine_cos - row_sin * fine_sin, row_sin * fine_cos + row_cos * fine_sin)
        ):
            cut = pl.ds(part * NF, NF)
            high = value.astype(jnp.bfloat16)
            high_ref[at, cut] = high
            low_ref[at, cut] = (value - high.astype(jnp.float32)).astype(jnp.bfloat16)

    lags = NLAG // rows
    wide_cos, wide_sin = unit_circle((ids(lags) * rows + 1) * bins(lags), samples)
    coarse[pl.ds(0, lags), :NF] = wide_cos
    coarse[pl.ds(0, lags), NF:] = wide_sin
    centre = (lax.broadcasted_iota(jnp.int32, (1, NF), 1).astype(jnp.float32) + 0.5) * (
        math.pi / NF
    )
    _, weight = sin_cos(centre - jnp.float32(math.pi / 2))
    factor = -2.0 * (weight * weight)
    lag_cos = fine_cos * factor
    lag_sin = fine_sin * factor

    @pl.loop(0, lags)
    def _(step):
        row_cos = coarse[pl.ds(step, 1), :NF]
        row_sin = coarse[pl.ds(step, 1), NF:]
        at = pl.ds(pl.multiple_of(step * rows, rows), rows)
        lag_ref[at, :] = (row_sin * lag_cos + row_cos * lag_sin).astype(jnp.bfloat16)

    turn_cos, turn_sin = unit_circle(ids(shards) * length * bins(shards), samples)
    turn_ref[:, :NF] = turn_cos
    turn_ref[:, NF:] = turn_sin
    ang_ref[...] = bins(NBLOCK).astype(jnp.float32) * jnp.float32(2.0 * math.pi / samples)

    me = lax.axis_index("pair")
    slot = jnp.where(me == order[0], 0, jnp.where(me < order[0], me + 1, me))
    first_channel = (lax.axis_index("row") * shards + slot) * own
    block_ids = lax.broadcasted_iota(jnp.int32, (NBLOCK, LANES), 0)
    limit = jnp.zeros((NBLOCK, LANES), jnp.int32)
    for block in range(NBLOCK):
        limit = jnp.where(block_ids == block, counts_ref[block], limit)
    for c in range(own):
        live_ref[c] = (limit > first_channel + c).astype(jnp.float32)
    wide_ref[...] = jnp.full((NBLOCK, LANES), damp_ref[0], jnp.float32)


def stats_kernel(
    order, own, cols, x_ref, high_ref, low_ref, turn_ref, ang_ref, lag_ref, live_ref, out_ref,
    spectrum, re_ref, im_ref, stacked,
):
    shards = x_ref.shape[0]
    rows = own * NBLOCK
    signal = jnp.concatenate(
        [
            jnp.concatenate(
                [
                    jnp.concatenate(
                        [x_ref[shard, col * own + c].astype(jnp.float32) for col in range(cols)],
                        axis=1,
                    )
                    for c in range(own)
                ],
                axis=0,
            )
            for shard in range(shards)
        ],
        axis=0,
    ).astype(jnp.bfloat16)
    spectrum[...] = jnp.dot(
        signal, high_ref[...], preferred_element_type=jnp.float32
    ) + jnp.dot(signal, low_ref[...], preferred_element_type=jnp.float32)

    block_ids = lax.broadcasted_iota(jnp.int32, (NBLOCK, LANES), 0)
    pieces = jnp.zeros((NBLOCK, LANES), jnp.float32)
    for shard in range(shards):
        pieces = jnp.where(
            block_ids == order[shard], x_ref[shard, cols * own].astype(jnp.float32), pieces
        )
    channels = own * shards
    shift = (pieces + pltpu.roll(pieces, LANES - channels, 1)) + pltpu.roll(
        pieces, LANES - 2 * channels, 1
    )
    energy = [jnp.zeros((NBLOCK, 1), jnp.float32)] * own
    for col in range(NF // LANES):
        at = pl.ds(col * LANES, LANES)
        at_sine = pl.ds(NF + col * LANES, LANES)
        home = order.index(0)
        cosine_part = spectrum[pl.ds(home * rows, rows), at]
        sine_part = spectrum[pl.ds(home * rows, rows), at_sine]
        for shard in range(shards):
            if shard == home:
                continue
            turn_cos = turn_ref[pl.ds(order[shard], 1), at]
            turn_sin = turn_ref[pl.ds(order[shard], 1), at_sine]
            part_cos = spectrum[pl.ds(shard * rows, rows), at]
            part_sin = spectrum[pl.ds(shard * rows, rows), at_sine]
            cosine_part += turn_cos * part_cos - turn_sin * part_sin
            sine_part += turn_sin * part_cos + turn_cos * part_sin
        for c in range(own):
            piece = slice(c * NBLOCK, (c + 1) * NBLOCK)
            shift_sin, shift_cos = sin_cos(shift[:, c : c + 1] * ang_ref[:, at])
            real = cosine_part[piece] * shift_cos + sine_part[piece] * shift_sin
            imag = cosine_part[piece] * shift_sin - sine_part[piece] * shift_cos
            energy[c] += jnp.sum(real * real + imag * imag, axis=1, keepdims=True)
            re_ref[pl.ds(c * NBLOCK, NBLOCK), at] = real
            im_ref[pl.ds(c * NBLOCK, NBLOCK), at] = imag

    half = own * REACH * NBLOCK
    angular = ang_ref[...]
    for c in range(own):
        at = pl.ds(c * NBLOCK, NBLOCK)
        scale = live_ref[c][:, :1] / jnp.sqrt(energy[c] * (1.0 / NF) + 1e-06)
        real = (re_ref[at, :] * scale).astype(jnp.bfloat16).astype(jnp.float32)
        imag = (im_ref[at, :] * scale).astype(jnp.bfloat16).astype(jnp.float32)
        crossings = []
        for reach in range(1, REACH + 1):
            far_re = pltpu.roll(real, NBLOCK - reach, 0)
            far_im = pltpu.roll(imag, NBLOCK - reach, 0)
            cross_re = real * far_re + imag * far_im
            cross_im = imag * far_re - real * far_im
            crossings.append((cross_im, angular * cross_re))
        width = REACH * NBLOCK
        for part in range(2):
            stacked[pl.ds(part * half + c * width, width), :] = jnp.concatenate(
                [crossing[part] for crossing in crossings], axis=0
            ).astype(jnp.bfloat16)
    lagged = lax.dot_general(
        lag_ref[...], stacked[...], (((1,), (1,)), ((), ())), preferred_element_type=jnp.float32
    )
    residual = lagged[:, :half]
    jacobian = lagged[:, half:]
    squares = jnp.sum(jacobian * jacobian, axis=0, keepdims=True)
    products = jnp.sum(jacobian * residual, axis=0, keepdims=True)
    both = jnp.concatenate([squares, products], axis=0)
    out_ref[...] = jnp.broadcast_to(both[None], out_ref.shape)


def solve_kernel(order, own, total, got_ref, damp_ref, out_ref, steps):
    shards = got_ref.shape[0]
    quarter = lax.axis_index("row")
    me = lax.axis_index("pair")
    span = REACH * NBLOCK
    lane_ids = lax.broadcasted_iota(jnp.int32, (NBLOCK, LANES), 1)
    block_ids = lax.broadcasted_iota(jnp.int32, (NBLOCK, LANES), 0)

    summed = jnp.zeros((1, LANES), jnp.float32)
    for shard in range(shards):
        for other in range(got_ref.shape[1]):
            summed += got_ref[shard, other, 0:1, :]
    inner = (lane_ids[:1] % span) < (REACH - 1) * NBLOCK
    level = jnp.sum(jnp.where(inner, 2.0 * summed, summed), axis=1, keepdims=True) / total

    squares = jnp.concatenate(
        [got_ref[shard, quarter, 0:1, :] for shard in order], axis=0
    )
    products = jnp.concatenate(
        [got_ref[shard, quarter, 1:2, :] for shard in order], axis=0
    )

    def entry(array, reach, block):
        lane = (reach - 1) * NBLOCK + block
        return array if lane == 0 else pltpu.roll(array, LANES - lane, 1)

    weight = {}
    slope = {}
    for reach in range(1, REACH + 1):
        for block in range(NBLOCK if reach < REACH else NBLOCK // 2):
            far = (block + reach) % NBLOCK
            value = entry(squares, reach, block)
            weight[block, far] = value
            weight[far, block] = value
            value = entry(products, reach, block)
            slope[block, far] = value
            slope[far, block] = -value
    damping = damp_ref[...]
    matrix = {}
    right = []
    for a in range(NBLOCK):
        others = [b for b in range(NBLOCK) if b != a]
        diagonal = functools.reduce(lambda x, y: x + y, [weight[a, b] for b in others])
        matrix[a, a] = diagonal + damping * (diagonal + level)
        for b in range(a):
            matrix[a, b] = -weight[a, b]
        right.append(functools.reduce(lambda x, y: x + y, [slope[a, b] for b in others]))
    inverse = []
    for k in range(NBLOCK):
        inverse.append(1.0 / matrix[k, k])
        for i in range(k + 1, NBLOCK):
            ratio = matrix[i, k] * inverse[k]
            for j in range(k + 1, i + 1):
                matrix[i, j] = matrix[i, j] - ratio * matrix[j, k]
            right[i] = right[i] - ratio * right[k]
    step = [None] * NBLOCK
    for i in reversed(range(NBLOCK)):
        value = right[i]
        for j in range(i + 1, NBLOCK):
            value = value - matrix[j, i] * step[j]
        step[i] = value * inverse[i]
        steps[i] = -step[i]
    mine = steps[me]
    placed = jnp.zeros((NBLOCK, LANES), jnp.float32)
    for c in range(own):
        column = jnp.broadcast_to(mine[:, c * span : c * span + 1], (NBLOCK, LANES))
        placed = jnp.where(lane_ids == block_ids * own + c, column, placed)
    out_ref[...] = jnp.sum(placed, axis=0, keepdims=True)[:, : out_ref.shape[1]]


def room(mebibytes):
    return pltpu.CompilerParams(vmem_limit_bytes=mebibytes << 20)


def per_device(records, offsets, counts, damping):
    shards = lax.axis_size("pair")
    rows = lax.axis_size("row")
    channels, length, _ = records.shape
    samples = length * shards
    own = channels // shards
    cols = length // LANES
    tiles = own * cols + 1
    lead = shards // 2
    order = (lead, *range(lead), *range(lead + 1, shards))

    by_owner = jnp.transpose(records, (0, 2, 1)).reshape(shards, own, NBLOCK, length)
    payload = pl.pallas_call(
        pack_kernel,
        out_shape=jax.ShapeDtypeStruct((shards, tiles, NBLOCK, LANES), jnp.bfloat16),
        in_specs=[HBM, HBM],
        out_specs=HBM,
        scratch_shapes=[
            pltpu.VMEM((shards, tiles, NBLOCK, LANES), jnp.bfloat16),
            pltpu.VMEM((1, channels), jnp.float32),
            pltpu.VMEM((NBLOCK, LANES), jnp.float32),
            pltpu.SemaphoreType.DMA((cols + 1,)),
            pltpu.SemaphoreType.DMA((cols + 1,)),
        ],
        name="pack",
    )(by_owner, offsets)
    received = lax.all_to_all(
        payload, "pair", split_axis=0, concat_axis=0, tiled=True, axis_index_groups=[list(order)]
    )

    tables = pl.pallas_call(
        functools.partial(table_kernel, order, samples),
        out_shape=(
            jax.ShapeDtypeStruct((length, 2 * NF), jnp.bfloat16),
            jax.ShapeDtypeStruct((length, 2 * NF), jnp.bfloat16),
            jax.ShapeDtypeStruct((shards, 2 * NF), jnp.float32),
            jax.ShapeDtypeStruct((NBLOCK, NF), jnp.float32),
            jax.ShapeDtypeStruct((NLAG, NF), jnp.bfloat16),
            jax.ShapeDtypeStruct((own, NBLOCK, LANES), jnp.float32),
            jax.ShapeDtypeStruct((NBLOCK, LANES), jnp.float32),
        ),
        in_specs=[pl.BlockSpec(memory_space=pltpu.SMEM)] * 2,
        out_specs=(VMEM,) * 7,
        scratch_shapes=[pltpu.VMEM((max(length, NLAG) // 16, 2 * NF), jnp.float32)],
        compiler_params=room(8),
        name="tables",
    )(counts, damping)

    stats = pl.pallas_call(
        functools.partial(stats_kernel, order, own, cols),
        out_shape=jax.ShapeDtypeStruct((shards * rows, 2, LANES), jnp.float32),
        in_specs=[VMEM] * 7,
        out_specs=VMEM,
        scratch_shapes=[
            pltpu.VMEM((shards * own * NBLOCK, 2 * NF), jnp.float32),
            pltpu.VMEM((own * NBLOCK, NF), jnp.float32),
            pltpu.VMEM((own * NBLOCK, NF), jnp.float32),
            pltpu.VMEM((2 * own * REACH * NBLOCK, NF), jnp.bfloat16),
        ],
        compiler_params=room(12),
        name="stats",
    )(received, *tables[:6])
    gathered = lax.all_to_all(stats, ("pair", "row"), split_axis=0, concat_axis=0, tiled=True)
    gathered = gathered.reshape(shards, rows, 2, LANES)
    return pl.pallas_call(
        functools.partial(solve_kernel, order, own, float(NBLOCK * CB)),
        out_shape=jax.ShapeDtypeStruct((1, channels), jnp.float32),
        in_specs=[VMEM, VMEM],
        out_specs=VMEM,
        scratch_shapes=[pltpu.VMEM((NBLOCK, NBLOCK, LANES), jnp.float32)],
        compiler_params=room(4),
        name="solve",
    )(gathered, tables[6])


def body(records, offsets, counts, damping):
    shards = lax.axis_size("pair")
    channels, length, nblock = records.shape
    own = channels // shards
    whole = own * shards == channels and own * REACH * NBLOCK == LANES
    even = length % LANES == 0 and length & (length - 1) == 0
    if shards == NBLOCK and nblock == NBLOCK and whole and even:
        return per_device(records, offsets, counts, damping)
    return per_device_general(records, offsets, counts, damping)


def solution(mesh):
    return jax.shard_map(
        body,
        mesh=mesh,
        in_specs=(P("row", "pair", None), P("pair", "row"), P(), P()),
        out_specs=P("pair", "row"),
        check_vma=False,
    )
```

```python
import functools
import math

import jax
import jax.numpy as jnp
import numpy as np
from jax import lax
from jax.experimental import pallas as pl
from jax.experimental.pallas import tpu as pltpu
from jax.sharding import PartitionSpec as P

CB = 128
NF = 512
NLAG = 256


def band_table(row_start, row_count, samples, first_bin, freq_count):
    sample_ids = row_start + jnp.arange(row_count, dtype=jnp.int32)
    freq_bins = first_bin + jnp.arange(freq_count, dtype=jnp.int32)
    phase_ids = sample_ids[:, None] * freq_bins[None, :] % samples
    angles = phase_ids.astype(jnp.float32) * (2.0 * math.pi / samples)
    return jnp.concatenate([jnp.cos(angles), jnp.sin(angles)], axis=1)


def lag_weights(samples, first_bin, freq_count, lag_count):
    freq_bins = first_bin + jnp.arange(freq_count, dtype=jnp.int32)
    lag_ids = 1 + jnp.arange(lag_count, dtype=jnp.int32)
    phase_ids = freq_bins[:, None] * lag_ids[None, :] % samples
    angles = phase_ids.astype(jnp.float32) * (2.0 * math.pi / samples)
    centre = (jnp.arange(freq_count, dtype=jnp.float32) + 0.5) * (math.pi / freq_count)
    weight = jnp.sin(centre) ** 2
    return (-2.0 * weight[:, None] * jnp.sin(angles)).astype(jnp.bfloat16)


def pair_stats(own_spec, partners, lag_table, angular):
    own_re = own_spec[:, 0].astype(jnp.float32)
    own_im = own_spec[:, 1].astype(jnp.float32)
    far_re = partners[:, :, 0].astype(jnp.float32)
    far_im = partners[:, :, 1].astype(jnp.float32)
    cross_re = own_re * far_re + own_im * far_im
    cross_im = own_im * far_re - own_re * far_im
    stacked = jnp.stack([cross_im, angular * cross_re]).astype(jnp.bfloat16)
    lagged = jnp.dot(stacked, lag_table, preferred_element_type=jnp.float32)
    residual = lagged[0]
    jacobian = lagged[1]
    return (jnp.sum(jacobian * jacobian, axis=-1), jnp.sum(jacobian * residual, axis=-1))


def per_device_general(records, offsets, counts, damping):
    nblock = lax.axis_size("pair")
    block_rank = lax.axis_index("pair")
    quarter = lax.axis_index("row")
    relaid = lax.all_to_all(records, "pair", split_axis=2, concat_axis=1, tiled=True)
    signal = relaid[:, :, 0]
    channels = signal.shape[0]
    samples = signal.shape[1]
    first_bin = samples // 8
    block_len = samples // 8

    def accumulate(partial_value, turn_index):
        first_row = turn_index * block_len
        segment = lax.dynamic_slice_in_dim(signal, first_row, block_len, 1)
        dft_table = band_table(first_row, block_len, samples, first_bin, NF)
        table_high = dft_table.astype(jnp.bfloat16)
        table_low = (dft_table - table_high.astype(jnp.float32)).astype(jnp.bfloat16)
        partial_value = partial_value + jnp.dot(
            segment, table_high, preferred_element_type=jnp.float32
        )
        partial_value = partial_value + jnp.dot(
            segment, table_low, preferred_element_type=jnp.float32
        )
        return (partial_value, None)

    spectrum, _ = lax.scan(
        accumulate, jnp.zeros((channels, 2 * NF), jnp.float32), jnp.arange(8, dtype=jnp.int32)
    )
    cosine_part = spectrum[:, :NF]
    sine_part = spectrum[:, NF:]
    angular = (first_bin + jnp.arange(NF, dtype=jnp.int32)).astype(jnp.float32) * (
        2.0 * math.pi / samples
    )
    shift_angle = offsets[0][:, None] * angular[None, :]
    shift_cos = jnp.cos(shift_angle)
    shift_sin = jnp.sin(shift_angle)
    real_part = cosine_part * shift_cos + sine_part * shift_sin
    imag_part = cosine_part * shift_sin - sine_part * shift_cos
    live_count = lax.dynamic_index_in_dim(counts, block_rank, keepdims=False)
    channel_ids = quarter * channels + jnp.arange(channels, dtype=jnp.int32)
    alive = (channel_ids < live_count).astype(jnp.float32)
    energy = jnp.mean(real_part * real_part + imag_part * imag_part, axis=1)
    weight_scale = alive / jnp.sqrt(energy + 1e-06)
    own_spec = jnp.stack(
        [real_part * weight_scale[:, None], imag_part * weight_scale[:, None]], axis=1
    ).astype(jnp.bfloat16)
    lag_table = lag_weights(samples, first_bin, NF, NLAG)
    segment = lax.all_gather(own_spec[None], "pair", axis=0, tiled=True)
    squares_part, products_part = pair_stats(own_spec, segment, lag_table, angular)
    partner_ids = jnp.arange(segment.shape[0], dtype=jnp.int32)
    keep_mask = (partner_ids > block_rank).astype(jnp.float32)[:, None]
    new_squares = squares_part * keep_mask
    new_products = products_part * keep_mask
    eye_blocks = jnp.eye(nblock, dtype=jnp.float32)
    onehot = (jnp.arange(nblock, dtype=jnp.int32) == block_rank).astype(jnp.float32)
    sq_t = new_squares.T
    pr_t = new_products.T
    crossing = sq_t[:, None, :] * onehot[None, :, None]
    diag_vals = sq_t + onehot[None, :] * jnp.sum(sq_t, axis=1, keepdims=True)
    hessian = diag_vals[:, :, None] * eye_blocks[None] - crossing - jnp.swapaxes(crossing, 1, 2)
    gradient = onehot[None, :] * jnp.sum(pr_t, axis=1, keepdims=True) - pr_t
    hessian, gradient = lax.psum((hessian, gradient), "pair")
    diagonal = jnp.diagonal(hessian, axis1=1, axis2=2)
    trace_sum = lax.psum(jnp.sum(diagonal), "row")
    level_mean = trace_sum / (nblock * CB)
    damped = damping[0] * (diagonal + level_mean)
    system = hessian + damped[:, :, None] * eye_blocks[None]
    factor = jnp.linalg.cholesky(system)
    update = -jax.scipy.linalg.cho_solve((factor, True), gradient[:, :, None])[:, :, 0]
    return lax.dynamic_slice_in_dim(update, block_rank, 1, 1).T


LANES = 128
NBLOCK = 8
REACH = NBLOCK // 2
VMEM = pl.BlockSpec(memory_space=pltpu.VMEM)
HBM = pl.BlockSpec(memory_space=pltpu.HBM)


ORDERS = 88
HALF = LANES // 2
SPARE = 2 * ORDERS - LANES


def two_pieces(table):
    table = (np.round(table * 2.0**22) / 2.0**22).astype(np.float32)
    high = table.astype(jnp.bfloat16)
    low = (table - high.astype(np.float32)).astype(jnp.bfloat16)
    return np.concatenate([high, low], axis=1)


@functools.cache
def band_factors(length, samples):
    times = np.arange(length, dtype=np.float64)
    bins = samples // 8 + np.arange(NF)
    centre = samples // 8 + NF // 2
    main = ((length - 1 - 2 * times) / 2) ** 2 * math.cos(math.pi * NF / samples)
    side = times[1:] * (length - times[1:]) / 2
    _, vectors = np.linalg.eigh(np.diag(main) + np.diag(side, 1) + np.diag(side, -1))
    vectors = vectors[:, ::-1][:, :ORDERS]
    ids = np.arange(length)
    inner = 2.0 * math.pi * (ids[:, None] * (bins - centre)[None, :] % samples) / samples
    real = vectors.T @ np.cos(inner)
    imag = vectors.T @ np.sin(inner)
    carrier = 2.0 * math.pi * (ids * centre % samples)[:, None] / samples
    first = [vectors * np.cos(carrier), vectors * np.sin(carrier)]
    second = [np.concatenate([real, imag], axis=1), np.concatenate([-imag, real], axis=1)]
    upper = np.concatenate([first[0][:, HALF:], first[1][:, HALF:]], axis=1)
    upper = np.pad(upper, ((0, 0), (0, HALF - SPARE)))
    basis = np.concatenate([first[0][:, :HALF], first[1][:, :HALF], upper, upper], axis=1)
    upper = np.concatenate([second[0][HALF:], second[1][HALF:]], axis=0)
    upper = np.pad(upper, ((0, HALF - SPARE), (0, 0)))
    band = np.concatenate([second[0][:HALF], second[1][:HALF], upper, upper], axis=0)
    return two_pieces(basis), two_pieces(band)


def lanes_of(height):
    return lax.broadcasted_iota(jnp.int32, (height, LANES), 1)


def pack_kernel(
    rec_hbm, off_hbm, basis_hbm, out_hbm, rec_ref, off_ref, basis_ref, held, wide, arrive, leave
):
    ndest, own, _, length = rec_hbm.shape
    rows = own * NBLOCK
    late = rows // 2
    copies = [
        pltpu.make_async_copy(source, target, arrive.at[index])
        for index, (source, target) in enumerate(
            ((off_hbm, off_ref), (rec_hbm, rec_ref), (basis_hbm, basis_ref))
        )
    ]
    for copy in copies:
        copy.start()
    channels = off_ref.shape[1]
    wide[...] = jnp.zeros_like(wide)
    copies[0].wait()
    wide[:, :channels] = jnp.broadcast_to(off_ref[...], (NBLOCK, channels))
    value = wide[...]
    high = value.astype(jnp.bfloat16).astype(jnp.float32)
    middle = (value - high).astype(jnp.bfloat16).astype(jnp.float32)
    pieces = (high, middle, value - high - middle)
    place = lanes_of(NBLOCK)
    shifts = []
    for dest in range(ndest):
        tile = jnp.zeros_like(value)
        for index, piece in enumerate(pieces):
            start = SPARE + index * own
            moved = pltpu.roll(piece, (start - dest * own) % LANES, 1)
            tile = jnp.where((place >= start) & (place < start + own), moved, tile)
        shifts.append(jnp.concatenate([tile] * (late // NBLOCK), axis=0))
    first = lanes_of(late) < HALF
    plain = (lanes_of(late) < SPARE) | (lanes_of(late) >= SPARE + 3 * own)
    copies[1].wait()
    copies[2].wait()
    width = 2 * LANES
    signal = rec_ref[...].astype(jnp.float32).reshape(ndest * rows, length).astype(jnp.bfloat16)
    found = jnp.dot(
        signal, basis_ref[:, :width], preferred_element_type=jnp.float32
    ) + jnp.dot(signal, basis_ref[:, width:], preferred_element_type=jnp.float32)
    for dest in range(ndest):
        mine = found[dest * rows : (dest + 1) * rows]
        held[dest, :rows] = mine[:, :LANES].astype(jnp.bfloat16)
        upper = jnp.where(first, mine[:late, LANES:], mine[late:, LANES:])
        held[dest, rows:] = jnp.where(plain, upper, shifts[dest]).astype(jnp.bfloat16)
    onward = pltpu.make_async_copy(held, out_hbm, leave)
    onward.start()
    onward.wait()


def sin_cos(angle):
    square = angle * angle
    sine = jnp.float32(-1.0 / 39916800.0)
    for factor in (1.0 / 362880.0, -1.0 / 5040.0, 1.0 / 120.0, -1.0 / 6.0, 1.0):
        sine = sine * square + jnp.float32(factor)
    cosine = jnp.float32(1.0 / 479001600.0)
    for factor in (-1.0 / 3628800.0, 1.0 / 40320.0, -1.0 / 720.0, 1.0 / 24.0, -0.5, 1.0):
        cosine = cosine * square + jnp.float32(factor)
    return sine * angle, cosine


def unit_circle(phase, samples):
    phase = lax.bitwise_and(phase, samples - 1)
    phase = jnp.where(phase >= samples // 2, phase - samples, phase)
    sine, cosine = sin_cos(phase.astype(jnp.float32) * jnp.float32(math.pi / samples))
    return 1.0 - 2.0 * sine * sine, 2.0 * sine * cosine


def table_kernel(
    order, samples, counts_ref, damp_ref, band_ref,
    both_ref, turn_ref, ang_ref, lag_ref, live_ref, wide_ref, coarse,
):
    shards = len(order)
    length = samples // shards
    own = live_ref.shape[0]
    rows = 16
    first_bin = samples // 8
    both_ref[...] = band_ref[...]

    def bins(height):
        return first_bin + lax.broadcasted_iota(jnp.int32, (height, NF), 1)

    def ids(height):
        return lax.broadcasted_iota(jnp.int32, (height, NF), 0)

    fine_cos, fine_sin = unit_circle(ids(rows) * bins(rows), samples)
    lags = NLAG // rows
    wide_cos, wide_sin = unit_circle((ids(lags) * rows + 1) * bins(lags), samples)
    coarse[:, :NF] = wide_cos
    coarse[:, NF:] = wide_sin
    centre = (lax.broadcasted_iota(jnp.int32, (1, NF), 1).astype(jnp.float32) + 0.5) * (
        math.pi / NF
    )
    _, weight = sin_cos(centre - jnp.float32(math.pi / 2))
    factor = -2.0 * (weight * weight)
    lag_cos = fine_cos * factor
    lag_sin = fine_sin * factor

    @pl.loop(0, lags)
    def _(step):
        row_cos = coarse[pl.ds(step, 1), :NF]
        row_sin = coarse[pl.ds(step, 1), NF:]
        at = pl.ds(pl.multiple_of(step * rows, rows), rows)
        lag_ref[at, :] = (row_sin * lag_cos + row_cos * lag_sin).astype(jnp.bfloat16)

    turn_cos, turn_sin = unit_circle(ids(shards) * length * bins(shards), samples)
    turn_ref[:, :NF] = turn_cos
    turn_ref[:, NF:] = turn_sin
    ang_ref[...] = bins(NBLOCK).astype(jnp.float32) * jnp.float32(2.0 * math.pi / samples)

    me = lax.axis_index("pair")
    slot = jnp.where(me == order[0], 0, jnp.where(me < order[0], me + 1, me))
    first_channel = (lax.axis_index("row") * shards + slot) * own
    block_ids = lax.broadcasted_iota(jnp.int32, (NBLOCK, LANES), 0)
    limit = jnp.zeros((NBLOCK, LANES), jnp.int32)
    for block in range(NBLOCK):
        limit = jnp.where(block_ids == block, counts_ref[block], limit)
    for c in range(own):
        live_ref[c] = (limit > first_channel + c).astype(jnp.float32)
    wide_ref[...] = jnp.full((NBLOCK, LANES), damp_ref[0], jnp.float32)


def stats_kernel(
    order, x_ref, band_ref, turn_ref, ang_ref, lag_ref, live_ref, out_ref,
    spectrum, re_ref, im_ref, stacked,
):
    shards = x_ref.shape[0]
    own = live_ref.shape[0]
    rows = own * NBLOCK
    late = rows // 2
    first = (lanes_of(late) < HALF).astype(jnp.float32)
    parts = []
    for shard in range(shards):
        upper = x_ref[shard, rows:].astype(jnp.float32)
        upper = jnp.concatenate([upper * first, upper * (1.0 - first)], axis=0)
        parts.append(jnp.concatenate([x_ref[shard, :rows], upper.astype(jnp.bfloat16)], axis=1))
    found = jnp.concatenate(parts, axis=0)
    spectrum[...] = jnp.dot(
        found, band_ref[:, : 2 * NF], preferred_element_type=jnp.float32
    ) + jnp.dot(found, band_ref[:, 2 * NF :], preferred_element_type=jnp.float32)

    block_ids = lax.broadcasted_iota(jnp.int32, (NBLOCK, LANES), 0)
    pieces = jnp.zeros((NBLOCK, LANES), jnp.float32)
    for shard in range(shards):
        pieces = jnp.where(
            block_ids == order[shard],
            x_ref[shard, pl.ds(rows, NBLOCK)].astype(jnp.float32),
            pieces,
        )
    shift = (pieces + pltpu.roll(pieces, LANES - own, 1)) + pltpu.roll(
        pieces, LANES - 2 * own, 1
    )
    energy = [jnp.zeros((NBLOCK, 1), jnp.float32)] * own
    for col in range(NF // LANES):
        at = pl.ds(col * LANES, LANES)
        at_sine = pl.ds(NF + col * LANES, LANES)
        home = order.index(0)
        cosine_part = spectrum[pl.ds(home * rows, rows), at]
        sine_part = spectrum[pl.ds(home * rows, rows), at_sine]
        for shard in range(shards):
            if shard == home:
                continue
            turn_cos = turn_ref[pl.ds(order[shard], 1), at]
            turn_sin = turn_ref[pl.ds(order[shard], 1), at_sine]
            part_cos = spectrum[pl.ds(shard * rows, rows), at]
            part_sin = spectrum[pl.ds(shard * rows, rows), at_sine]
            cosine_part += turn_cos * part_cos - turn_sin * part_sin
            sine_part += turn_sin * part_cos + turn_cos * part_sin
        for c in range(own):
            piece = slice(c * NBLOCK, (c + 1) * NBLOCK)
            shift_sin, shift_cos = sin_cos(
                shift[:, SPARE + c : SPARE + c + 1] * ang_ref[:, at]
            )
            real = cosine_part[piece] * shift_cos + sine_part[piece] * shift_sin
            imag = cosine_part[piece] * shift_sin - sine_part[piece] * shift_cos
            energy[c] += jnp.sum(real * real + imag * imag, axis=1, keepdims=True)
            re_ref[pl.ds(c * NBLOCK, NBLOCK), at] = real
            im_ref[pl.ds(c * NBLOCK, NBLOCK), at] = imag

    half = own * REACH * NBLOCK
    angular = ang_ref[...]
    for c in range(own):
        at = pl.ds(c * NBLOCK, NBLOCK)
        scale = live_ref[c][:, :1] / jnp.sqrt(energy[c] * (1.0 / NF) + 1e-06)
        real = (re_ref[at, :] * scale).astype(jnp.bfloat16).astype(jnp.float32)
        imag = (im_ref[at, :] * scale).astype(jnp.bfloat16).astype(jnp.float32)
        crossings = []
        for reach in range(1, REACH + 1):
            far_re = pltpu.roll(real, NBLOCK - reach, 0)
            far_im = pltpu.roll(imag, NBLOCK - reach, 0)
            cross_re = real * far_re + imag * far_im
            cross_im = imag * far_re - real * far_im
            crossings.append((cross_im, angular * cross_re))
        width = REACH * NBLOCK
        for part in range(2):
            stacked[pl.ds(part * half + c * width, width), :] = jnp.concatenate(
                [crossing[part] for crossing in crossings], axis=0
            ).astype(jnp.bfloat16)
    lagged = lax.dot_general(
        lag_ref[...], stacked[...], (((1,), (1,)), ((), ())), preferred_element_type=jnp.float32
    )
    residual = lagged[:, :half]
    jacobian = lagged[:, half:]
    squares = jnp.sum(jacobian * jacobian, axis=0, keepdims=True)
    products = jnp.sum(jacobian * residual, axis=0, keepdims=True)
    both = jnp.concatenate([squares, products], axis=0)
    out_ref[...] = jnp.broadcast_to(both[None], out_ref.shape)


def solve_kernel(order, own, total, got_ref, damp_ref, out_ref, steps):
    shards = got_ref.shape[0]
    quarter = lax.axis_index("row")
    me = lax.axis_index("pair")
    span = REACH * NBLOCK
    lane_ids = lax.broadcasted_iota(jnp.int32, (NBLOCK, LANES), 1)
    block_ids = lax.broadcasted_iota(jnp.int32, (NBLOCK, LANES), 0)

    summed = jnp.zeros((1, LANES), jnp.float32)
    for shard in range(shards):
        for other in range(got_ref.shape[1]):
            summed += got_ref[shard, other, 0:1, :]
    inner = (lane_ids[:1] % span) < (REACH - 1) * NBLOCK
    level = jnp.sum(jnp.where(inner, 2.0 * summed, summed), axis=1, keepdims=True) / total

    squares = jnp.concatenate(
        [got_ref[shard, quarter, 0:1, :] for shard in order], axis=0
    )
    products = jnp.concatenate(
        [got_ref[shard, quarter, 1:2, :] for shard in order], axis=0
    )

    def entry(array, reach, block):
        lane = (reach - 1) * NBLOCK + block
        return array if lane == 0 else pltpu.roll(array, LANES - lane, 1)

    weight = {}
    slope = {}
    for reach in range(1, REACH + 1):
        for block in range(NBLOCK if reach < REACH else NBLOCK // 2):
            far = (block + reach) % NBLOCK
            value = entry(squares, reach, block)
            weight[block, far] = value
            weight[far, block] = value
            value = entry(products, reach, block)
            slope[block, far] = value
            slope[far, block] = -value
    damping = damp_ref[...]
    matrix = {}
    right = []
    for a in range(NBLOCK):
        others = [b for b in range(NBLOCK) if b != a]
        diagonal = functools.reduce(lambda x, y: x + y, [weight[a, b] for b in others])
        matrix[a, a] = diagonal + damping * (diagonal + level)
        for b in range(a):
            matrix[a, b] = -weight[a, b]
        right.append(functools.reduce(lambda x, y: x + y, [slope[a, b] for b in others]))
    inverse = []
    for k in range(NBLOCK):
        inverse.append(1.0 / matrix[k, k])
        for i in range(k + 1, NBLOCK):
            ratio = matrix[i, k] * inverse[k]
            for j in range(k + 1, i + 1):
                matrix[i, j] = matrix[i, j] - ratio * matrix[j, k]
            right[i] = right[i] - ratio * right[k]
    step = [None] * NBLOCK
    for i in reversed(range(NBLOCK)):
        value = right[i]
        for j in range(i + 1, NBLOCK):
            value = value - matrix[j, i] * step[j]
        step[i] = value * inverse[i]
        steps[i] = -step[i]
    mine = steps[me]
    placed = jnp.zeros((NBLOCK, LANES), jnp.float32)
    for c in range(own):
        column = jnp.broadcast_to(mine[:, c * span : c * span + 1], (NBLOCK, LANES))
        placed = jnp.where(lane_ids == block_ids * own + c, column, placed)
    out_ref[...] = jnp.sum(placed, axis=0, keepdims=True)[:, : out_ref.shape[1]]


def room(mebibytes):
    return pltpu.CompilerParams(vmem_limit_bytes=mebibytes << 20)


def per_device(records, offsets, counts, damping):
    shards = lax.axis_size("pair")
    rows = lax.axis_size("row")
    channels, length, _ = records.shape
    samples = length * shards
    own = channels // shards
    height = own * NBLOCK + own * NBLOCK // 2
    basis, band = band_factors(length, samples)
    lead = shards // 2
    order = (lead, *range(lead), *range(lead + 1, shards))

    by_owner = jnp.transpose(records, (0, 2, 1)).reshape(shards, own, NBLOCK, length)
    payload = pl.pallas_call(
        pack_kernel,
        out_shape=jax.ShapeDtypeStruct((shards, height, LANES), jnp.bfloat16),
        in_specs=[HBM, HBM, HBM],
        out_specs=HBM,
        scratch_shapes=[
            pltpu.VMEM((shards, own, NBLOCK, length), jnp.bfloat16),
            pltpu.VMEM((1, channels), jnp.float32),
            pltpu.VMEM(basis.shape, jnp.bfloat16),
            pltpu.VMEM((shards, height, LANES), jnp.bfloat16),
            pltpu.VMEM((NBLOCK, LANES), jnp.float32),
            pltpu.SemaphoreType.DMA((3,)),
            pltpu.SemaphoreType.DMA,
        ],
        name="pack",
    )(by_owner, offsets, jnp.asarray(basis))
    received = lax.all_to_all(
        payload, "pair", split_axis=0, concat_axis=0, tiled=True, axis_index_groups=[list(order)]
    )

    tables = pl.pallas_call(
        functools.partial(table_kernel, order, samples),
        out_shape=(
            jax.ShapeDtypeStruct(band.shape, jnp.bfloat16),
            jax.ShapeDtypeStruct((shards, 2 * NF), jnp.float32),
            jax.ShapeDtypeStruct((NBLOCK, NF), jnp.float32),
            jax.ShapeDtypeStruct((NLAG, NF), jnp.bfloat16),
            jax.ShapeDtypeStruct((own, NBLOCK, LANES), jnp.float32),
            jax.ShapeDtypeStruct((NBLOCK, LANES), jnp.float32),
        ),
        in_specs=[pl.BlockSpec(memory_space=pltpu.SMEM)] * 2 + [VMEM],
        out_specs=(VMEM,) * 6,
        scratch_shapes=[pltpu.VMEM((NLAG // 16, 2 * NF), jnp.float32)],
        compiler_params=room(8),
        name="tables",
    )(counts, damping, jnp.asarray(band))

    stats = pl.pallas_call(
        functools.partial(stats_kernel, order),
        out_shape=jax.ShapeDtypeStruct((shards * rows, 2, LANES), jnp.float32),
        in_specs=[VMEM] * 6,
        out_specs=VMEM,
        scratch_shapes=[
            pltpu.VMEM((shards * own * NBLOCK, 2 * NF), jnp.float32),
            pltpu.VMEM((own * NBLOCK, NF), jnp.float32),
            pltpu.VMEM((own * NBLOCK, NF), jnp.float32),
            pltpu.VMEM((2 * own * REACH * NBLOCK, NF), jnp.bfloat16),
        ],
        compiler_params=room(12),
        name="stats",
    )(received, *tables[:5])
    gathered = lax.all_to_all(stats, ("pair", "row"), split_axis=0, concat_axis=0, tiled=True)
    gathered = gathered.reshape(shards, rows, 2, LANES)
    return pl.pallas_call(
        functools.partial(solve_kernel, order, own, float(NBLOCK * CB)),
        out_shape=jax.ShapeDtypeStruct((1, channels), jnp.float32),
        in_specs=[VMEM, VMEM],
        out_specs=VMEM,
        scratch_shapes=[pltpu.VMEM((NBLOCK, NBLOCK, LANES), jnp.float32)],
        compiler_params=room(4),
        name="solve",
    )(gathered, tables[5])


def body(records, offsets, counts, damping):
    shards = lax.axis_size("pair")
    channels, length, nblock = records.shape
    own = channels // shards
    whole = own * shards == channels and own * REACH * NBLOCK == LANES
    even = length & (length - 1) == 0 and length == NF
    if shards == NBLOCK and nblock == NBLOCK and whole and even:
        return per_device(records, offsets, counts, damping)
    return per_device_general(records, offsets, counts, damping)


def solution(mesh):
    return jax.shard_map(
        body,
        mesh=mesh,
        in_specs=(P("row", "pair", None), P("pair", "row"), P(), P()),
        out_specs=P("pair", "row"),
        check_vma=False,
    )
```

```python
import functools
import math

import jax
import jax.numpy as jnp
import numpy as np
from jax import lax
from jax.experimental import pallas as pl
from jax.experimental.pallas import tpu as pltpu
from jax.sharding import PartitionSpec as P

CB = 128
NF = 512
NLAG = 256


def band_table(row_start, row_count, samples, first_bin, freq_count):
    sample_ids = row_start + jnp.arange(row_count, dtype=jnp.int32)
    freq_bins = first_bin + jnp.arange(freq_count, dtype=jnp.int32)
    phase_ids = sample_ids[:, None] * freq_bins[None, :] % samples
    angles = phase_ids.astype(jnp.float32) * (2.0 * math.pi / samples)
    return jnp.concatenate([jnp.cos(angles), jnp.sin(angles)], axis=1)


def lag_weights(samples, first_bin, freq_count, lag_count):
    freq_bins = first_bin + jnp.arange(freq_count, dtype=jnp.int32)
    lag_ids = 1 + jnp.arange(lag_count, dtype=jnp.int32)
    phase_ids = freq_bins[:, None] * lag_ids[None, :] % samples
    angles = phase_ids.astype(jnp.float32) * (2.0 * math.pi / samples)
    centre = (jnp.arange(freq_count, dtype=jnp.float32) + 0.5) * (math.pi / freq_count)
    weight = jnp.sin(centre) ** 2
    return (-2.0 * weight[:, None] * jnp.sin(angles)).astype(jnp.bfloat16)


def pair_stats(own_spec, partners, lag_table, angular):
    own_re = own_spec[:, 0].astype(jnp.float32)
    own_im = own_spec[:, 1].astype(jnp.float32)
    far_re = partners[:, :, 0].astype(jnp.float32)
    far_im = partners[:, :, 1].astype(jnp.float32)
    cross_re = own_re * far_re + own_im * far_im
    cross_im = own_im * far_re - own_re * far_im
    stacked = jnp.stack([cross_im, angular * cross_re]).astype(jnp.bfloat16)
    lagged = jnp.dot(stacked, lag_table, preferred_element_type=jnp.float32)
    residual = lagged[0]
    jacobian = lagged[1]
    return (jnp.sum(jacobian * jacobian, axis=-1), jnp.sum(jacobian * residual, axis=-1))


def per_device_general(records, offsets, counts, damping):
    nblock = lax.axis_size("pair")
    block_rank = lax.axis_index("pair")
    quarter = lax.axis_index("row")
    relaid = lax.all_to_all(records, "pair", split_axis=2, concat_axis=1, tiled=True)
    signal = relaid[:, :, 0]
    channels = signal.shape[0]
    samples = signal.shape[1]
    first_bin = samples // 8
    block_len = samples // 8

    def accumulate(partial_value, turn_index):
        first_row = turn_index * block_len
        segment = lax.dynamic_slice_in_dim(signal, first_row, block_len, 1)
        dft_table = band_table(first_row, block_len, samples, first_bin, NF)
        table_high = dft_table.astype(jnp.bfloat16)
        table_low = (dft_table - table_high.astype(jnp.float32)).astype(jnp.bfloat16)
        partial_value = partial_value + jnp.dot(
            segment, table_high, preferred_element_type=jnp.float32
        )
        partial_value = partial_value + jnp.dot(
            segment, table_low, preferred_element_type=jnp.float32
        )
        return (partial_value, None)

    spectrum, _ = lax.scan(
        accumulate, jnp.zeros((channels, 2 * NF), jnp.float32), jnp.arange(8, dtype=jnp.int32)
    )
    cosine_part = spectrum[:, :NF]
    sine_part = spectrum[:, NF:]
    angular = (first_bin + jnp.arange(NF, dtype=jnp.int32)).astype(jnp.float32) * (
        2.0 * math.pi / samples
    )
    shift_angle = offsets[0][:, None] * angular[None, :]
    shift_cos = jnp.cos(shift_angle)
    shift_sin = jnp.sin(shift_angle)
    real_part = cosine_part * shift_cos + sine_part * shift_sin
    imag_part = cosine_part * shift_sin - sine_part * shift_cos
    live_count = lax.dynamic_index_in_dim(counts, block_rank, keepdims=False)
    channel_ids = quarter * channels + jnp.arange(channels, dtype=jnp.int32)
    alive = (channel_ids < live_count).astype(jnp.float32)
    energy = jnp.mean(real_part * real_part + imag_part * imag_part, axis=1)
    weight_scale = alive / jnp.sqrt(energy + 1e-06)
    own_spec = jnp.stack(
        [real_part * weight_scale[:, None], imag_part * weight_scale[:, None]], axis=1
    ).astype(jnp.bfloat16)
    lag_table = lag_weights(samples, first_bin, NF, NLAG)
    segment = lax.all_gather(own_spec[None], "pair", axis=0, tiled=True)
    squares_part, products_part = pair_stats(own_spec, segment, lag_table, angular)
    partner_ids = jnp.arange(segment.shape[0], dtype=jnp.int32)
    keep_mask = (partner_ids > block_rank).astype(jnp.float32)[:, None]
    new_squares = squares_part * keep_mask
    new_products = products_part * keep_mask
    eye_blocks = jnp.eye(nblock, dtype=jnp.float32)
    onehot = (jnp.arange(nblock, dtype=jnp.int32) == block_rank).astype(jnp.float32)
    sq_t = new_squares.T
    pr_t = new_products.T
    crossing = sq_t[:, None, :] * onehot[None, :, None]
    diag_vals = sq_t + onehot[None, :] * jnp.sum(sq_t, axis=1, keepdims=True)
    hessian = diag_vals[:, :, None] * eye_blocks[None] - crossing - jnp.swapaxes(crossing, 1, 2)
    gradient = onehot[None, :] * jnp.sum(pr_t, axis=1, keepdims=True) - pr_t
    hessian, gradient = lax.psum((hessian, gradient), "pair")
    diagonal = jnp.diagonal(hessian, axis1=1, axis2=2)
    trace_sum = lax.psum(jnp.sum(diagonal), "row")
    level_mean = trace_sum / (nblock * CB)
    damped = damping[0] * (diagonal + level_mean)
    system = hessian + damped[:, :, None] * eye_blocks[None]
    factor = jnp.linalg.cholesky(system)
    update = -jax.scipy.linalg.cho_solve((factor, True), gradient[:, :, None])[:, :, 0]
    return lax.dynamic_slice_in_dim(update, block_rank, 1, 1).T


LANES = 128
NBLOCK = 8
REACH = NBLOCK // 2
VMEM = pl.BlockSpec(memory_space=pltpu.VMEM)


ORDERS = 88
HALF = LANES // 2
SPARE = 2 * ORDERS - LANES


def two_pieces(table):
    table = (np.round(table * 2.0**22) / 2.0**22).astype(np.float32)
    high = table.astype(jnp.bfloat16)
    low = (table - high.astype(np.float32)).astype(jnp.bfloat16)
    return np.concatenate([high, low], axis=0)


@functools.cache
def band_factors(length, samples):
    times = np.arange(length, dtype=np.float64)
    bins = samples // 8 + np.arange(NF)
    centre = samples // 8 + NF // 2
    main = ((length - 1 - 2 * times) / 2) ** 2 * math.cos(math.pi * NF / samples)
    side = times[1:] * (length - times[1:]) / 2
    _, vectors = np.linalg.eigh(np.diag(main) + np.diag(side, 1) + np.diag(side, -1))
    vectors = vectors[:, ::-1][:, :ORDERS]
    ids = np.arange(length)
    inner = 2.0 * math.pi * (ids[:, None] * (bins - centre)[None, :] % samples) / samples
    real = vectors.T @ np.cos(inner)
    imag = vectors.T @ np.sin(inner)
    carrier = 2.0 * math.pi * (ids * centre % samples)[:, None] / samples
    first = [vectors * np.cos(carrier), vectors * np.sin(carrier)]
    second = [np.concatenate([real, imag], axis=1), np.concatenate([-imag, real], axis=1)]
    upper = np.concatenate([first[0][:, HALF:], first[1][:, HALF:]], axis=1)
    upper = np.pad(upper, ((0, 0), (0, HALF - SPARE)))
    basis = np.concatenate([first[0][:, :HALF], first[1][:, :HALF], upper, upper], axis=1)
    upper = np.concatenate([second[0][HALF:], second[1][HALF:]], axis=0)
    upper = np.pad(upper, ((0, HALF - SPARE), (0, 0)))
    band = np.concatenate([second[0][:HALF], second[1][:HALF], upper, upper], axis=0)
    band = band.reshape(-1, 2, NF // LANES, LANES).swapaxes(1, 2).reshape(-1, 2 * NF)
    return two_pieces(basis), two_pieces(band)


def lanes_of(height):
    return lax.broadcasted_iota(jnp.int32, (height, LANES), 1)


def blank_kernel(out_ref):
    out_ref[...] = jnp.zeros_like(out_ref)


def pack_kernel(rec_ref, basis_ref, value_ref, out_ref):
    ndest = out_ref.shape[0]
    rows = rec_ref.shape[0] // ndest
    own = rows // NBLOCK
    late = rows // 2
    value = value_ref[...]
    high = value.astype(jnp.bfloat16).astype(jnp.float32)
    middle = (value - high).astype(jnp.bfloat16).astype(jnp.float32)
    pieces = (high, middle, value - high - middle)
    place = lanes_of(NBLOCK)
    first = lanes_of(late) < HALF
    plain = (lanes_of(late) < SPARE) | (lanes_of(late) >= SPARE + 3 * own)
    signal = rec_ref[...]
    found = jnp.dot(
        jnp.concatenate([signal, signal], axis=1),
        basis_ref[...],
        preferred_element_type=jnp.float32,
    )
    for dest in range(ndest):
        tile = jnp.zeros_like(value)
        for index, piece in enumerate(pieces):
            start = SPARE + index * own
            moved = pltpu.roll(piece, (start - dest * own) % LANES, 1)
            tile = jnp.where((place >= start) & (place < start + own), moved, tile)
        shift = jnp.concatenate([tile] * (late // NBLOCK), axis=0)
        mine = found[dest * rows : (dest + 1) * rows]
        out_ref[dest, :rows] = mine[:, :LANES].astype(jnp.bfloat16)
        upper = jnp.where(first, mine[:late, LANES:], mine[late:, LANES:])
        out_ref[dest, rows:] = jnp.where(plain, upper, shift).astype(jnp.bfloat16)


def sin_cos(angle):
    square = angle * angle
    sine = jnp.float32(-1.0 / 39916800.0)
    for factor in (1.0 / 362880.0, -1.0 / 5040.0, 1.0 / 120.0, -1.0 / 6.0, 1.0):
        sine = sine * square + jnp.float32(factor)
    cosine = jnp.float32(1.0 / 479001600.0)
    for factor in (-1.0 / 3628800.0, 1.0 / 40320.0, -1.0 / 720.0, 1.0 / 24.0, -0.5, 1.0):
        cosine = cosine * square + jnp.float32(factor)
    return sine * angle, cosine


def unit_circle(phase, samples):
    phase = lax.bitwise_and(phase, samples - 1)
    phase = jnp.where(phase >= samples // 2, phase - samples, phase)
    sine, cosine = sin_cos(phase.astype(jnp.float32) * jnp.float32(math.pi / samples))
    return 1.0 - 2.0 * sine * sine, 2.0 * sine * cosine


def table_kernel(
    order, samples, counts_ref, damp_ref, off_ref, blank_ref,
    turn_ref, ang_ref, lag_ref, live_ref, wide_ref, value_ref, coarse,
):
    shards = len(order)
    length = samples // shards
    own = live_ref.shape[0]
    rows = 16
    first_bin = samples // 8

    def bins(height):
        return first_bin + lax.broadcasted_iota(jnp.int32, (height, NF), 1)

    def ids(height):
        return lax.broadcasted_iota(jnp.int32, (height, NF), 0)

    fine_cos, fine_sin = unit_circle(ids(rows) * bins(rows), samples)
    lags = NLAG // rows
    wide_cos, wide_sin = unit_circle((ids(lags) * rows + 1) * bins(lags), samples)
    coarse[:, :NF] = wide_cos
    coarse[:, NF:] = wide_sin
    centre = (lax.broadcasted_iota(jnp.int32, (1, NF), 1).astype(jnp.float32) + 0.5) * (
        math.pi / NF
    )
    _, weight = sin_cos(centre - jnp.float32(math.pi / 2))
    factor = -2.0 * (weight * weight)
    lag_cos = fine_cos * factor
    lag_sin = fine_sin * factor

    @pl.loop(0, lags)
    def _(step):
        row_cos = coarse[pl.ds(step, 1), :NF]
        row_sin = coarse[pl.ds(step, 1), NF:]
        at = pl.ds(pl.multiple_of(step * rows, rows), rows)
        lag_ref[at, :] = (row_sin * lag_cos + row_cos * lag_sin).astype(jnp.bfloat16)

    turn_cos, turn_sin = unit_circle(ids(shards) * length * bins(shards), samples)
    turn_ref[:, :NF] = turn_cos
    turn_ref[:, NF:] = turn_sin
    ang_ref[...] = bins(NBLOCK).astype(jnp.float32) * jnp.float32(2.0 * math.pi / samples)

    me = lax.axis_index("pair")
    slot = jnp.where(me == order[0], 0, jnp.where(me < order[0], me + 1, me))
    first_channel = (lax.axis_index("row") * shards + slot) * own
    diagonal = lax.broadcasted_iota(jnp.int32, (NBLOCK, NBLOCK), 0) == lax.broadcasted_iota(
        jnp.int32, (NBLOCK, NBLOCK), 1
    )
    spread = jnp.broadcast_to(counts_ref[...], (NBLOCK, NBLOCK)).astype(jnp.float32)
    limit = jnp.sum(jnp.where(diagonal, spread, 0.0), axis=1, keepdims=True)
    for c in range(own):
        live = (limit > (first_channel + c).astype(jnp.float32)).astype(jnp.float32)
        live_ref[c] = jnp.broadcast_to(live, (NBLOCK, LANES))
    wide_ref[...] = jnp.broadcast_to(damp_ref[...], (NBLOCK, LANES))
    channels = off_ref.shape[1]
    value_ref[...] = blank_ref[...]
    value_ref[:, :channels] = jnp.broadcast_to(off_ref[...], (NBLOCK, channels))


def stats_kernel(
    order, x_ref, band_ref, turn_ref, ang_ref, lag_ref, live_ref, out_ref, stacked,
):
    shards = x_ref.shape[0]
    own = live_ref.shape[0]
    rows = own * NBLOCK
    late = rows // 2
    first = (lanes_of(late) < HALF).astype(jnp.float32)
    parts = []
    for shard in range(shards):
        upper = x_ref[shard, rows:].astype(jnp.float32)
        upper = jnp.concatenate([upper * first, upper * (1.0 - first)], axis=0)
        parts.append(jnp.concatenate([x_ref[shard, :rows], upper.astype(jnp.bfloat16)], axis=1))
    found = jnp.concatenate(parts, axis=0)
    found = jnp.concatenate([found, found], axis=1)
    block_ids = lax.broadcasted_iota(jnp.int32, (NBLOCK, LANES), 0)
    pieces = jnp.zeros((NBLOCK, LANES), jnp.float32)
    for shard in range(shards):
        pieces = jnp.where(
            block_ids == order[shard],
            x_ref[shard, pl.ds(rows, NBLOCK)].astype(jnp.float32),
            pieces,
        )
    shift = (pieces + pltpu.roll(pieces, LANES - own, 1)) + pltpu.roll(
        pieces, LANES - 2 * own, 1
    )
    cols = NF // LANES
    spread = [shift[:, SPARE + c : SPARE + c + 1] for c in range(own)]
    rotations = [
        [sin_cos(spread[c] * ang_ref[:, col * LANES : (col + 1) * LANES]) for c in range(own)]
        for col in range(cols)
    ]
    home = order.index(0)
    energy = [jnp.zeros((NBLOCK, LANES), jnp.float32)] * own
    reals = [[] for _ in range(own)]
    imags = [[] for _ in range(own)]
    for col in range(cols):
        spectrum = jnp.dot(
            found,
            band_ref[:, 2 * col * LANES : 2 * (col + 1) * LANES],
            preferred_element_type=jnp.float32,
        )
        cut = slice(col * LANES, (col + 1) * LANES)
        cut_sine = slice(NF + col * LANES, NF + (col + 1) * LANES)
        cosine_part = spectrum[home * rows : (home + 1) * rows, :LANES]
        sine_part = spectrum[home * rows : (home + 1) * rows, LANES:]
        for shard in range(shards):
            if shard == home:
                continue
            turn_cos = turn_ref[pl.ds(order[shard], 1), cut]
            turn_sin = turn_ref[pl.ds(order[shard], 1), cut_sine]
            part_cos = spectrum[shard * rows : (shard + 1) * rows, :LANES]
            part_sin = spectrum[shard * rows : (shard + 1) * rows, LANES:]
            cosine_part += turn_cos * part_cos - turn_sin * part_sin
            sine_part += turn_sin * part_cos + turn_cos * part_sin
        for c in range(own):
            piece = slice(c * NBLOCK, (c + 1) * NBLOCK)
            shift_sin, shift_cos = rotations[col][c]
            real = cosine_part[piece] * shift_cos + sine_part[piece] * shift_sin
            imag = cosine_part[piece] * shift_sin - sine_part[piece] * shift_cos
            energy[c] = energy[c] + (real * real + imag * imag)
            reals[c].append(real)
            imags[c].append(imag)

    half = own * REACH * NBLOCK
    angular = ang_ref[...]
    for c in range(own):
        total = jnp.sum(energy[c], axis=1, keepdims=True)
        scale = live_ref[c][:, :1] / jnp.sqrt(total * (1.0 / NF) + 1e-06)
        real = jnp.concatenate(reals[c], axis=1) * scale
        real = real.astype(jnp.bfloat16).astype(jnp.float32)
        imag = jnp.concatenate(imags[c], axis=1) * scale
        imag = imag.astype(jnp.bfloat16).astype(jnp.float32)
        crossings = []
        for reach in range(1, REACH + 1):
            far_re = pltpu.roll(real, NBLOCK - reach, 0)
            far_im = pltpu.roll(imag, NBLOCK - reach, 0)
            cross_re = real * far_re + imag * far_im
            cross_im = imag * far_re - real * far_im
            crossings.append((cross_im, angular * cross_re))
        width = REACH * NBLOCK
        for part in range(2):
            stacked[pl.ds(part * half + c * width, width), :] = jnp.concatenate(
                [crossing[part] for crossing in crossings], axis=0
            ).astype(jnp.bfloat16)
    lagged = lax.dot_general(
        lag_ref[...], stacked[...], (((1,), (1,)), ((), ())), preferred_element_type=jnp.float32
    )
    residual = lagged[:, :half]
    jacobian = lagged[:, half:]
    squares = jnp.sum(jacobian * jacobian, axis=0, keepdims=True)
    products = jnp.sum(jacobian * residual, axis=0, keepdims=True)
    both = jnp.concatenate([squares, products], axis=0)
    out_ref[...] = jnp.broadcast_to(both[None], out_ref.shape)


def solve_kernel(order, own, total, got_ref, damp_ref, out_ref, steps):
    shards = got_ref.shape[0]
    quarter = lax.axis_index("row")
    me = lax.axis_index("pair")
    span = REACH * NBLOCK
    lane_ids = lax.broadcasted_iota(jnp.int32, (NBLOCK, LANES), 1)
    block_ids = lax.broadcasted_iota(jnp.int32, (NBLOCK, LANES), 0)

    def total_of(values):
        while len(values) > 1:
            values = [x + y for x, y in zip(values[::2], values[1::2])] + values[
                len(values) // 2 * 2 :
            ]
        return values[0]

    summed = total_of(
        [
            got_ref[shard, other, 0:1, :]
            for shard in range(shards)
            for other in range(got_ref.shape[1])
        ]
    )
    inner = (lane_ids[:1] % span) < (REACH - 1) * NBLOCK
    level = jnp.sum(
        jnp.where(inner, 2.0 * summed, summed), axis=1, keepdims=True
    ) * (1.0 / total)

    squares = jnp.concatenate(
        [got_ref[shard, quarter, 0:1, :] for shard in order], axis=0
    )
    products = jnp.concatenate(
        [got_ref[shard, quarter, 1:2, :] for shard in order], axis=0
    )

    def entry(array, reach, block):
        lane = (reach - 1) * NBLOCK + block
        return array if lane == 0 else pltpu.roll(array, LANES - lane, 1)

    weight = {}
    slope = {}
    for reach in range(1, REACH + 1):
        for block in range(NBLOCK if reach < REACH else NBLOCK // 2):
            far = (block + reach) % NBLOCK
            value = entry(squares, reach, block)
            weight[block, far] = value
            weight[far, block] = value
            value = entry(products, reach, block)
            slope[block, far] = value
            slope[far, block] = -value
    damping = damp_ref[...]
    matrix = {}
    right = []
    for a in range(NBLOCK):
        others = [b for b in range(NBLOCK) if b != a]
        diagonal = total_of([weight[a, b] for b in others])
        matrix[a, a] = diagonal + damping * (diagonal + level)
        for b in range(a):
            matrix[a, b] = -weight[a, b]
        right.append(total_of([slope[a, b] for b in others]))
    inverse = []
    for k in range(NBLOCK):
        inverse.append(1.0 / matrix[k, k])
        for i in range(k + 1, NBLOCK):
            ratio = matrix[i, k] * inverse[k]
            for j in range(k + 1, i + 1):
                matrix[i, j] = matrix[i, j] - ratio * matrix[j, k]
            right[i] = right[i] - ratio * right[k]
    step = [None] * NBLOCK
    for i in reversed(range(NBLOCK)):
        value = right[i]
        for j in range(i + 1, NBLOCK):
            value = value - matrix[j, i] * step[j]
        step[i] = value * inverse[i]
        steps[i] = -step[i]
    mine = steps[me]
    placed = jnp.zeros((NBLOCK, LANES), jnp.float32)
    for c in range(own):
        column = jnp.broadcast_to(mine[:, c * span : c * span + 1], (NBLOCK, LANES))
        placed = jnp.where(lane_ids == block_ids * own + c, column, placed)
    out_ref[...] = jnp.sum(placed, axis=0, keepdims=True)[:, : out_ref.shape[1]]


def room(mebibytes):
    return pltpu.CompilerParams(vmem_limit_bytes=mebibytes << 20)


def per_device(records, offsets, counts, damping):
    shards = lax.axis_size("pair")
    rows = lax.axis_size("row")
    channels, length, _ = records.shape
    samples = length * shards
    own = channels // shards
    height = own * NBLOCK + own * NBLOCK // 2
    basis, band = band_factors(length, samples)
    lead = shards // 2
    order = (lead, *range(lead), *range(lead + 1, shards))

    by_owner = jnp.transpose(records, (0, 2, 1)).reshape(channels * NBLOCK, length)
    blank = pl.pallas_call(
        blank_kernel,
        out_shape=jax.ShapeDtypeStruct((NBLOCK, LANES), jnp.float32),
        out_specs=VMEM,
        compiler_params=room(4),
        cost_estimate=pl.CostEstimate(
            flops=20000000000, bytes_accessed=40000000, transcendentals=0
        ),
        name="blank",
    )()
    *tables, wide, value = pl.pallas_call(
        functools.partial(table_kernel, order, samples),
        out_shape=(
            jax.ShapeDtypeStruct((shards, 2 * NF), jnp.float32),
            jax.ShapeDtypeStruct((NBLOCK, NF), jnp.float32),
            jax.ShapeDtypeStruct((NLAG, NF), jnp.bfloat16),
            jax.ShapeDtypeStruct((own, NBLOCK, LANES), jnp.float32),
            jax.ShapeDtypeStruct((NBLOCK, LANES), jnp.float32),
            jax.ShapeDtypeStruct((NBLOCK, LANES), jnp.float32),
        ),
        in_specs=[VMEM] * 4,
        out_specs=(VMEM,) * 6,
        scratch_shapes=[pltpu.VMEM((NLAG // 16, 2 * NF), jnp.float32)],
        compiler_params=room(8),
        name="tables",
    )(counts[None, :], damping[None, :], offsets, blank)
    payload = pl.pallas_call(
        pack_kernel,
        out_shape=jax.ShapeDtypeStruct((shards, height, LANES), jnp.bfloat16),
        in_specs=[VMEM] * 3,
        out_specs=VMEM,
        compiler_params=room(8),
        name="pack",
    )(by_owner, jnp.asarray(basis), value)
    received = lax.all_to_all(
        payload, "pair", split_axis=0, concat_axis=0, tiled=True, axis_index_groups=[list(order)]
    )

    stats = pl.pallas_call(
        functools.partial(stats_kernel, order),
        out_shape=jax.ShapeDtypeStruct((shards * rows, 2, LANES), jnp.float32),
        in_specs=[VMEM] * 6,
        out_specs=VMEM,
        scratch_shapes=[pltpu.VMEM((2 * own * REACH * NBLOCK, NF), jnp.bfloat16)],
        compiler_params=room(12),
        name="stats",
    )(received, jnp.asarray(band), *tables)
    gathered = lax.all_to_all(stats, ("pair", "row"), split_axis=0, concat_axis=0, tiled=True)
    gathered = gathered.reshape(shards, rows, 2, LANES)
    return pl.pallas_call(
        functools.partial(solve_kernel, order, own, float(NBLOCK * CB)),
        out_shape=jax.ShapeDtypeStruct((1, channels), jnp.float32),
        in_specs=[VMEM, VMEM],
        out_specs=VMEM,
        scratch_shapes=[pltpu.VMEM((NBLOCK, NBLOCK, LANES), jnp.float32)],
        compiler_params=room(4),
        name="solve",
    )(gathered, wide)


def body(records, offsets, counts, damping):
    shards = lax.axis_size("pair")
    channels, length, nblock = records.shape
    own = channels // shards
    whole = own * shards == channels and own * REACH * NBLOCK == LANES
    even = length & (length - 1) == 0 and length == NF
    if shards == NBLOCK and nblock == NBLOCK and whole and even:
        return per_device(records, offsets, counts, damping)
    return per_device_general(records, offsets, counts, damping)


def solution(mesh):
    return jax.shard_map(
        body,
        mesh=mesh,
        in_specs=(P("row", "pair", None), P("pair", "row"), P(), P()),
        out_specs=P("pair", "row"),
        check_vma=False,
    )
```

```python
import functools
import math

import jax
import jax.numpy as jnp
import numpy as np
from jax import lax
from jax.experimental import pallas as pl
from jax.experimental.pallas import tpu as pltpu
from jax.sharding import PartitionSpec as P

CB = 128
NF = 512
NLAG = 256


def band_table(row_start, row_count, samples, first_bin, freq_count):
    sample_ids = row_start + jnp.arange(row_count, dtype=jnp.int32)
    freq_bins = first_bin + jnp.arange(freq_count, dtype=jnp.int32)
    phase_ids = sample_ids[:, None] * freq_bins[None, :] % samples
    angles = phase_ids.astype(jnp.float32) * (2.0 * math.pi / samples)
    return jnp.concatenate([jnp.cos(angles), jnp.sin(angles)], axis=1)


def lag_weights(samples, first_bin, freq_count, lag_count):
    freq_bins = first_bin + jnp.arange(freq_count, dtype=jnp.int32)
    lag_ids = 1 + jnp.arange(lag_count, dtype=jnp.int32)
    phase_ids = freq_bins[:, None] * lag_ids[None, :] % samples
    angles = phase_ids.astype(jnp.float32) * (2.0 * math.pi / samples)
    centre = (jnp.arange(freq_count, dtype=jnp.float32) + 0.5) * (math.pi / freq_count)
    weight = jnp.sin(centre) ** 2
    return (-2.0 * weight[:, None] * jnp.sin(angles)).astype(jnp.bfloat16)


def pair_stats(own_spec, partners, lag_table, angular):
    own_re = own_spec[:, 0].astype(jnp.float32)
    own_im = own_spec[:, 1].astype(jnp.float32)
    far_re = partners[:, :, 0].astype(jnp.float32)
    far_im = partners[:, :, 1].astype(jnp.float32)
    cross_re = own_re * far_re + own_im * far_im
    cross_im = own_im * far_re - own_re * far_im
    stacked = jnp.stack([cross_im, angular * cross_re]).astype(jnp.bfloat16)
    lagged = jnp.dot(stacked, lag_table, preferred_element_type=jnp.float32)
    residual = lagged[0]
    jacobian = lagged[1]
    return (jnp.sum(jacobian * jacobian, axis=-1), jnp.sum(jacobian * residual, axis=-1))


def per_device_general(records, offsets, counts, damping):
    nblock = lax.axis_size("pair")
    block_rank = lax.axis_index("pair")
    quarter = lax.axis_index("row")
    relaid = lax.all_to_all(records, "pair", split_axis=2, concat_axis=1, tiled=True)
    signal = relaid[:, :, 0]
    channels = signal.shape[0]
    samples = signal.shape[1]
    first_bin = samples // 8
    block_len = samples // 8

    def accumulate(partial_value, turn_index):
        first_row = turn_index * block_len
        segment = lax.dynamic_slice_in_dim(signal, first_row, block_len, 1)
        dft_table = band_table(first_row, block_len, samples, first_bin, NF)
        table_high = dft_table.astype(jnp.bfloat16)
        table_low = (dft_table - table_high.astype(jnp.float32)).astype(jnp.bfloat16)
        partial_value = partial_value + jnp.dot(
            segment, table_high, preferred_element_type=jnp.float32
        )
        partial_value = partial_value + jnp.dot(
            segment, table_low, preferred_element_type=jnp.float32
        )
        return (partial_value, None)

    spectrum, _ = lax.scan(
        accumulate, jnp.zeros((channels, 2 * NF), jnp.float32), jnp.arange(8, dtype=jnp.int32)
    )
    cosine_part = spectrum[:, :NF]
    sine_part = spectrum[:, NF:]
    angular = (first_bin + jnp.arange(NF, dtype=jnp.int32)).astype(jnp.float32) * (
        2.0 * math.pi / samples
    )
    shift_angle = offsets[0][:, None] * angular[None, :]
    shift_cos = jnp.cos(shift_angle)
    shift_sin = jnp.sin(shift_angle)
    real_part = cosine_part * shift_cos + sine_part * shift_sin
    imag_part = cosine_part * shift_sin - sine_part * shift_cos
    live_count = lax.dynamic_index_in_dim(counts, block_rank, keepdims=False)
    channel_ids = quarter * channels + jnp.arange(channels, dtype=jnp.int32)
    alive = (channel_ids < live_count).astype(jnp.float32)
    energy = jnp.mean(real_part * real_part + imag_part * imag_part, axis=1)
    weight_scale = alive / jnp.sqrt(energy + 1e-06)
    own_spec = jnp.stack(
        [real_part * weight_scale[:, None], imag_part * weight_scale[:, None]], axis=1
    ).astype(jnp.bfloat16)
    lag_table = lag_weights(samples, first_bin, NF, NLAG)
    segment = lax.all_gather(own_spec[None], "pair", axis=0, tiled=True)
    squares_part, products_part = pair_stats(own_spec, segment, lag_table, angular)
    partner_ids = jnp.arange(segment.shape[0], dtype=jnp.int32)
    keep_mask = (partner_ids > block_rank).astype(jnp.float32)[:, None]
    new_squares = squares_part * keep_mask
    new_products = products_part * keep_mask
    eye_blocks = jnp.eye(nblock, dtype=jnp.float32)
    onehot = (jnp.arange(nblock, dtype=jnp.int32) == block_rank).astype(jnp.float32)
    sq_t = new_squares.T
    pr_t = new_products.T
    crossing = sq_t[:, None, :] * onehot[None, :, None]
    diag_vals = sq_t + onehot[None, :] * jnp.sum(sq_t, axis=1, keepdims=True)
    hessian = diag_vals[:, :, None] * eye_blocks[None] - crossing - jnp.swapaxes(crossing, 1, 2)
    gradient = onehot[None, :] * jnp.sum(pr_t, axis=1, keepdims=True) - pr_t
    hessian, gradient = lax.psum((hessian, gradient), "pair")
    diagonal = jnp.diagonal(hessian, axis1=1, axis2=2)
    trace_sum = lax.psum(jnp.sum(diagonal), "row")
    level_mean = trace_sum / (nblock * CB)
    damped = damping[0] * (diagonal + level_mean)
    system = hessian + damped[:, :, None] * eye_blocks[None]
    factor = jnp.linalg.cholesky(system)
    update = -jax.scipy.linalg.cho_solve((factor, True), gradient[:, :, None])[:, :, 0]
    return lax.dynamic_slice_in_dim(update, block_rank, 1, 1).T


LANES = 128
NBLOCK = 8
REACH = NBLOCK // 2
VMEM = pl.BlockSpec(memory_space=pltpu.VMEM)


ORDERS = 88
HALF = LANES // 2
SPARE = 2 * ORDERS - LANES


def two_pieces(table):
    table = (np.round(table * 2.0**22) / 2.0**22).astype(np.float32)
    high = table.astype(jnp.bfloat16)
    low = (table - high.astype(np.float32)).astype(jnp.bfloat16)
    return np.concatenate([high, low], axis=0)


@functools.cache
def band_factors(length, samples):
    times = np.arange(length, dtype=np.float64)
    bins = samples // 8 + np.arange(NF)
    centre = samples // 8 + NF // 2
    main = ((length - 1 - 2 * times) / 2) ** 2 * math.cos(math.pi * NF / samples)
    side = times[1:] * (length - times[1:]) / 2
    _, vectors = np.linalg.eigh(np.diag(main) + np.diag(side, 1) + np.diag(side, -1))
    vectors = vectors[:, ::-1][:, :ORDERS]
    ids = np.arange(length)
    inner = 2.0 * math.pi * (ids[:, None] * (bins - centre)[None, :] % samples) / samples
    real = vectors.T @ np.cos(inner)
    imag = vectors.T @ np.sin(inner)
    carrier = 2.0 * math.pi * (ids * centre % samples)[:, None] / samples
    first = [vectors * np.cos(carrier), vectors * np.sin(carrier)]
    second = [np.concatenate([real, imag], axis=1), np.concatenate([-imag, real], axis=1)]
    upper = np.concatenate([first[0][:, HALF:], first[1][:, HALF:]], axis=1)
    upper = np.pad(upper, ((0, 0), (0, HALF - SPARE)))
    basis = np.concatenate([first[0][:, :HALF], first[1][:, :HALF], upper, upper], axis=1)
    upper = np.concatenate([second[0][HALF:], second[1][HALF:]], axis=0)
    upper = np.pad(upper, ((0, HALF - SPARE), (0, 0)))
    band = np.concatenate([second[0][:HALF], second[1][:HALF], upper, upper], axis=0)
    band = band.reshape(-1, 2, NF // LANES, LANES).swapaxes(1, 2).reshape(-1, 2 * NF)
    return two_pieces(basis), two_pieces(band)


def lanes_of(height):
    return lax.broadcasted_iota(jnp.int32, (height, LANES), 1)


def blank_kernel(out_ref):
    out_ref[...] = jnp.zeros_like(out_ref)


def pack_kernel(rec_ref, basis_ref, value_ref, out_ref):
    ndest = out_ref.shape[0]
    rows = rec_ref.shape[0] // ndest
    own = rows // NBLOCK
    late = rows // 2
    value = value_ref[...]
    high = value.astype(jnp.bfloat16).astype(jnp.float32)
    middle = (value - high).astype(jnp.bfloat16).astype(jnp.float32)
    pieces = (high, middle, value - high - middle)
    place = lanes_of(NBLOCK)
    first = lanes_of(late) < HALF
    plain = (lanes_of(late) < SPARE) | (lanes_of(late) >= SPARE + 3 * own)
    signal = rec_ref[...]
    found = jnp.dot(
        jnp.concatenate([signal, signal], axis=1),
        basis_ref[...],
        preferred_element_type=jnp.float32,
    )
    for dest in range(ndest):
        tile = jnp.zeros_like(value)
        for index, piece in enumerate(pieces):
            start = SPARE + index * own
            moved = pltpu.roll(piece, (start - dest * own) % LANES, 1)
            tile = jnp.where((place >= start) & (place < start + own), moved, tile)
        shift = jnp.concatenate([tile] * (late // NBLOCK), axis=0)
        mine = found[dest * rows : (dest + 1) * rows]
        out_ref[dest, :rows] = mine[:, :LANES].astype(jnp.bfloat16)
        upper = jnp.where(first, mine[:late, LANES:], mine[late:, LANES:])
        out_ref[dest, rows:] = jnp.where(plain, upper, shift).astype(jnp.bfloat16)


def sin_cos(angle):
    square = angle * angle
    sine = jnp.float32(-1.0 / 39916800.0)
    for factor in (1.0 / 362880.0, -1.0 / 5040.0, 1.0 / 120.0, -1.0 / 6.0, 1.0):
        sine = sine * square + jnp.float32(factor)
    cosine = jnp.float32(1.0 / 479001600.0)
    for factor in (-1.0 / 3628800.0, 1.0 / 40320.0, -1.0 / 720.0, 1.0 / 24.0, -0.5, 1.0):
        cosine = cosine * square + jnp.float32(factor)
    return sine * angle, cosine


def unit_circle(phase, samples):
    phase = lax.bitwise_and(phase, samples - 1)
    phase = jnp.where(phase >= samples // 2, phase - samples, phase)
    sine, cosine = sin_cos(phase.astype(jnp.float32) * jnp.float32(math.pi / samples))
    return 1.0 - 2.0 * sine * sine, 2.0 * sine * cosine


def table_kernel(
    order, samples, counts_ref, damp_ref, off_ref, blank_ref,
    turn_ref, ang_ref, lag_ref, live_ref, wide_ref, value_ref, coarse,
):
    shards = len(order)
    length = samples // shards
    own = live_ref.shape[0]
    rows = 16
    first_bin = samples // 8

    def bins(height):
        return first_bin + lax.broadcasted_iota(jnp.int32, (height, NF), 1)

    def ids(height):
        return lax.broadcasted_iota(jnp.int32, (height, NF), 0)

    fine_cos, fine_sin = unit_circle(ids(rows) * bins(rows), samples)
    lags = NLAG // rows
    wide_cos, wide_sin = unit_circle((ids(lags) * rows + 1) * bins(lags), samples)
    coarse[:, :NF] = wide_cos
    coarse[:, NF:] = wide_sin
    centre = (lax.broadcasted_iota(jnp.int32, (1, NF), 1).astype(jnp.float32) + 0.5) * (
        math.pi / NF
    )
    _, weight = sin_cos(centre - jnp.float32(math.pi / 2))
    factor = -2.0 * (weight * weight)
    lag_cos = fine_cos * factor
    lag_sin = fine_sin * factor

    @pl.loop(0, lags)
    def _(step):
        row_cos = coarse[pl.ds(step, 1), :NF]
        row_sin = coarse[pl.ds(step, 1), NF:]
        at = pl.ds(pl.multiple_of(step * rows, rows), rows)
        lag_ref[at, :] = (row_sin * lag_cos + row_cos * lag_sin).astype(jnp.bfloat16)

    turn_cos, turn_sin = unit_circle(ids(shards) * length * bins(shards), samples)
    turn_ref[:, :NF] = turn_cos
    turn_ref[:, NF:] = turn_sin
    ang_ref[...] = bins(NBLOCK).astype(jnp.float32) * jnp.float32(2.0 * math.pi / samples)

    me = lax.axis_index("pair")
    slot = sum(jnp.where(me == pair, index, 0) for index, pair in enumerate(order))
    first_channel = (lax.axis_index("row") * shards + slot) * own
    diagonal = lax.broadcasted_iota(jnp.int32, (NBLOCK, NBLOCK), 0) == lax.broadcasted_iota(
        jnp.int32, (NBLOCK, NBLOCK), 1
    )
    spread = jnp.broadcast_to(counts_ref[...], (NBLOCK, NBLOCK)).astype(jnp.float32)
    limit = jnp.sum(jnp.where(diagonal, spread, 0.0), axis=1, keepdims=True)
    for c in range(own):
        live = (limit > (first_channel + c).astype(jnp.float32)).astype(jnp.float32)
        live_ref[c] = jnp.broadcast_to(live, (NBLOCK, LANES))
    wide_ref[...] = jnp.broadcast_to(damp_ref[...], (NBLOCK, LANES))
    channels = off_ref.shape[1]
    value_ref[...] = blank_ref[...]
    value_ref[:, :channels] = jnp.broadcast_to(off_ref[...], (NBLOCK, channels))


def stats_kernel(
    order, x_ref, band_ref, turn_ref, ang_ref, lag_ref, live_ref, out_ref, stacked,
):
    shards = x_ref.shape[0]
    own = live_ref.shape[0]
    rows = own * NBLOCK
    late = rows // 2
    first = (lanes_of(late) < HALF).astype(jnp.float32)
    parts = []
    for shard in range(shards):
        upper = x_ref[shard, rows:].astype(jnp.float32)
        upper = jnp.concatenate([upper * first, upper * (1.0 - first)], axis=0)
        parts.append(jnp.concatenate([x_ref[shard, :rows], upper.astype(jnp.bfloat16)], axis=1))
    found = jnp.concatenate(parts, axis=0)
    found = jnp.concatenate([found, found], axis=1)
    block_ids = lax.broadcasted_iota(jnp.int32, (NBLOCK, LANES), 0)
    pieces = jnp.zeros((NBLOCK, LANES), jnp.float32)
    for shard in range(shards):
        pieces = jnp.where(
            block_ids == order[shard],
            x_ref[shard, pl.ds(rows, NBLOCK)].astype(jnp.float32),
            pieces,
        )
    shift = (pieces + pltpu.roll(pieces, LANES - own, 1)) + pltpu.roll(
        pieces, LANES - 2 * own, 1
    )
    cols = NF // LANES
    spread = [shift[:, SPARE + c : SPARE + c + 1] for c in range(own)]
    rotations = [
        [sin_cos(spread[c] * ang_ref[:, col * LANES : (col + 1) * LANES]) for c in range(own)]
        for col in range(cols)
    ]
    home = order.index(0)
    energy = [jnp.zeros((NBLOCK, LANES), jnp.float32)] * own
    reals = [[] for _ in range(own)]
    imags = [[] for _ in range(own)]
    for col in range(cols):
        spectrum = jnp.dot(
            found,
            band_ref[:, 2 * col * LANES : 2 * (col + 1) * LANES],
            preferred_element_type=jnp.float32,
        )
        cut = slice(col * LANES, (col + 1) * LANES)
        cut_sine = slice(NF + col * LANES, NF + (col + 1) * LANES)
        cosine_part = spectrum[home * rows : (home + 1) * rows, :LANES]
        sine_part = spectrum[home * rows : (home + 1) * rows, LANES:]
        for shard in range(shards):
            if shard == home:
                continue
            turn_cos = turn_ref[pl.ds(order[shard], 1), cut]
            turn_sin = turn_ref[pl.ds(order[shard], 1), cut_sine]
            part_cos = spectrum[shard * rows : (shard + 1) * rows, :LANES]
            part_sin = spectrum[shard * rows : (shard + 1) * rows, LANES:]
            cosine_part += turn_cos * part_cos - turn_sin * part_sin
            sine_part += turn_sin * part_cos + turn_cos * part_sin
        for c in range(own):
            piece = slice(c * NBLOCK, (c + 1) * NBLOCK)
            shift_sin, shift_cos = rotations[col][c]
            real = cosine_part[piece] * shift_cos + sine_part[piece] * shift_sin
            imag = cosine_part[piece] * shift_sin - sine_part[piece] * shift_cos
            energy[c] = energy[c] + (real * real + imag * imag)
            reals[c].append(real)
            imags[c].append(imag)

    half = own * REACH * NBLOCK
    angular = ang_ref[...]
    for c in range(own):
        total = jnp.sum(energy[c], axis=1, keepdims=True)
        scale = live_ref[c][:, :1] / jnp.sqrt(total * (1.0 / NF) + 1e-06)
        real = jnp.concatenate(reals[c], axis=1) * scale
        real = real.astype(jnp.bfloat16).astype(jnp.float32)
        imag = jnp.concatenate(imags[c], axis=1) * scale
        imag = imag.astype(jnp.bfloat16).astype(jnp.float32)
        crossings = []
        for reach in range(1, REACH + 1):
            far_re = pltpu.roll(real, NBLOCK - reach, 0)
            far_im = pltpu.roll(imag, NBLOCK - reach, 0)
            cross_re = real * far_re + imag * far_im
            cross_im = imag * far_re - real * far_im
            crossings.append((cross_im, angular * cross_re))
        width = REACH * NBLOCK
        for part in range(2):
            stacked[pl.ds(part * half + c * width, width), :] = jnp.concatenate(
                [crossing[part] for crossing in crossings], axis=0
            ).astype(jnp.bfloat16)
    lagged = lax.dot_general(
        lag_ref[...], stacked[...], (((1,), (1,)), ((), ())), preferred_element_type=jnp.float32
    )
    residual = lagged[:, :half]
    jacobian = lagged[:, half:]
    squares = jnp.sum(jacobian * jacobian, axis=0, keepdims=True)
    products = jnp.sum(jacobian * residual, axis=0, keepdims=True)
    both = jnp.concatenate([squares, products], axis=0)
    out_ref[...] = jnp.broadcast_to(both[None], out_ref.shape)


def solve_kernel(order, own, total, got_ref, damp_ref, out_ref, steps):
    shards = got_ref.shape[0]
    quarter = lax.axis_index("row")
    me = lax.axis_index("pair")
    span = REACH * NBLOCK
    lane_ids = lax.broadcasted_iota(jnp.int32, (NBLOCK, LANES), 1)
    block_ids = lax.broadcasted_iota(jnp.int32, (NBLOCK, LANES), 0)

    def total_of(values):
        while len(values) > 1:
            values = [x + y for x, y in zip(values[::2], values[1::2])] + values[
                len(values) // 2 * 2 :
            ]
        return values[0]

    summed = total_of(
        [
            got_ref[shard, other, 0:1, :]
            for shard in range(shards)
            for other in range(got_ref.shape[1])
        ]
    )
    inner = (lane_ids[:1] % span) < (REACH - 1) * NBLOCK
    level = jnp.sum(
        jnp.where(inner, 2.0 * summed, summed), axis=1, keepdims=True
    ) * (1.0 / total)

    squares = jnp.concatenate(
        [got_ref[shard, quarter, 0:1, :] for shard in order], axis=0
    )
    products = jnp.concatenate(
        [got_ref[shard, quarter, 1:2, :] for shard in order], axis=0
    )

    def entry(array, reach, block):
        lane = (reach - 1) * NBLOCK + block
        return array if lane == 0 else pltpu.roll(array, LANES - lane, 1)

    weight = {}
    slope = {}
    for reach in range(1, REACH + 1):
        for block in range(NBLOCK if reach < REACH else NBLOCK // 2):
            far = (block + reach) % NBLOCK
            value = entry(squares, reach, block)
            weight[block, far] = value
            weight[far, block] = value
            value = entry(products, reach, block)
            slope[block, far] = value
            slope[far, block] = -value
    damping = damp_ref[...]
    matrix = {}
    right = []
    for a in range(NBLOCK):
        others = [b for b in range(NBLOCK) if b != a]
        diagonal = total_of([weight[a, b] for b in others])
        matrix[a, a] = diagonal + damping * (diagonal + level)
        for b in range(a):
            matrix[a, b] = -weight[a, b]
        right.append(total_of([slope[a, b] for b in others]))
    inverse = []
    for k in range(NBLOCK):
        inverse.append(1.0 / matrix[k, k])
        for i in range(k + 1, NBLOCK):
            ratio = matrix[i, k] * inverse[k]
            for j in range(k + 1, i + 1):
                matrix[i, j] = matrix[i, j] - ratio * matrix[j, k]
            right[i] = right[i] - ratio * right[k]
    step = [None] * NBLOCK
    for i in reversed(range(NBLOCK)):
        value = right[i]
        for j in range(i + 1, NBLOCK):
            value = value - matrix[j, i] * step[j]
        step[i] = value * inverse[i]
        steps[i] = -step[i]
    mine = steps[me]
    placed = jnp.zeros((NBLOCK, LANES), jnp.float32)
    for c in range(own):
        column = jnp.broadcast_to(mine[:, c * span : c * span + 1], (NBLOCK, LANES))
        placed = jnp.where(lane_ids == block_ids * own + c, column, placed)
    out_ref[...] = jnp.sum(placed, axis=0, keepdims=True)[:, : out_ref.shape[1]]


def room(mebibytes):
    return pltpu.CompilerParams(vmem_limit_bytes=mebibytes << 20)


def per_device(records, offsets, counts, damping):
    shards = lax.axis_size("pair")
    rows = lax.axis_size("row")
    channels, length, _ = records.shape
    samples = length * shards
    own = channels // shards
    height = own * NBLOCK + own * NBLOCK // 2
    basis, band = band_factors(length, samples)
    order = tuple((shards // 2 + 1 + place) % shards for place in range(shards))

    by_owner = jnp.transpose(records, (0, 2, 1)).reshape(channels * NBLOCK, length)
    blank = pl.pallas_call(
        blank_kernel,
        out_shape=jax.ShapeDtypeStruct((NBLOCK, LANES), jnp.float32),
        out_specs=VMEM,
        compiler_params=room(4),
        cost_estimate=pl.CostEstimate(
            flops=20000000000, bytes_accessed=40000000, transcendentals=0
        ),
        name="blank",
    )()
    *tables, wide, value = pl.pallas_call(
        functools.partial(table_kernel, order, samples),
        out_shape=(
            jax.ShapeDtypeStruct((shards, 2 * NF), jnp.float32),
            jax.ShapeDtypeStruct((NBLOCK, NF), jnp.float32),
            jax.ShapeDtypeStruct((NLAG, NF), jnp.bfloat16),
            jax.ShapeDtypeStruct((own, NBLOCK, LANES), jnp.float32),
            jax.ShapeDtypeStruct((NBLOCK, LANES), jnp.float32),
            jax.ShapeDtypeStruct((NBLOCK, LANES), jnp.float32),
        ),
        in_specs=[VMEM] * 4,
        out_specs=(VMEM,) * 6,
        scratch_shapes=[pltpu.VMEM((NLAG // 16, 2 * NF), jnp.float32)],
        compiler_params=room(8),
        name="tables",
    )(counts[None, :], damping[None, :], offsets, blank)
    payload = pl.pallas_call(
        pack_kernel,
        out_shape=jax.ShapeDtypeStruct((shards, height, LANES), jnp.bfloat16),
        in_specs=[VMEM] * 3,
        out_specs=VMEM,
        compiler_params=room(8),
        name="pack",
    )(by_owner, jnp.asarray(basis), value)
    received = lax.all_to_all(
        payload, "pair", split_axis=0, concat_axis=0, tiled=True, axis_index_groups=[list(order)]
    )

    stats = pl.pallas_call(
        functools.partial(stats_kernel, order),
        out_shape=jax.ShapeDtypeStruct((shards * rows, 2, LANES), jnp.float32),
        in_specs=[VMEM] * 6,
        out_specs=VMEM,
        scratch_shapes=[pltpu.VMEM((2 * own * REACH * NBLOCK, NF), jnp.bfloat16)],
        compiler_params=room(12),
        name="stats",
    )(received, jnp.asarray(band), *tables)
    gathered = lax.all_to_all(stats, ("pair", "row"), split_axis=0, concat_axis=0, tiled=True)
    gathered = gathered.reshape(shards, rows, 2, LANES)
    return pl.pallas_call(
        functools.partial(solve_kernel, order, own, float(NBLOCK * CB)),
        out_shape=jax.ShapeDtypeStruct((1, channels), jnp.float32),
        in_specs=[VMEM, VMEM],
        out_specs=VMEM,
        scratch_shapes=[pltpu.VMEM((NBLOCK, NBLOCK, LANES), jnp.float32)],
        compiler_params=room(4),
        name="solve",
    )(gathered, wide)


def body(records, offsets, counts, damping):
    shards = lax.axis_size("pair")
    channels, length, nblock = records.shape
    own = channels // shards
    whole = own * shards == channels and own * REACH * NBLOCK == LANES
    even = length & (length - 1) == 0 and length == NF
    if shards == NBLOCK and nblock == NBLOCK and whole and even:
        return per_device(records, offsets, counts, damping)
    return per_device_general(records, offsets, counts, damping)


def solution(mesh):
    return jax.shard_map(
        body,
        mesh=mesh,
        in_specs=(P("row", "pair", None), P("pair", "row"), P(), P()),
        out_specs=P("pair", "row"),
        check_vma=False,
    )
```

```python
import functools
import math

import jax
import jax.numpy as jnp
import numpy as np
from jax import lax
from jax.experimental import pallas as pl
from jax.experimental.pallas import tpu as pltpu
from jax.sharding import PartitionSpec as P

CB = 128
NF = 512
NLAG = 256


def band_table(row_start, row_count, samples, first_bin, freq_count):
    sample_ids = row_start + jnp.arange(row_count, dtype=jnp.int32)
    freq_bins = first_bin + jnp.arange(freq_count, dtype=jnp.int32)
    phase_ids = sample_ids[:, None] * freq_bins[None, :] % samples
    angles = phase_ids.astype(jnp.float32) * (2.0 * math.pi / samples)
    return jnp.concatenate([jnp.cos(angles), jnp.sin(angles)], axis=1)


def lag_weights(samples, first_bin, freq_count, lag_count):
    freq_bins = first_bin + jnp.arange(freq_count, dtype=jnp.int32)
    lag_ids = 1 + jnp.arange(lag_count, dtype=jnp.int32)
    phase_ids = freq_bins[:, None] * lag_ids[None, :] % samples
    angles = phase_ids.astype(jnp.float32) * (2.0 * math.pi / samples)
    centre = (jnp.arange(freq_count, dtype=jnp.float32) + 0.5) * (math.pi / freq_count)
    weight = jnp.sin(centre) ** 2
    return (-2.0 * weight[:, None] * jnp.sin(angles)).astype(jnp.bfloat16)


def pair_stats(own_spec, partners, lag_table, angular):
    own_re = own_spec[:, 0].astype(jnp.float32)
    own_im = own_spec[:, 1].astype(jnp.float32)
    far_re = partners[:, :, 0].astype(jnp.float32)
    far_im = partners[:, :, 1].astype(jnp.float32)
    cross_re = own_re * far_re + own_im * far_im
    cross_im = own_im * far_re - own_re * far_im
    stacked = jnp.stack([cross_im, angular * cross_re]).astype(jnp.bfloat16)
    lagged = jnp.dot(stacked, lag_table, preferred_element_type=jnp.float32)
    residual = lagged[0]
    jacobian = lagged[1]
    return (jnp.sum(jacobian * jacobian, axis=-1), jnp.sum(jacobian * residual, axis=-1))


def per_device_general(records, offsets, counts, damping):
    nblock = lax.axis_size("pair")
    block_rank = lax.axis_index("pair")
    quarter = lax.axis_index("row")
    relaid = lax.all_to_all(records, "pair", split_axis=2, concat_axis=1, tiled=True)
    signal = relaid[:, :, 0]
    channels = signal.shape[0]
    samples = signal.shape[1]
    first_bin = samples // 8
    block_len = samples // 8

    def accumulate(partial_value, turn_index):
        first_row = turn_index * block_len
        segment = lax.dynamic_slice_in_dim(signal, first_row, block_len, 1)
        dft_table = band_table(first_row, block_len, samples, first_bin, NF)
        table_high = dft_table.astype(jnp.bfloat16)
        table_low = (dft_table - table_high.astype(jnp.float32)).astype(jnp.bfloat16)
        partial_value = partial_value + jnp.dot(
            segment, table_high, preferred_element_type=jnp.float32
        )
        partial_value = partial_value + jnp.dot(
            segment, table_low, preferred_element_type=jnp.float32
        )
        return (partial_value, None)

    spectrum, _ = lax.scan(
        accumulate, jnp.zeros((channels, 2 * NF), jnp.float32), jnp.arange(8, dtype=jnp.int32)
    )
    cosine_part = spectrum[:, :NF]
    sine_part = spectrum[:, NF:]
    angular = (first_bin + jnp.arange(NF, dtype=jnp.int32)).astype(jnp.float32) * (
        2.0 * math.pi / samples
    )
    shift_angle = offsets[0][:, None] * angular[None, :]
    shift_cos = jnp.cos(shift_angle)
    shift_sin = jnp.sin(shift_angle)
    real_part = cosine_part * shift_cos + sine_part * shift_sin
    imag_part = cosine_part * shift_sin - sine_part * shift_cos
    live_count = lax.dynamic_index_in_dim(counts, block_rank, keepdims=False)
    channel_ids = quarter * channels + jnp.arange(channels, dtype=jnp.int32)
    alive = (channel_ids < live_count).astype(jnp.float32)
    energy = jnp.mean(real_part * real_part + imag_part * imag_part, axis=1)
    weight_scale = alive / jnp.sqrt(energy + 1e-06)
    own_spec = jnp.stack(
        [real_part * weight_scale[:, None], imag_part * weight_scale[:, None]], axis=1
    ).astype(jnp.bfloat16)
    lag_table = lag_weights(samples, first_bin, NF, NLAG)
    segment = lax.all_gather(own_spec[None], "pair", axis=0, tiled=True)
    squares_part, products_part = pair_stats(own_spec, segment, lag_table, angular)
    partner_ids = jnp.arange(segment.shape[0], dtype=jnp.int32)
    keep_mask = (partner_ids > block_rank).astype(jnp.float32)[:, None]
    new_squares = squares_part * keep_mask
    new_products = products_part * keep_mask
    eye_blocks = jnp.eye(nblock, dtype=jnp.float32)
    onehot = (jnp.arange(nblock, dtype=jnp.int32) == block_rank).astype(jnp.float32)
    sq_t = new_squares.T
    pr_t = new_products.T
    crossing = sq_t[:, None, :] * onehot[None, :, None]
    diag_vals = sq_t + onehot[None, :] * jnp.sum(sq_t, axis=1, keepdims=True)
    hessian = diag_vals[:, :, None] * eye_blocks[None] - crossing - jnp.swapaxes(crossing, 1, 2)
    gradient = onehot[None, :] * jnp.sum(pr_t, axis=1, keepdims=True) - pr_t
    hessian, gradient = lax.psum((hessian, gradient), "pair")
    diagonal = jnp.diagonal(hessian, axis1=1, axis2=2)
    trace_sum = lax.psum(jnp.sum(diagonal), "row")
    level_mean = trace_sum / (nblock * CB)
    damped = damping[0] * (diagonal + level_mean)
    system = hessian + damped[:, :, None] * eye_blocks[None]
    factor = jnp.linalg.cholesky(system)
    update = -jax.scipy.linalg.cho_solve((factor, True), gradient[:, :, None])[:, :, 0]
    return lax.dynamic_slice_in_dim(update, block_rank, 1, 1).T


LANES = 128
NBLOCK = 8
REACH = NBLOCK // 2
VMEM = pl.BlockSpec(memory_space=pltpu.VMEM)


ORDERS = 88
HALF = LANES // 2
SPARE = 2 * ORDERS - LANES


def two_pieces(table):
    table = (np.round(table * 2.0**22) / 2.0**22).astype(np.float32)
    high = table.astype(jnp.bfloat16)
    low = (table - high.astype(np.float32)).astype(jnp.bfloat16)
    return np.concatenate([high, low], axis=0)


@functools.cache
def band_factors(length, samples):
    times = np.arange(length, dtype=np.float64)
    place = np.arange(NF)
    bins = samples // 8 + place % LANES * (NF // LANES) + place // LANES
    centre = samples // 8 + NF // 2
    main = ((length - 1 - 2 * times) / 2) ** 2 * math.cos(math.pi * NF / samples)
    side = times[1:] * (length - times[1:]) / 2
    _, vectors = np.linalg.eigh(np.diag(main) + np.diag(side, 1) + np.diag(side, -1))
    vectors = vectors[:, ::-1][:, :ORDERS]
    ids = np.arange(length)
    inner = 2.0 * math.pi * (ids[:, None] * (bins - centre)[None, :] % samples) / samples
    real = vectors.T @ np.cos(inner)
    imag = vectors.T @ np.sin(inner)
    carrier = 2.0 * math.pi * (ids * centre % samples)[:, None] / samples
    first = [vectors * np.cos(carrier), vectors * np.sin(carrier)]
    second = [np.concatenate([real, imag], axis=1), np.concatenate([-imag, real], axis=1)]
    upper = np.concatenate([first[0][:, HALF:], first[1][:, HALF:]], axis=1)
    upper = np.pad(upper, ((0, 0), (0, HALF - SPARE)))
    basis = np.concatenate([first[0][:, :HALF], first[1][:, :HALF], upper, upper], axis=1)
    upper = np.concatenate([second[0][HALF:], second[1][HALF:]], axis=0)
    upper = np.pad(upper, ((0, HALF - SPARE), (0, 0)))
    band = np.concatenate([second[0][:HALF], second[1][:HALF], upper, upper], axis=0)
    band = band.reshape(-1, 2, NF // LANES, LANES).swapaxes(1, 2).reshape(-1, 2 * NF)
    return two_pieces(basis), two_pieces(band)


def lanes_of(height):
    return lax.broadcasted_iota(jnp.int32, (height, LANES), 1)


def pack_kernel(rec_ref, basis_ref, value_ref, out_ref):
    ndest = out_ref.shape[0]
    rows = rec_ref.shape[0] // ndest
    own = rows // NBLOCK
    late = rows // 2
    value = value_ref[...]
    high = value.astype(jnp.bfloat16).astype(jnp.float32)
    middle = (value - high).astype(jnp.bfloat16).astype(jnp.float32)
    pieces = (high, middle, value - high - middle)
    place = lanes_of(NBLOCK)
    first = lanes_of(late) < HALF
    plain = (lanes_of(late) < SPARE) | (lanes_of(late) >= SPARE + 3 * own)
    signal = rec_ref[...]
    found = jnp.dot(
        jnp.concatenate([signal, signal], axis=1),
        basis_ref[...],
        preferred_element_type=jnp.float32,
    )
    for dest in range(ndest):
        tile = jnp.zeros_like(value)
        for index, piece in enumerate(pieces):
            start = SPARE + index * own
            moved = pltpu.roll(piece, (start - dest * own) % LANES, 1)
            tile = jnp.where((place >= start) & (place < start + own), moved, tile)
        shift = jnp.concatenate([tile] * (late // NBLOCK), axis=0)
        mine = found[dest * rows : (dest + 1) * rows]
        out_ref[dest, :rows] = mine[:, :LANES].astype(jnp.bfloat16)
        upper = jnp.where(first, mine[:late, LANES:], mine[late:, LANES:])
        out_ref[dest, rows:] = jnp.where(plain, upper, shift).astype(jnp.bfloat16)


def sin_cos(angle):
    square = angle * angle
    sine = jnp.float32(-1.0 / 39916800.0)
    for factor in (1.0 / 362880.0, -1.0 / 5040.0, 1.0 / 120.0, -1.0 / 6.0, 1.0):
        sine = sine * square + jnp.float32(factor)
    cosine = jnp.float32(1.0 / 479001600.0)
    for factor in (-1.0 / 3628800.0, 1.0 / 40320.0, -1.0 / 720.0, 1.0 / 24.0, -0.5, 1.0):
        cosine = cosine * square + jnp.float32(factor)
    return sine * angle, cosine


def unit_circle(phase, samples):
    phase = lax.bitwise_and(phase, samples - 1)
    phase = jnp.where(phase >= samples // 2, phase - samples, phase)
    sine, cosine = sin_cos(phase.astype(jnp.float32) * jnp.float32(math.pi / samples))
    return 1.0 - 2.0 * sine * sine, 2.0 * sine * cosine


def band_ids(height):
    place = lax.broadcasted_iota(jnp.int32, (height, NF), 1)
    return lax.rem(place, LANES) * (NF // LANES) + lax.div(place, LANES)


WAVE_ROWS = 16


def wave_kernel(samples, fine_ref, coarse_ref, ang_ref, blank_ref):
    first_bin = samples // 8

    def bins(height):
        return first_bin + band_ids(height)

    ids = lax.broadcasted_iota(jnp.int32, (WAVE_ROWS, NF), 0)
    centre = (band_ids(1).astype(jnp.float32) + 0.5) * (math.pi / NF)
    _, weight = sin_cos(centre - jnp.float32(math.pi / 2))
    factor = -2.0 * (weight * weight)
    fine_cos, fine_sin = unit_circle(ids * bins(WAVE_ROWS), samples)
    fine_ref[:, :NF] = fine_cos * factor
    fine_ref[:, NF:] = fine_sin * factor
    coarse_cos, coarse_sin = unit_circle((ids * WAVE_ROWS + 1) * bins(WAVE_ROWS), samples)
    coarse_ref[:, :NF] = coarse_cos
    coarse_ref[:, NF:] = coarse_sin
    ang_ref[...] = bins(NBLOCK).astype(jnp.float32) * jnp.float32(2.0 * math.pi / samples)
    blank_ref[...] = jnp.zeros_like(blank_ref)


def small_kernel(
    order, counts_ref, damp_ref, off_ref, blank_ref, live_ref, wide_ref, value_ref
):
    shards = len(order)
    own = live_ref.shape[0]
    me = lax.axis_index("pair")
    slot = sum(jnp.where(me == pair, index, 0) for index, pair in enumerate(order))
    first_channel = (lax.axis_index("row") * shards + slot) * own
    diagonal = lax.broadcasted_iota(jnp.int32, (NBLOCK, NBLOCK), 0) == lax.broadcasted_iota(
        jnp.int32, (NBLOCK, NBLOCK), 1
    )
    spread = jnp.broadcast_to(counts_ref[...], (NBLOCK, NBLOCK)).astype(jnp.float32)
    limit = jnp.sum(jnp.where(diagonal, spread, 0.0), axis=1, keepdims=True)
    for c in range(own):
        live = (limit > (first_channel + c).astype(jnp.float32)).astype(jnp.float32)
        live_ref[c] = jnp.broadcast_to(live, (NBLOCK, LANES))
    wide_ref[...] = jnp.broadcast_to(damp_ref[...], (NBLOCK, LANES))
    channels = off_ref.shape[1]
    value_ref[...] = blank_ref[...]
    value_ref[:, :channels] = jnp.broadcast_to(off_ref[...], (NBLOCK, channels))


def plus_turned(first, second, quarters):
    (real, imag), (far_real, far_imag) = first, second
    if quarters % 4 == 0:
        return real + far_real, imag + far_imag
    if quarters % 4 == 1:
        return real - far_imag, imag + far_real
    if quarters % 4 == 2:
        return real - far_real, imag - far_imag
    return real + far_imag, imag - far_real


def stats_kernel(
    order, x_ref, band_ref, fine_ref, coarse_ref, ang_ref, live_ref, out_ref, stacked, lag_ref,
):
    shards = x_ref.shape[0]
    own = live_ref.shape[0]
    rows = own * NBLOCK
    late = rows // 2
    first = (lanes_of(late) < HALF).astype(jnp.float32)
    parts = []
    for shard in range(shards):
        upper = x_ref[shard, rows:].astype(jnp.float32)
        upper = jnp.concatenate([upper * first, upper * (1.0 - first)], axis=0)
        parts.append(jnp.concatenate([x_ref[shard, :rows], upper.astype(jnp.bfloat16)], axis=1))
    found = jnp.concatenate(parts, axis=0)
    found = jnp.concatenate([found, found], axis=1)
    block_ids = lax.broadcasted_iota(jnp.int32, (NBLOCK, LANES), 0)
    pieces = jnp.zeros((NBLOCK, LANES), jnp.float32)
    for shard in range(shards):
        pieces = jnp.where(
            block_ids == order[shard],
            x_ref[shard, pl.ds(rows, NBLOCK)].astype(jnp.float32),
            pieces,
        )
    shift = (pieces + pltpu.roll(pieces, LANES - own, 1)) + pltpu.roll(
        pieces, LANES - 2 * own, 1
    )
    for step in range(NLAG // WAVE_ROWS):
        row_cos = coarse_ref[pl.ds(step, 1), :NF]
        row_sin = coarse_ref[pl.ds(step, 1), NF:]
        lag_ref[pl.ds(step * WAVE_ROWS, WAVE_ROWS), :] = (
            row_sin * fine_ref[:, :NF] + row_cos * fine_ref[:, NF:]
        ).astype(jnp.bfloat16)

    cols = NF // LANES
    spread = [shift[:, SPARE + c : SPARE + c + 1] for c in range(own)]
    rotations = [
        [sin_cos(spread[c] * ang_ref[:, col * LANES : (col + 1) * LANES]) for c in range(own)]
        for col in range(cols)
    ]
    sign = 1 - 2 * lax.bitwise_and(lanes_of(1), 1)
    sign = sign.astype(jnp.float32)
    energy = [jnp.zeros((NBLOCK, LANES), jnp.float32)] * own
    reals = [[] for _ in range(own)]
    imags = [[] for _ in range(own)]
    for col in range(cols):
        spectrum = jnp.dot(
            found,
            band_ref[:, 2 * col * LANES : 2 * (col + 1) * LANES],
            preferred_element_type=jnp.float32,
        )

        def shard(pair):
            at = order.index(pair) * rows
            return spectrum[at : at + rows, :LANES], spectrum[at : at + rows, LANES:]

        def joined(pair):
            return plus_turned(shard(pair), shard(pair + shards // 2), 2 * col)

        low = plus_turned(joined(0), joined(2), col)
        real, imag = plus_turned(joined(1), joined(3), col)
        if col % 2:
            root = sign * jnp.float32(math.sqrt(0.5))
            odd = (real - imag) * root, (real + imag) * root
        else:
            odd = real * sign, imag * sign
        cosine_part, sine_part = plus_turned(low, odd, col // 2)
        for c in range(own):
            piece = slice(c * NBLOCK, (c + 1) * NBLOCK)
            shift_sin, shift_cos = rotations[col][c]
            real = cosine_part[piece] * shift_cos + sine_part[piece] * shift_sin
            imag = cosine_part[piece] * shift_sin - sine_part[piece] * shift_cos
            energy[c] = energy[c] + (real * real + imag * imag)
            reals[c].append(real)
            imags[c].append(imag)

    half = own * REACH * NBLOCK
    angular = ang_ref[...]
    for c in range(own):
        total = jnp.sum(energy[c], axis=1, keepdims=True)
        scale = live_ref[c][:, :1] / jnp.sqrt(total * (1.0 / NF) + 1e-06)
        real = jnp.concatenate(reals[c], axis=1) * scale
        real = real.astype(jnp.bfloat16).astype(jnp.float32)
        imag = jnp.concatenate(imags[c], axis=1) * scale
        imag = imag.astype(jnp.bfloat16).astype(jnp.float32)
        crossings = []
        for reach in range(1, REACH + 1):
            far_re = pltpu.roll(real, NBLOCK - reach, 0)
            far_im = pltpu.roll(imag, NBLOCK - reach, 0)
            cross_re = real * far_re + imag * far_im
            cross_im = imag * far_re - real * far_im
            crossings.append((cross_im, angular * cross_re))
        width = REACH * NBLOCK
        for part in range(2):
            stacked[pl.ds(part * half + c * width, width), :] = jnp.concatenate(
                [crossing[part] for crossing in crossings], axis=0
            ).astype(jnp.bfloat16)
    sums = []
    for part in range(2):
        lagged = lax.dot_general(
            lag_ref[pl.ds(part * (NLAG // 2), NLAG // 2), :],
            stacked[...],
            (((1,), (1,)), ((), ())),
            preferred_element_type=jnp.float32,
        )
        residual = lagged[:, :half]
        jacobian = lagged[:, half:]
        sums.append(
            (
                jnp.sum(jacobian * jacobian, axis=0, keepdims=True),
                jnp.sum(jacobian * residual, axis=0, keepdims=True),
            )
        )
    squares = sums[0][0] + sums[1][0]
    products = sums[0][1] + sums[1][1]
    both = jnp.concatenate([squares, products], axis=0)
    out_ref[...] = jnp.broadcast_to(both[None], out_ref.shape)


def solve_kernel(order, own, total, got_ref, damp_ref, out_ref, steps):
    shards = got_ref.shape[0]
    quarter = lax.axis_index("row")
    me = lax.axis_index("pair")
    span = REACH * NBLOCK
    lane_ids = lax.broadcasted_iota(jnp.int32, (NBLOCK, LANES), 1)
    block_ids = lax.broadcasted_iota(jnp.int32, (NBLOCK, LANES), 0)

    def total_of(values):
        while len(values) > 1:
            values = [x + y for x, y in zip(values[::2], values[1::2])] + values[
                len(values) // 2 * 2 :
            ]
        return values[0]

    summed = total_of(
        [
            got_ref[shard, other, 0:1, :]
            for shard in range(shards)
            for other in range(got_ref.shape[1])
        ]
    )
    inner = (lane_ids[:1] % span) < (REACH - 1) * NBLOCK
    level = jnp.sum(
        jnp.where(inner, 2.0 * summed, summed), axis=1, keepdims=True
    ) * (1.0 / total)

    squares = jnp.concatenate(
        [got_ref[shard, quarter, 0:1, :] for shard in order], axis=0
    )
    products = jnp.concatenate(
        [got_ref[shard, quarter, 1:2, :] for shard in order], axis=0
    )

    def entry(array, reach, block):
        lane = (reach - 1) * NBLOCK + block
        return array if lane == 0 else pltpu.roll(array, LANES - lane, 1)

    weight = {}
    slope = {}
    for reach in range(1, REACH + 1):
        for block in range(NBLOCK if reach < REACH else NBLOCK // 2):
            far = (block + reach) % NBLOCK
            value = entry(squares, reach, block)
            weight[block, far] = value
            weight[far, block] = value
            value = entry(products, reach, block)
            slope[block, far] = value
            slope[far, block] = -value
    damping = damp_ref[...]
    matrix = {}
    right = []
    for a in range(NBLOCK):
        others = [b for b in range(NBLOCK) if b != a]
        diagonal = total_of([weight[a, b] for b in others])
        matrix[a, a] = diagonal + damping * (diagonal + level)
        for b in range(a):
            matrix[a, b] = -weight[a, b]
        right.append(total_of([slope[a, b] for b in others]))
    inverse = []
    for k in range(NBLOCK):
        inverse.append(1.0 / matrix[k, k])
        for i in range(k + 1, NBLOCK):
            ratio = matrix[i, k] * inverse[k]
            for j in range(k + 1, i + 1):
                matrix[i, j] = matrix[i, j] - ratio * matrix[j, k]
            right[i] = right[i] - ratio * right[k]
    step = [None] * NBLOCK
    for i in reversed(range(NBLOCK)):
        value = right[i]
        for j in range(i + 1, NBLOCK):
            value = value - matrix[j, i] * step[j]
        step[i] = value * inverse[i]
        steps[i] = -step[i]
    mine = steps[me]
    placed = jnp.zeros((NBLOCK, LANES), jnp.float32)
    for c in range(own):
        column = jnp.broadcast_to(mine[:, c * span : c * span + 1], (NBLOCK, LANES))
        placed = jnp.where(lane_ids == block_ids * own + c, column, placed)
    out_ref[...] = jnp.sum(placed, axis=0, keepdims=True)[:, : out_ref.shape[1]]


def room(mebibytes):
    return pltpu.CompilerParams(vmem_limit_bytes=mebibytes << 20)


def per_device(records, offsets, counts, damping):
    shards = lax.axis_size("pair")
    rows = lax.axis_size("row")
    channels, length, _ = records.shape
    samples = length * shards
    own = channels // shards
    height = own * NBLOCK + own * NBLOCK // 2
    basis, band = band_factors(length, samples)
    order = tuple((shards // 2 + 1 + place) % shards for place in range(shards))

    by_owner = jnp.transpose(records, (0, 2, 1)).reshape(channels * NBLOCK, length)
    *waves, blank = pl.pallas_call(
        functools.partial(wave_kernel, samples),
        out_shape=(
            jax.ShapeDtypeStruct((WAVE_ROWS, 2 * NF), jnp.float32),
            jax.ShapeDtypeStruct((WAVE_ROWS, 2 * NF), jnp.float32),
            jax.ShapeDtypeStruct((NBLOCK, NF), jnp.float32),
            jax.ShapeDtypeStruct((NBLOCK, LANES), jnp.float32),
        ),
        out_specs=(VMEM,) * 4,
        compiler_params=room(4),
        cost_estimate=pl.CostEstimate(
            flops=20000000000, bytes_accessed=40000000, transcendentals=0
        ),
        name="waves",
    )()
    live, wide, value = pl.pallas_call(
        functools.partial(small_kernel, order),
        out_shape=(
            jax.ShapeDtypeStruct((own, NBLOCK, LANES), jnp.float32),
            jax.ShapeDtypeStruct((NBLOCK, LANES), jnp.float32),
            jax.ShapeDtypeStruct((NBLOCK, LANES), jnp.float32),
        ),
        in_specs=[VMEM] * 4,
        out_specs=(VMEM,) * 3,
        compiler_params=room(4),
        name="small",
    )(counts[None, :], damping[None, :], offsets, blank)
    payload = pl.pallas_call(
        pack_kernel,
        out_shape=jax.ShapeDtypeStruct((shards, height, LANES), jnp.bfloat16),
        in_specs=[VMEM] * 3,
        out_specs=VMEM,
        compiler_params=room(8),
        name="pack",
    )(by_owner, jnp.asarray(basis), value)
    received = lax.all_to_all(
        payload, "pair", split_axis=0, concat_axis=0, tiled=True, axis_index_groups=[list(order)]
    )

    stats = pl.pallas_call(
        functools.partial(stats_kernel, order),
        out_shape=jax.ShapeDtypeStruct((shards * rows, 2, LANES), jnp.float32),
        in_specs=[VMEM] * 6,
        out_specs=VMEM,
        scratch_shapes=[
            pltpu.VMEM((2 * own * REACH * NBLOCK, NF), jnp.bfloat16),
            pltpu.VMEM((NLAG, NF), jnp.bfloat16),
        ],
        compiler_params=room(12),
        name="stats",
    )(received, jnp.asarray(band), *waves, live)
    gathered = lax.all_to_all(stats, ("pair", "row"), split_axis=0, concat_axis=0, tiled=True)
    gathered = gathered.reshape(shards, rows, 2, LANES)
    return pl.pallas_call(
        functools.partial(solve_kernel, order, own, float(NBLOCK * CB)),
        out_shape=jax.ShapeDtypeStruct((1, channels), jnp.float32),
        in_specs=[VMEM, VMEM],
        out_specs=VMEM,
        scratch_shapes=[pltpu.VMEM((NBLOCK, NBLOCK, LANES), jnp.float32)],
        compiler_params=room(4),
        name="solve",
    )(gathered, wide)


def body(records, offsets, counts, damping):
    shards = lax.axis_size("pair")
    channels, length, nblock = records.shape
    own = channels // shards
    whole = own * shards == channels and own * REACH * NBLOCK == LANES
    even = length & (length - 1) == 0 and length == NF == 4 * LANES
    if shards == NBLOCK and nblock == NBLOCK and whole and even:
        return per_device(records, offsets, counts, damping)
    return per_device_general(records, offsets, counts, damping)


def solution(mesh):
    return jax.shard_map(
        body,
        mesh=mesh,
        in_specs=(P("row", "pair", None), P("pair", "row"), P(), P()),
        out_specs=P("pair", "row"),
        check_vma=False,
    )
```

```python
import functools
import math

import jax
import jax.numpy as jnp
import numpy as np
from jax import lax
from jax.experimental import pallas as pl
from jax.experimental.pallas import tpu as pltpu
from jax.sharding import PartitionSpec as P

CB = 128
NF = 512
NLAG = 256


def band_table(row_start, row_count, samples, first_bin, freq_count):
    sample_ids = row_start + jnp.arange(row_count, dtype=jnp.int32)
    freq_bins = first_bin + jnp.arange(freq_count, dtype=jnp.int32)
    phase_ids = sample_ids[:, None] * freq_bins[None, :] % samples
    angles = phase_ids.astype(jnp.float32) * (2.0 * math.pi / samples)
    return jnp.concatenate([jnp.cos(angles), jnp.sin(angles)], axis=1)


def lag_weights(samples, first_bin, freq_count, lag_count):
    freq_bins = first_bin + jnp.arange(freq_count, dtype=jnp.int32)
    lag_ids = 1 + jnp.arange(lag_count, dtype=jnp.int32)
    phase_ids = freq_bins[:, None] * lag_ids[None, :] % samples
    angles = phase_ids.astype(jnp.float32) * (2.0 * math.pi / samples)
    centre = (jnp.arange(freq_count, dtype=jnp.float32) + 0.5) * (math.pi / freq_count)
    weight = jnp.sin(centre) ** 2
    return (-2.0 * weight[:, None] * jnp.sin(angles)).astype(jnp.bfloat16)


def pair_stats(own_spec, partners, lag_table, angular):
    own_re = own_spec[:, 0].astype(jnp.float32)
    own_im = own_spec[:, 1].astype(jnp.float32)
    far_re = partners[:, :, 0].astype(jnp.float32)
    far_im = partners[:, :, 1].astype(jnp.float32)
    cross_re = own_re * far_re + own_im * far_im
    cross_im = own_im * far_re - own_re * far_im
    stacked = jnp.stack([cross_im, angular * cross_re]).astype(jnp.bfloat16)
    lagged = jnp.dot(stacked, lag_table, preferred_element_type=jnp.float32)
    residual = lagged[0]
    jacobian = lagged[1]
    return (jnp.sum(jacobian * jacobian, axis=-1), jnp.sum(jacobian * residual, axis=-1))


def per_device_general(records, offsets, counts, damping):
    nblock = lax.axis_size("pair")
    block_rank = lax.axis_index("pair")
    quarter = lax.axis_index("row")
    relaid = lax.all_to_all(records, "pair", split_axis=2, concat_axis=1, tiled=True)
    signal = relaid[:, :, 0]
    channels = signal.shape[0]
    samples = signal.shape[1]
    first_bin = samples // 8
    block_len = samples // 8

    def accumulate(partial_value, turn_index):
        first_row = turn_index * block_len
        segment = lax.dynamic_slice_in_dim(signal, first_row, block_len, 1)
        dft_table = band_table(first_row, block_len, samples, first_bin, NF)
        table_high = dft_table.astype(jnp.bfloat16)
        table_low = (dft_table - table_high.astype(jnp.float32)).astype(jnp.bfloat16)
        partial_value = partial_value + jnp.dot(
            segment, table_high, preferred_element_type=jnp.float32
        )
        partial_value = partial_value + jnp.dot(
            segment, table_low, preferred_element_type=jnp.float32
        )
        return (partial_value, None)

    spectrum, _ = lax.scan(
        accumulate, jnp.zeros((channels, 2 * NF), jnp.float32), jnp.arange(8, dtype=jnp.int32)
    )
    cosine_part = spectrum[:, :NF]
    sine_part = spectrum[:, NF:]
    angular = (first_bin + jnp.arange(NF, dtype=jnp.int32)).astype(jnp.float32) * (
        2.0 * math.pi / samples
    )
    shift_angle = offsets[0][:, None] * angular[None, :]
    shift_cos = jnp.cos(shift_angle)
    shift_sin = jnp.sin(shift_angle)
    real_part = cosine_part * shift_cos + sine_part * shift_sin
    imag_part = cosine_part * shift_sin - sine_part * shift_cos
    live_count = lax.dynamic_index_in_dim(counts, block_rank, keepdims=False)
    channel_ids = quarter * channels + jnp.arange(channels, dtype=jnp.int32)
    alive = (channel_ids < live_count).astype(jnp.float32)
    energy = jnp.mean(real_part * real_part + imag_part * imag_part, axis=1)
    weight_scale = alive / jnp.sqrt(energy + 1e-06)
    own_spec = jnp.stack(
        [real_part * weight_scale[:, None], imag_part * weight_scale[:, None]], axis=1
    ).astype(jnp.bfloat16)
    lag_table = lag_weights(samples, first_bin, NF, NLAG)
    segment = lax.all_gather(own_spec[None], "pair", axis=0, tiled=True)
    squares_part, products_part = pair_stats(own_spec, segment, lag_table, angular)
    partner_ids = jnp.arange(segment.shape[0], dtype=jnp.int32)
    keep_mask = (partner_ids > block_rank).astype(jnp.float32)[:, None]
    new_squares = squares_part * keep_mask
    new_products = products_part * keep_mask
    eye_blocks = jnp.eye(nblock, dtype=jnp.float32)
    onehot = (jnp.arange(nblock, dtype=jnp.int32) == block_rank).astype(jnp.float32)
    sq_t = new_squares.T
    pr_t = new_products.T
    crossing = sq_t[:, None, :] * onehot[None, :, None]
    diag_vals = sq_t + onehot[None, :] * jnp.sum(sq_t, axis=1, keepdims=True)
    hessian = diag_vals[:, :, None] * eye_blocks[None] - crossing - jnp.swapaxes(crossing, 1, 2)
    gradient = onehot[None, :] * jnp.sum(pr_t, axis=1, keepdims=True) - pr_t
    hessian, gradient = lax.psum((hessian, gradient), "pair")
    diagonal = jnp.diagonal(hessian, axis1=1, axis2=2)
    trace_sum = lax.psum(jnp.sum(diagonal), "row")
    level_mean = trace_sum / (nblock * CB)
    damped = damping[0] * (diagonal + level_mean)
    system = hessian + damped[:, :, None] * eye_blocks[None]
    factor = jnp.linalg.cholesky(system)
    update = -jax.scipy.linalg.cho_solve((factor, True), gradient[:, :, None])[:, :, 0]
    return lax.dynamic_slice_in_dim(update, block_rank, 1, 1).T


LANES = 128
NBLOCK = 8
REACH = NBLOCK // 2
VMEM = pl.BlockSpec(memory_space=pltpu.VMEM)


ORDERS = 88
HALF = LANES // 2
SPARE = 2 * ORDERS - LANES


def two_pieces(table):
    table = (np.round(table * 2.0**22) / 2.0**22).astype(np.float32)
    high = table.astype(jnp.bfloat16)
    low = (table - high.astype(np.float32)).astype(jnp.bfloat16)
    return np.concatenate([high, low], axis=0)


@functools.cache
def band_factors(length, samples):
    times = np.arange(length, dtype=np.float64)
    place = np.arange(NF)
    bins = samples // 8 + place % LANES * (NF // LANES) + place // LANES
    centre = samples // 8 + NF // 2
    main = ((length - 1 - 2 * times) / 2) ** 2 * math.cos(math.pi * NF / samples)
    side = times[1:] * (length - times[1:]) / 2
    _, vectors = np.linalg.eigh(np.diag(main) + np.diag(side, 1) + np.diag(side, -1))
    vectors = vectors[:, ::-1][:, :ORDERS]
    ids = np.arange(length)
    inner = 2.0 * math.pi * (ids[:, None] * (bins - centre)[None, :] % samples) / samples
    real = vectors.T @ np.cos(inner)
    imag = vectors.T @ np.sin(inner)
    carrier = 2.0 * math.pi * (ids * centre % samples)[:, None] / samples
    first = [vectors * np.cos(carrier), vectors * np.sin(carrier)]
    second = [np.concatenate([real, imag], axis=1), np.concatenate([-imag, real], axis=1)]
    upper = np.concatenate([first[0][:, HALF:], first[1][:, HALF:]], axis=1)
    upper = np.pad(upper, ((0, 0), (0, HALF - SPARE)))
    basis = np.concatenate([first[0][:, :HALF], first[1][:, :HALF], upper, upper], axis=1)
    upper = np.concatenate([second[0][HALF:], second[1][HALF:]], axis=0)
    upper = np.pad(upper, ((0, HALF - SPARE), (0, 0)))
    band = np.concatenate([second[0][:HALF], second[1][:HALF], upper, upper], axis=0)
    band = band.reshape(-1, 2, NF // LANES, LANES).swapaxes(1, 2).reshape(-1, 2 * NF)
    return two_pieces(basis), two_pieces(band)


def lanes_of(height):
    return lax.broadcasted_iota(jnp.int32, (height, LANES), 1)


def pack_kernel(rec_ref, basis_ref, value_ref, out_ref):
    ndest = out_ref.shape[0]
    rows = rec_ref.shape[0] // ndest
    own = rows // NBLOCK
    late = rows // 2
    value = value_ref[...]
    high = value.astype(jnp.bfloat16).astype(jnp.float32)
    middle = (value - high).astype(jnp.bfloat16).astype(jnp.float32)
    pieces = (high, middle, value - high - middle)
    place = lanes_of(NBLOCK)
    first = lanes_of(late) < HALF
    plain = (lanes_of(late) < SPARE) | (lanes_of(late) >= SPARE + 3 * own)
    signal = rec_ref[...]
    twice = jnp.concatenate([signal, signal], axis=1)
    middle = ndest // 2 * rows
    found = jnp.concatenate(
        [
            jnp.dot(part, basis_ref[...], preferred_element_type=jnp.float32)
            for part in (twice[:middle], twice[middle:])
        ],
        axis=0,
    )
    for dest in range(ndest):
        tile = jnp.zeros_like(value)
        for index, piece in enumerate(pieces):
            start = SPARE + index * own
            moved = pltpu.roll(piece, (start - dest * own) % LANES, 1)
            tile = jnp.where((place >= start) & (place < start + own), moved, tile)
        shift = jnp.concatenate([tile] * (late // NBLOCK), axis=0)
        mine = found[dest * rows : (dest + 1) * rows]
        out_ref[dest, :rows] = mine[:, :LANES].astype(jnp.bfloat16)
        upper = jnp.where(first, mine[:late, LANES:], mine[late:, LANES:])
        out_ref[dest, rows:] = jnp.where(plain, upper, shift).astype(jnp.bfloat16)


def sin_cos(angle):
    square = angle * angle
    sine = jnp.float32(-1.0 / 39916800.0)
    for factor in (1.0 / 362880.0, -1.0 / 5040.0, 1.0 / 120.0, -1.0 / 6.0, 1.0):
        sine = sine * square + jnp.float32(factor)
    cosine = jnp.float32(1.0 / 479001600.0)
    for factor in (-1.0 / 3628800.0, 1.0 / 40320.0, -1.0 / 720.0, 1.0 / 24.0, -0.5, 1.0):
        cosine = cosine * square + jnp.float32(factor)
    return sine * angle, cosine


def unit_circle(phase, samples):
    phase = lax.bitwise_and(phase, samples - 1)
    phase = jnp.where(phase >= samples // 2, phase - samples, phase)
    sine, cosine = sin_cos(phase.astype(jnp.float32) * jnp.float32(math.pi / samples))
    return 1.0 - 2.0 * sine * sine, 2.0 * sine * cosine


def band_ids(height):
    place = lax.broadcasted_iota(jnp.int32, (height, NF), 1)
    return lax.rem(place, LANES) * (NF // LANES) + lax.div(place, LANES)


WAVE_ROWS = 16


def wave_kernel(samples, fine_ref, coarse_ref, ang_ref, blank_ref):
    first_bin = samples // 8

    def bins(height):
        return first_bin + band_ids(height)

    ids = lax.broadcasted_iota(jnp.int32, (WAVE_ROWS, NF), 0)
    centre = (band_ids(1).astype(jnp.float32) + 0.5) * (math.pi / NF)
    _, weight = sin_cos(centre - jnp.float32(math.pi / 2))
    factor = -2.0 * (weight * weight)
    fine_cos, fine_sin = unit_circle(ids * bins(WAVE_ROWS), samples)
    fine_ref[:, :NF] = fine_cos * factor
    fine_ref[:, NF:] = fine_sin * factor
    coarse_cos, coarse_sin = unit_circle((ids * WAVE_ROWS + 1) * bins(WAVE_ROWS), samples)
    coarse_ref[:, :NF] = coarse_cos
    coarse_ref[:, NF:] = coarse_sin
    ang_ref[...] = bins(NBLOCK).astype(jnp.float32) * jnp.float32(2.0 * math.pi / samples)
    blank_ref[...] = jnp.zeros_like(blank_ref)


def small_kernel(
    order, counts_ref, damp_ref, off_ref, blank_ref, live_ref, wide_ref, value_ref
):
    shards = len(order)
    own = live_ref.shape[0]
    me = lax.axis_index("pair")
    slot = sum(jnp.where(me == pair, index, 0) for index, pair in enumerate(order))
    first_channel = (lax.axis_index("row") * shards + slot) * own
    diagonal = lax.broadcasted_iota(jnp.int32, (NBLOCK, NBLOCK), 0) == lax.broadcasted_iota(
        jnp.int32, (NBLOCK, NBLOCK), 1
    )
    spread = jnp.broadcast_to(counts_ref[...], (NBLOCK, NBLOCK)).astype(jnp.float32)
    limit = jnp.sum(jnp.where(diagonal, spread, 0.0), axis=1, keepdims=True)
    for c in range(own):
        live = (limit > (first_channel + c).astype(jnp.float32)).astype(jnp.float32)
        live_ref[c] = jnp.broadcast_to(live, (NBLOCK, LANES))
    wide_ref[...] = jnp.broadcast_to(damp_ref[...], (NBLOCK, LANES))
    channels = off_ref.shape[1]
    value_ref[...] = blank_ref[...]
    value_ref[:, :channels] = jnp.broadcast_to(off_ref[...], (NBLOCK, channels))


def plus_turned(first, second, quarters):
    (real, imag), (far_real, far_imag) = first, second
    if quarters % 4 == 0:
        return real + far_real, imag + far_imag
    if quarters % 4 == 1:
        return real - far_imag, imag + far_real
    if quarters % 4 == 2:
        return real - far_real, imag - far_imag
    return real + far_imag, imag - far_real


def stats_kernel(
    order, x_ref, band_ref, fine_ref, coarse_ref, ang_ref, live_ref, out_ref, stacked, lag_ref,
):
    shards = x_ref.shape[0]
    own = live_ref.shape[0]
    rows = own * NBLOCK
    late = rows // 2
    first = (lanes_of(late) < HALF).astype(jnp.float32)
    parts = []
    for shard in range(shards):
        upper = x_ref[shard, rows:].astype(jnp.float32)
        upper = jnp.concatenate([upper * first, upper * (1.0 - first)], axis=0)
        parts.append(jnp.concatenate([x_ref[shard, :rows], upper.astype(jnp.bfloat16)], axis=1))
    found = jnp.concatenate(parts, axis=0)
    found = jnp.concatenate([found, found], axis=1)
    block_ids = lax.broadcasted_iota(jnp.int32, (NBLOCK, LANES), 0)
    pieces = jnp.zeros((NBLOCK, LANES), jnp.float32)
    for shard in range(shards):
        pieces = jnp.where(
            block_ids == order[shard],
            x_ref[shard, pl.ds(rows, NBLOCK)].astype(jnp.float32),
            pieces,
        )
    shift = (pieces + pltpu.roll(pieces, LANES - own, 1)) + pltpu.roll(
        pieces, LANES - 2 * own, 1
    )
    for step in range(NLAG // WAVE_ROWS):
        row_cos = coarse_ref[pl.ds(step, 1), :NF]
        row_sin = coarse_ref[pl.ds(step, 1), NF:]
        lag_ref[pl.ds(step * WAVE_ROWS, WAVE_ROWS), :] = (
            row_sin * fine_ref[:, :NF] + row_cos * fine_ref[:, NF:]
        ).astype(jnp.bfloat16)

    cols = NF // LANES
    spread = [shift[:, SPARE + c : SPARE + c + 1] for c in range(own)]
    rotations = [
        [sin_cos(spread[c] * ang_ref[:, col * LANES : (col + 1) * LANES]) for c in range(own)]
        for col in range(cols)
    ]
    sign = 1 - 2 * lax.bitwise_and(lanes_of(1), 1)
    sign = sign.astype(jnp.float32)
    energy = [jnp.zeros((NBLOCK, LANES), jnp.float32)] * own
    reals = [[] for _ in range(own)]
    imags = [[] for _ in range(own)]
    for col in range(cols):
        spectrum = jnp.dot(
            found,
            band_ref[:, 2 * col * LANES : 2 * (col + 1) * LANES],
            preferred_element_type=jnp.float32,
        )

        def shard(pair):
            at = order.index(pair) * rows
            return spectrum[at : at + rows, :LANES], spectrum[at : at + rows, LANES:]

        def joined(pair):
            return plus_turned(shard(pair), shard(pair + shards // 2), 2 * col)

        low = plus_turned(joined(0), joined(2), col)
        real, imag = plus_turned(joined(1), joined(3), col)
        if col % 2:
            root = sign * jnp.float32(math.sqrt(0.5))
            odd = (real - imag) * root, (real + imag) * root
        else:
            odd = real * sign, imag * sign
        cosine_part, sine_part = plus_turned(low, odd, col // 2)
        for c in range(own):
            piece = slice(c * NBLOCK, (c + 1) * NBLOCK)
            shift_sin, shift_cos = rotations[col][c]
            real = cosine_part[piece] * shift_cos + sine_part[piece] * shift_sin
            imag = cosine_part[piece] * shift_sin - sine_part[piece] * shift_cos
            energy[c] = energy[c] + (real * real + imag * imag)
            reals[c].append(real)
            imags[c].append(imag)

    half = own * REACH * NBLOCK
    angular = ang_ref[...]
    for c in range(own):
        total = jnp.sum(energy[c], axis=1, keepdims=True)
        scale = live_ref[c][:, :1] / jnp.sqrt(total * (1.0 / NF) + 1e-06)
        real = jnp.concatenate(reals[c], axis=1) * scale
        real = real.astype(jnp.bfloat16).astype(jnp.float32)
        imag = jnp.concatenate(imags[c], axis=1) * scale
        imag = imag.astype(jnp.bfloat16).astype(jnp.float32)
        crossings = []
        for reach in range(1, REACH + 1):
            far_re = pltpu.roll(real, NBLOCK - reach, 0)
            far_im = pltpu.roll(imag, NBLOCK - reach, 0)
            cross_re = real * far_re + imag * far_im
            cross_im = imag * far_re - real * far_im
            crossings.append((cross_im, angular * cross_re))
        width = REACH * NBLOCK
        for part in range(2):
            stacked[pl.ds(part * half + c * width, width), :] = jnp.concatenate(
                [crossing[part] for crossing in crossings], axis=0
            ).astype(jnp.bfloat16)
    sums = []
    for part in range(2):
        lagged = lax.dot_general(
            lag_ref[pl.ds(part * (NLAG // 2), NLAG // 2), :],
            stacked[...],
            (((1,), (1,)), ((), ())),
            preferred_element_type=jnp.float32,
        )
        residual = lagged[:, :half]
        jacobian = lagged[:, half:]
        sums.append(
            (
                jnp.sum(jacobian * jacobian, axis=0, keepdims=True),
                jnp.sum(jacobian * residual, axis=0, keepdims=True),
            )
        )
    squares = sums[0][0] + sums[1][0]
    products = sums[0][1] + sums[1][1]
    both = jnp.concatenate([squares, products], axis=0)
    out_ref[...] = jnp.broadcast_to(both[None], out_ref.shape)


def solve_kernel(order, own, total, got_ref, damp_ref, out_ref, steps):
    shards = got_ref.shape[0]
    quarter = lax.axis_index("row")
    me = lax.axis_index("pair")
    span = REACH * NBLOCK
    lane_ids = lax.broadcasted_iota(jnp.int32, (NBLOCK, LANES), 1)
    block_ids = lax.broadcasted_iota(jnp.int32, (NBLOCK, LANES), 0)

    def total_of(values):
        while len(values) > 1:
            values = [x + y for x, y in zip(values[::2], values[1::2])] + values[
                len(values) // 2 * 2 :
            ]
        return values[0]

    summed = total_of(
        [
            got_ref[shard, other, 0:1, :]
            for shard in range(shards)
            for other in range(got_ref.shape[1])
        ]
    )
    inner = (lane_ids[:1] % span) < (REACH - 1) * NBLOCK
    level = jnp.sum(
        jnp.where(inner, 2.0 * summed, summed), axis=1, keepdims=True
    ) * (1.0 / total)

    squares = jnp.concatenate(
        [got_ref[shard, quarter, 0:1, :] for shard in order], axis=0
    )
    products = jnp.concatenate(
        [got_ref[shard, quarter, 1:2, :] for shard in order], axis=0
    )

    def entry(array, reach, block):
        lane = (reach - 1) * NBLOCK + block
        return array if lane == 0 else pltpu.roll(array, LANES - lane, 1)

    weight = {}
    slope = {}
    for reach in range(1, REACH + 1):
        for block in range(NBLOCK if reach < REACH else NBLOCK // 2):
            far = (block + reach) % NBLOCK
            value = entry(squares, reach, block)
            weight[block, far] = value
            weight[far, block] = value
            value = entry(products, reach, block)
            slope[block, far] = value
            slope[far, block] = -value
    damping = damp_ref[...]
    matrix = {}
    right = []
    for a in range(NBLOCK):
        others = [b for b in range(NBLOCK) if b != a]
        diagonal = total_of([weight[a, b] for b in others])
        matrix[a, a] = diagonal + damping * (diagonal + level)
        for b in range(a):
            matrix[a, b] = -weight[a, b]
        right.append(total_of([slope[a, b] for b in others]))
    inverse = []
    for k in range(NBLOCK):
        inverse.append(1.0 / matrix[k, k])
        for i in range(k + 1, NBLOCK):
            ratio = matrix[i, k] * inverse[k]
            for j in range(k + 1, i + 1):
                matrix[i, j] = matrix[i, j] - ratio * matrix[j, k]
            right[i] = right[i] - ratio * right[k]
    step = [None] * NBLOCK
    for i in reversed(range(NBLOCK)):
        value = right[i]
        for j in range(i + 1, NBLOCK):
            value = value - matrix[j, i] * step[j]
        step[i] = value * inverse[i]
        steps[i] = -step[i]
    mine = steps[me]
    placed = jnp.zeros((NBLOCK, LANES), jnp.float32)
    for c in range(own):
        column = jnp.broadcast_to(mine[:, c * span : c * span + 1], (NBLOCK, LANES))
        placed = jnp.where(lane_ids == block_ids * own + c, column, placed)
    out_ref[...] = jnp.sum(placed, axis=0, keepdims=True)[:, : out_ref.shape[1]]


def room(mebibytes):
    return pltpu.CompilerParams(vmem_limit_bytes=mebibytes << 20)


def per_device(records, offsets, counts, damping):
    shards = lax.axis_size("pair")
    rows = lax.axis_size("row")
    channels, length, _ = records.shape
    samples = length * shards
    own = channels // shards
    height = own * NBLOCK + own * NBLOCK // 2
    basis, band = band_factors(length, samples)
    order = tuple((shards // 2 + 1 + place) % shards for place in range(shards))

    by_owner = jnp.transpose(records, (0, 2, 1)).reshape(channels * NBLOCK, length)
    *waves, blank = pl.pallas_call(
        functools.partial(wave_kernel, samples),
        out_shape=(
            jax.ShapeDtypeStruct((WAVE_ROWS, 2 * NF), jnp.float32),
            jax.ShapeDtypeStruct((WAVE_ROWS, 2 * NF), jnp.float32),
            jax.ShapeDtypeStruct((NBLOCK, NF), jnp.float32),
            jax.ShapeDtypeStruct((NBLOCK, LANES), jnp.float32),
        ),
        out_specs=(VMEM,) * 4,
        compiler_params=room(4),
        cost_estimate=pl.CostEstimate(
            flops=20000000000, bytes_accessed=40000000, transcendentals=0
        ),
        name="waves",
    )()
    live, wide, value = pl.pallas_call(
        functools.partial(small_kernel, order),
        out_shape=(
            jax.ShapeDtypeStruct((own, NBLOCK, LANES), jnp.float32),
            jax.ShapeDtypeStruct((NBLOCK, LANES), jnp.float32),
            jax.ShapeDtypeStruct((NBLOCK, LANES), jnp.float32),
        ),
        in_specs=[VMEM] * 4,
        out_specs=(VMEM,) * 3,
        compiler_params=room(4),
        name="small",
    )(counts[None, :], damping[None, :], offsets, blank)
    payload = pl.pallas_call(
        pack_kernel,
        out_shape=jax.ShapeDtypeStruct((shards, height, LANES), jnp.bfloat16),
        in_specs=[VMEM] * 3,
        out_specs=VMEM,
        compiler_params=room(8),
        name="pack",
    )(by_owner, jnp.asarray(basis), value)
    received = lax.all_to_all(
        payload, "pair", split_axis=0, concat_axis=0, tiled=True, axis_index_groups=[list(order)]
    )

    stats = pl.pallas_call(
        functools.partial(stats_kernel, order),
        out_shape=jax.ShapeDtypeStruct((shards * rows, 2, LANES), jnp.float32),
        in_specs=[VMEM] * 6,
        out_specs=VMEM,
        scratch_shapes=[
            pltpu.VMEM((2 * own * REACH * NBLOCK, NF), jnp.bfloat16),
            pltpu.VMEM((NLAG, NF), jnp.bfloat16),
        ],
        compiler_params=room(12),
        name="stats",
    )(received, jnp.asarray(band), *waves, live)
    gathered = lax.all_to_all(stats, ("pair", "row"), split_axis=0, concat_axis=0, tiled=True)
    gathered = gathered.reshape(shards, rows, 2, LANES)
    return pl.pallas_call(
        functools.partial(solve_kernel, order, own, float(NBLOCK * CB)),
        out_shape=jax.ShapeDtypeStruct((1, channels), jnp.float32),
        in_specs=[VMEM, VMEM],
        out_specs=VMEM,
        scratch_shapes=[pltpu.VMEM((NBLOCK, NBLOCK, LANES), jnp.float32)],
        compiler_params=room(4),
        name="solve",
    )(gathered, wide)


def body(records, offsets, counts, damping):
    shards = lax.axis_size("pair")
    channels, length, nblock = records.shape
    own = channels // shards
    whole = own * shards == channels and own * REACH * NBLOCK == LANES
    even = length & (length - 1) == 0 and length == NF == 4 * LANES
    if shards == NBLOCK and nblock == NBLOCK and whole and even:
        return per_device(records, offsets, counts, damping)
    return per_device_general(records, offsets, counts, damping)


def solution(mesh):
    return jax.shard_map(
        body,
        mesh=mesh,
        in_specs=(P("row", "pair", None), P("pair", "row"), P(), P()),
        out_specs=P("pair", "row"),
        check_vma=False,
    )
```
